32 devices in a mesh: dp: 8 (over z, y), tensor: 4 (over x, core).
Axes of the slice: x: 2, y: 2, z: 4, core: 2. Of those that a mesh axis runs over, the one named last changes fastest.
Arguments:
- frames: bfloat16 [16, 256, 1024], P('dp', 'tensor'), may hold values from -6 to 6
- lengths: int32 [16], P('dp'), may hold values from 128 to 256, as said below
- span_starts: int32 [16, 32], P('dp'), may hold values from 0 to 256, as said below
- mask_vector: bfloat16 [1024], P(('dp', 'tensor')), may hold values from -6 to 6
- ffn1_gain: float32 [1024], P(('dp', 'tensor')), may hold values from 0.5 to 1.5
- ffn1_up: bfloat16 [1024, 4096], P(None, 'tensor'), may hold values from -0.1875 to 0.1875
- ffn1_down: bfloat16 [4096, 1024], P('tensor'), may hold values from -0.1875 to 0.1875
- attn_gain: float32 [1024], P(('dp', 'tensor')), may hold values from 0.5 to 1.5
- query_weight: bfloat16 [1024, 1024], P(None, 'tensor'), may hold values from -0.1875 to 0.1875
- key_weight: bfloat16 [1024, 1024], P(None, 'tensor'), may hold values from -0.1875 to 0.1875
- value_weight: bfloat16 [1024, 1024], P(None, 'tensor'), may hold values from -0.1875 to 0.1875
- output_weight: bfloat16 [1024, 1024], P('tensor'), may hold values from -1.5 to 1.5
- rel_slope: float32 [8], P('tensor'), may hold values from -2 to 2
- conv_gain: float32 [1024], P(('dp', 'tensor')), may hold values from 0.5 to 1.5
- conv_up: bfloat16 [1024, 2, 1024], P('dp', None, 'tensor'), may hold values from -0.1875 to 0.1875
- conv_depth: float32 [5, 1024], P(None, 'tensor'), may hold values from -2.5 to 2.5
- bn_scale: float32 [1024], P('tensor'), may hold values from 0.5 to 1.5
- bn_shift: float32 [1024], P('tensor'), may hold values from -1 to 1
- conv_down: bfloat16 [1024, 1024], P('tensor', 'dp'), may hold values from -0.25 to 0.25
- ffn2_gain: float32 [1024], P(('dp', 'tensor')), may hold values from 0.5 to 1.5
- ffn2_up: bfloat16 [1024, 4096], P(None, 'tensor'), may hold values from -0.1875 to 0.1875
- ffn2_down: bfloat16 [4096, 1024], P('tensor'), may hold values from -0.1875 to 0.1875
- final_gain: float32 [1024], P(('dp', 'tensor')), may hold values from 0.5 to 1.5
- cotangent: bfloat16 [16, 256, 1024], P('dp', 'tensor'), may hold values from -6 to 6
Outputs:
- layer_out: bfloat16 [16, 256, 1024], P('dp', 'tensor')
- frames_grad: float32 [16, 256, 1024], P('dp', 'tensor')
- mask_vector_grad: float32 [1024], P(('dp', 'tensor'))
- ffn1_gain_grad: float32 [1024], P(('dp', 'tensor'))
- ffn1_up_grad: float32 [1024, 4096], P('dp', 'tensor')
- ffn1_down_grad: float32 [4096, 1024], P('tensor', 'dp')
- attn_gain_grad: float32 [1024], P(('dp', 'tensor'))
- query_weight_grad: float32 [1024, 1024], P('dp', 'tensor')
- key_weight_grad: float32 [1024, 1024], P('dp', 'tensor')
- value_weight_grad: float32 [1024, 1024], P('dp', 'tensor')
- output_weight_grad: float32 [1024, 1024], P('tensor', 'dp')
- rel_slope_grad: float32 [8], P('tensor')
- conv_gain_grad: float32 [1024], P(('dp', 'tensor'))
- conv_up_grad: float32 [1024, 2, 1024], P('dp', None, 'tensor')
- conv_depth_grad: float32 [5, 1024], P(None, 'tensor')
- bn_scale_grad: float32 [1024], P('tensor')
- bn_shift_grad: float32 [1024], P('tensor')
- conv_down_grad: float32 [1024, 1024], P('tensor', 'dp')
- ffn2_gain_grad: float32 [1024], P(('dp', 'tensor'))
- ffn2_up_grad: float32 [1024, 4096], P('dp', 'tensor')
- ffn2_down_grad: float32 [4096, 1024], P('tensor', 'dp')
- final_gain_grad: float32 [1024], P(('dp', 'tensor'))
The draws below stay inside these ranges and needn't reach their ends.
Inputs may be any that keep to these rules, and one draw needn't show every extreme that they name: `lengths`: the valid frames of an utterance are its first ones; in every draw some utterance has 256 valid frames and some has 128. `span_starts`: A start of 256 marks an unused span slot; used slots come first, and each utterance uses from 8 to 31 of them. Spans may intersect one another and the padding.
All inputs are finite; a program needn't handle non-finite values.
Results may differ from the reference program's by a relative error of at most 0.04.
Values may be sent and summed in bfloat16 or wider, within the bound.
No kernel may reach another device: no remote copies, remote signals or barrier semaphores. Data moves between devices by JAX's collectives and lax.ppermute only.
A program may use at most 128 MiB of HBM per device.

```python
import jax
import jax.numpy as jnp
from jax import lax

D = 1024
FF = 4096
H = 8
DH = 128
C = 1024
KW = 5
LEN = 256
MB = 2
SPAN = 10
REACH = 128
NSPAN = 32
UTTS = 16


def draw_lengths(key, part):
    drawn_values = jax.random.randint(jax.random.fold_in(key, 11), (UTTS,), LEN // 2, LEN + 1)
    chosen = jax.random.randint(jax.random.fold_in(key, 12), (), 0, UTTS)
    places = jnp.arange(UTTS)
    drawn_values = jnp.where(places == chosen, LEN, drawn_values)
    drawn_values = jnp.where(places == (chosen + 1) % UTTS, LEN // 2, drawn_values)
    return drawn_values.astype(jnp.int32)


def draw_span_starts(key, part):
    starts = jax.random.randint(jax.random.fold_in(key, 21), (UTTS, NSPAN), 0, LEN - SPAN + 1)
    counts = jax.random.randint(jax.random.fold_in(key, 22), (UTTS, 1), NSPAN // 4, NSPAN)
    starts = jnp.where(jnp.arange(NSPAN)[None, :] < counts, starts, LEN)
    return starts.astype(jnp.int32)


def level_of(key, dims, shards, least, high):
    loudness, own = 1.0, jax.random.fold_in(key, 6)
    for position, parts in shards:
        steps = jnp.exp(jax.random.uniform(jax.random.fold_in(own, position), (parts,), jnp.float32, least / len(shards), high / len(shards)))
        loudness = loudness * jnp.repeat(steps, dims[position] // parts).reshape([-1 if axis == position else 1 for axis in range(len(dims))])
    return loudness


def scatter_about(own_key, dims, width, bound, pieces=(), held_as=jnp.bfloat16):
    array = jax.random.normal(own_key, dims, jnp.float32) * width
    if len(pieces) > 0:
        array = level_of(own_key, dims, pieces, -0.22, 0.18) * array
    return jnp.clip(array, min=-bound, max=bound).astype(held_as)


def setup_inputs(seed: int = 0) -> dict:
    seeds = jax.random.split(jax.random.key(seed), 25)
    return {
        "frames": scatter_about(seeds[0], (UTTS, LEN, D), 1.0, 6.0, ((0, 8), (1, 4))),
        "lengths": draw_lengths(jax.random.fold_in(seeds[24], 71), 0),
        "span_starts": draw_span_starts(jax.random.fold_in(seeds[24], 71), 0),
        "mask_vector": scatter_about(seeds[3], (D,), 1.0, 6.0, ((0, 32),)),
        "ffn1_gain": jnp.clip(1.0 + 0.1 * jax.random.normal(seeds[4], (D,), jnp.float32), 0.5, 1.5),
        "ffn1_up": scatter_about(seeds[5], (D, FF), D ** -0.5, 0.1875, ((1, 4),)),
        "ffn1_down": scatter_about(seeds[6], (FF, D), (FF // 4) ** -0.5, 0.1875, ((0, 4),)),
        "attn_gain": jnp.clip(1.0 + 0.1 * jax.random.normal(seeds[7], (D,), jnp.float32), 0.5, 1.5),
        "query_weight": scatter_about(seeds[8], (D, H * DH), D ** -0.5, 0.1875, ((1, 4),)),
        "key_weight": scatter_about(seeds[9], (D, H * DH), D ** -0.5, 0.1875, ((1, 4),)),
        "value_weight": scatter_about(seeds[10], (D, H * DH), D ** -0.5, 0.1875, ((1, 4),)),
        "output_weight": scatter_about(seeds[11], (H * DH, D), (D // 64) ** -0.5, 1.5, ((0, 4),)),
        "rel_slope": jnp.clip(jax.random.uniform(seeds[12], (H,), jnp.float32, -2.0, 2.0) * level_of(seeds[12], (H,), ((0, 4),), -0.4, 0.0), -2.0, 2.0),
        "conv_gain": jnp.clip(1.0 + 0.1 * jax.random.normal(seeds[13], (D,), jnp.float32), 0.5, 1.5),
        "conv_up": scatter_about(seeds[14], (D, 2, C), D ** -0.5, 0.1875, ((0, 8), (2, 4))),
        "conv_depth": scatter_about(seeds[15], (KW, C), KW ** -0.5, 2.5, ((1, 4),), jnp.float32),
        "bn_scale": jnp.clip(1.0 + 0.1 * jax.random.normal(seeds[16], (C,), jnp.float32), 0.5, 1.5),
        "bn_shift": jnp.clip(jax.random.uniform(seeds[17], (C,), jnp.float32, -1.0, 1.0) * level_of(seeds[17], (C,), ((0, 4),), -0.4, 0.0), -1.0, 1.0),
        "conv_down": scatter_about(seeds[18], (C, D), (C // 2) ** -0.5, 0.25, ((0, 4), (1, 8))),
        "ffn2_gain": jnp.clip(1.0 + 0.1 * jax.random.normal(seeds[19], (D,), jnp.float32), 0.5, 1.5),
        "ffn2_up": scatter_about(seeds[20], (D, FF), D ** -0.5, 0.1875, ((1, 4),)),
        "ffn2_down": scatter_about(seeds[21], (FF, D), (FF // 4) ** -0.5, 0.1875, ((0, 4),)),
        "final_gain": jnp.clip(1.0 + 0.1 * jax.random.normal(seeds[22], (D,), jnp.float32), 0.5, 1.5),
        "cotangent": scatter_about(seeds[23], (UTTS, LEN, D), 1.0, 6.0, ((0, 8), (1, 4))),
    }


@jax.custom_vjp
def low(v):
    return lax.optimization_barrier(v.astype(jnp.bfloat16)).astype(jnp.float32)

@jax.custom_vjp
def low_back(v):
    return v

def low_keep(v):
    return (low(v), None)

def low_pass(kept, grad):
    return (grad,)

def back_keep(v):
    return (v, None)

def back_low(kept, grad):
    return (low(grad),)
low.defvjp(low_keep, low_pass)
low_back.defvjp(back_keep, back_low)
HIGHEST = lax.Precision.HIGHEST
EPSILON = 1e-05
MASKED_SCORE = -1000000000.0

def product(left, right):
    return jnp.dot(left, right, precision=HIGHEST, preferred_element_type=jnp.float32)

def layer_norm(values, gain_row):
    centre = lax.optimization_barrier(jnp.mean(values, axis=-1, keepdims=True))
    centred = values - centre
    variance = lax.optimization_barrier(jnp.mean(centred * centred, axis=-1, keepdims=True))
    return centred * lax.rsqrt(variance + EPSILON) * gain_row

def feed_forward(stream, gain_row, up_weight, down_weight):
    normed = low(layer_norm(stream, gain_row))
    hidden = low_back(product(normed, up_weight))
    active = low(jax.nn.silu(hidden))
    return low_back(product(active, down_weight))

def attention(stream, gain_row, query_weight, key_weight, value_weight, output_weight, rel_slope, valid_row, relative):
    normed = low(layer_norm(stream, gain_row))
    query_rows = low_back(low(product(normed, query_weight))).reshape(LEN, H, DH)
    key_rows = low_back(low(product(normed, key_weight))).reshape(LEN, H, DH)
    value_rows = low_back(low(product(normed, value_weight))).reshape(LEN, H, DH)
    scores = jnp.einsum('qhd,khd->hqk', query_rows, key_rows, precision=HIGHEST) * DH ** (-0.5)
    scores = scores + rel_slope[:, None, None] * relative[None]
    scores = low_back(scores)
    scores = jnp.where(valid_row[None, None, :], scores, MASKED_SCORE)
    row_peak = lax.optimization_barrier(jnp.max(scores, axis=-1, keepdims=True))
    raised = jnp.exp(scores - row_peak)
    weights_soft = raised / lax.optimization_barrier(jnp.sum(raised, axis=-1, keepdims=True))
    context = jnp.einsum('hqk,khd->qhd', low(weights_soft), value_rows, precision=HIGHEST).reshape(LEN, H * DH)
    context = low(low_back(context))
    return low_back(product(context, output_weight))

def conv_front(stream, gain_row, up_weight, depth_weight, valid_row):
    normed = low(layer_norm(stream, gain_row))
    mixed = low_back(product(normed, up_weight.reshape(D, 2 * C)))
    gated_rows = mixed[:, :C] * jax.nn.sigmoid(mixed[:, C:]) * valid_row.astype(jnp.float32)[:, None]
    padded = jnp.pad(gated_rows, ((KW // 2, KW // 2), (0, 0)))
    convolved = depth_weight[0] * padded[0:LEN]
    for offset in range(1, KW):
        convolved = convolved + depth_weight[offset] * padded[offset:offset + LEN]
    return convolved

def forward_pass(params, valid, masked, relative):
    frames, mask_vector, ffn1_gain, ffn1_up, ffn1_down, attn_gain, query_weight, key_weight, value_weight, output_weight, rel_slope, conv_gain, conv_up, conv_depth, bn_scale, bn_shift, conv_down, ffn2_gain, ffn2_up, ffn2_down, final_gain = params

    def front_part(inputs):
        row_block, valid_row, masked_row = inputs
        mixed_in = jnp.where(masked_row[:, None], mask_vector[None, :], row_block)
        stream_one = mixed_in + 0.5 * feed_forward(mixed_in, ffn1_gain, ffn1_up, ffn1_down)
        stream_two = stream_one + attention(stream_one, attn_gain, query_weight, key_weight, value_weight, output_weight, rel_slope, valid_row, relative)
        return (stream_two, conv_front(stream_two, conv_gain, conv_up, conv_depth, valid_row))
    results = []
    for batch_index in range(MB):
        valid_part = valid[batch_index::MB]
        stream_two, convolved = lax.map(jax.checkpoint(front_part), (frames[batch_index::MB], valid_part, masked[batch_index::MB]))
        valid_col = valid_part.astype(jnp.float32)[:, :, None]
        frame_count = jnp.sum(valid_col)
        centre = lax.optimization_barrier(jnp.sum(convolved * valid_col, axis=(0, 1))) / frame_count
        centred = convolved - centre
        variance = lax.optimization_barrier(jnp.sum(centred * centred * valid_col, axis=(0, 1))) / frame_count
        bn_inverse = lax.rsqrt(variance + EPSILON)

        def rear_part(inputs, centre=centre, bn_inverse=bn_inverse):
            stream_in, conv_rows = inputs
            shaped = (conv_rows - centre) * bn_inverse * bn_scale + bn_shift
            activated = low(jax.nn.silu(shaped))
            stream_three = stream_in + low_back(product(activated, conv_down))
            stream_four = stream_three + 0.5 * feed_forward(stream_three, ffn2_gain, ffn2_up, ffn2_down)
            return layer_norm(stream_four, final_gain)
        results.append(lax.map(jax.checkpoint(rear_part), (stream_two, convolved)))
    return jnp.stack(results, axis=1).reshape(UTTS, LEN, D)

def reference(frames, lengths, span_starts, mask_vector, ffn1_gain, ffn1_up, ffn1_down, attn_gain, query_weight, key_weight, value_weight, output_weight, rel_slope, conv_gain, conv_up, conv_depth, bn_scale, bn_shift, conv_down, ffn2_gain, ffn2_up, ffn2_down, final_gain, cotangent):
    places = jnp.arange(LEN, dtype=jnp.int32)
    valid = places[None, :] < lengths[:, None]
    begins = span_starts[:, :, None]
    covered = jnp.any((begins <= places[None, None, :]) & (places[None, None, :] < begins + SPAN), axis=1)
    masked = covered & valid
    relative = jnp.clip(places[None, :] - places[:, None], -REACH, REACH).astype(jnp.float32) / REACH
    floats = (frames, mask_vector, ffn1_gain, ffn1_up, ffn1_down, attn_gain, query_weight, key_weight, value_weight, output_weight, rel_slope, conv_gain, conv_up, conv_depth, bn_scale, bn_shift, conv_down, ffn2_gain, ffn2_up, ffn2_down, final_gain)
    primals = tuple((entry.astype(jnp.float32) for entry in floats))

    def whole_layer(*params):
        return forward_pass(params, valid, masked, relative)
    result, pull_back = jax.vjp(whole_layer, *primals)
    gradients = pull_back(cotangent.astype(jnp.float32))
    return (result.astype(jnp.bfloat16), gradients[0], gradients[1], gradients[2], gradients[3], gradients[4], gradients[5], gradients[6], gradients[7], gradients[8], gradients[9], gradients[10], gradients[11], gradients[12], gradients[13], gradients[14], gradients[15], gradients[16], gradients[17], gradients[18], gradients[19], gradients[20])
```

```python
import jax
import jax.numpy as jnp
from jax import lax
from jax.sharding import PartitionSpec as P

DH = 128
KW = 5
SPAN = 10
REACH = 128
EPSILON = 1e-05
MASKED_SCORE = -1000000000.0
BF = jnp.bfloat16
F32 = jnp.float32


def product(left, right):
    return jnp.dot(left, right, preferred_element_type=F32)


def inner_rows(left, right):
    return lax.dot_general(left, right, (((0,), (0,)), ((), ())), preferred_element_type=F32)


def times_back(left, right):
    return lax.dot_general(left, right, (((1,), (1,)), ((), ())), preferred_element_type=F32)


def norm_unit(values):
    centre = jnp.mean(values, axis=-1, keepdims=True)
    centred = values - centre
    inverse = lax.rsqrt(jnp.mean(centred * centred, axis=-1, keepdims=True) + EPSILON)
    return centred * inverse, inverse


def norm_back(grad_out, unit_rows, inverse, norm_gain):
    grad_unit = grad_out * norm_gain
    first_mean = jnp.mean(grad_unit, axis=-1, keepdims=True)
    second_mean = jnp.mean(grad_unit * unit_rows, axis=-1, keepdims=True)
    return (
        inverse * (grad_unit - first_mean - unit_rows * second_mean),
        jnp.sum(grad_out * unit_rows, axis=0),
    )


def silu_slope(values):
    gate_value = jax.nn.sigmoid(values)
    return gate_value * (1.0 + values * (1.0 - gate_value))


def swap(value, axis, bit):
    size = lax.axis_size(axis)
    return lax.ppermute(value, axis, [(place, place ^ bit) for place in range(size)])


def bit_of(axis, bit):
    return (lax.axis_index(axis) & bit) != 0


def pick(value, axis, second):
    halves = (lax.index_in_dim(value, 0, axis, False), lax.index_in_dim(value, 1, axis, False))
    return jnp.where(second, halves[1], halves[0])


def ordered(mine, theirs, axis, second):
    return jnp.stack(
        [jnp.where(second, theirs, mine), jnp.where(second, mine, theirs)], axis=axis
    )


def widen(half):
    rows = half.shape[0] // 2
    other = swap(half, "tensor", 1)
    low = bit_of("tensor", 1)
    shape = (2, rows, half.shape[1])
    return ordered(half.reshape(shape), other.reshape(shape), 1, low).reshape(
        4 * rows, half.shape[1]
    )


def narrow(partial_sum):
    rows = partial_sum.shape[0] // 4
    low = bit_of("tensor", 1)
    blocks = partial_sum.reshape(2, 2, rows, partial_sum.shape[1])
    sent = pick(blocks, 1, jnp.logical_not(low)).astype(BF)
    summed = (pick(blocks, 1, low) + swap(sent, "tensor", 1).astype(F32)).astype(BF)
    return summed


def narrow_sum(partial_sum):
    summed = narrow(partial_sum)
    other = swap(summed, "tensor", 2)
    total = summed.astype(F32) + other.astype(F32)
    return total.reshape(total.shape[0] * total.shape[1], total.shape[2])


def narrow_last(partial_sum):
    summed = narrow(partial_sum)
    high = bit_of("tensor", 2)
    sent = pick(summed, 0, jnp.logical_not(high))
    return pick(summed, 0, high).astype(F32) + swap(sent, "tensor", 2).astype(F32)


def gather_axis(block, axis):
    size = lax.axis_size(axis)
    bit = size // 2
    held = block
    depth = 0
    while bit:
        held = ordered(held, swap(held, axis, bit), depth, bit_of(axis, bit))
        depth += 1
        bit //= 2
    return held.reshape((size,) + block.shape)


def sum_axis(value, axis):
    bit = 1
    while bit < lax.axis_size(axis):
        value = value + swap(value, axis, bit)
        bit *= 2
    return value


def scatter_rows(partial_sum):
    size = lax.axis_size("dp")
    rows, columns = partial_sum.shape
    levels = size.bit_length() - 1
    held = partial_sum.reshape((2,) * levels + (rows // size, columns))
    for level in range(levels):
        axis = levels - 1 - level
        mine = bit_of("dp", 1 << level)
        sent = pick(held, axis, jnp.logical_not(mine)).astype(BF)
        held = pick(held, axis, mine) + swap(sent, "dp", 1 << level).astype(F32)
    return held


def relative_table(length):
    places = jnp.arange(length, dtype=jnp.int32)
    return jnp.clip(places[None, :] - places[:, None], -REACH, REACH).astype(F32) / REACH


def depthwise(padded, depth_weight, length):
    convolved = depth_weight[0] * padded[0:length]
    for offset in range(1, KW):
        convolved = convolved + depth_weight[offset] * padded[offset : offset + length]
    return convolved


def heads_of(rows, head_count):
    return rows.reshape(rows.shape[0], head_count, DH)


def attend(gathered, query_weight, key_weight, value_weight, slopes, relative, valid_keys):
    head_count = slopes.shape[0]
    length = gathered.shape[0]
    query = heads_of(product(gathered, query_weight).astype(BF), head_count)
    keys = heads_of(product(gathered, key_weight).astype(BF), head_count)
    values = heads_of(product(gathered, value_weight).astype(BF), head_count)
    scores = jnp.einsum("qhd,khd->hqk", query, keys, preferred_element_type=F32) * DH ** (-0.5)
    scores = scores + slopes[:, None, None] * relative[None]
    scores = jnp.where(valid_keys[None, None, :], scores, MASKED_SCORE)
    raised = jnp.exp(scores - jnp.max(scores, axis=-1, keepdims=True))
    weights = raised / jnp.sum(raised, axis=-1, keepdims=True)
    context = jnp.einsum("hqk,khd->qhd", weights.astype(BF), values, preferred_element_type=F32)
    context = context.reshape(length, head_count * DH).astype(BF)
    return context, (query, keys, values, weights)


def attend_back(grad_context, kept, relative):
    query, keys, values, weights = kept
    length, head_count, _ = query.shape
    grad_heads = heads_of(grad_context, head_count)
    width = head_count * DH
    grad_value = jnp.einsum(
        "hqk,qhd->khd", weights.astype(BF), grad_heads, preferred_element_type=F32
    )
    grad_weights = jnp.einsum("qhd,khd->hqk", grad_heads, values, preferred_element_type=F32)
    grad_scores = weights * (
        grad_weights - jnp.sum(weights * grad_weights, axis=-1, keepdims=True)
    )
    grad_scores = grad_scores.astype(BF)
    grad_slopes = jnp.sum(grad_scores.astype(F32) * relative[None], axis=(1, 2))
    grad_query = jnp.einsum("hqk,khd->qhd", grad_scores, keys, preferred_element_type=F32)
    grad_key = jnp.einsum("hqk,qhd->khd", grad_scores, query, preferred_element_type=F32)
    grads = tuple(
        (part * scale).reshape(length, width).astype(BF)
        for part, scale in (
            (grad_query, DH ** (-0.5)),
            (grad_key, DH ** (-0.5)),
            (grad_value, 1.0),
        )
    )
    return grads, grad_slopes


def both(parts):
    return jnp.concatenate(parts, axis=0)


def per_device(
    frames,
    lengths,
    span_starts,
    mask_vector,
    ffn1_gain,
    ffn1_up,
    ffn1_down,
    attn_gain,
    query_weight,
    key_weight,
    value_weight,
    output_weight,
    rel_slope,
    conv_gain,
    conv_up,
    conv_depth,
    bn_scale,
    bn_shift,
    conv_down,
    ffn2_gain,
    ffn2_up,
    ffn2_down,
    final_gain,
    cotangent,
):
    batches, row_count, width = frames.shape
    length = row_count * lax.axis_size("tensor")
    low_bit = bit_of("tensor", 1)
    high_bit = bit_of("tensor", 2)
    relative = relative_table(length)
    places = jnp.arange(length, dtype=jnp.int32)
    channels = conv_depth.shape[1]
    each = range(batches)

    small = jnp.stack(
        [mask_vector.astype(F32), ffn1_gain, attn_gain, conv_gain, ffn2_gain, final_gain]
    )
    small = gather_axis(gather_axis(small, "tensor"), "dp")
    small = jnp.moveaxis(small, 2, 0).reshape(6, width)
    mask_full, gain_one, gain_attn, gain_conv, gain_two, gain_final = (
        small[index] for index in range(6)
    )

    halves = ordered(frames, swap(frames, "tensor", 2), 1, high_bit)
    others = swap(halves, "tensor", 1)
    wholes = ordered(halves, others, 2, low_bit).reshape(batches, length, width)
    grads_out = ordered(cotangent, swap(cotangent, "tensor", 2), 1, high_bit)
    grads_out = grads_out.reshape(batches, 2 * row_count, width)

    up_full = gather_axis(conv_up.reshape(conv_up.shape[0], 2 * channels), "dp")
    up_full = up_full.reshape(width, 2 * channels)
    down_full = gather_axis(conv_down, "dp")
    down_full = jnp.moveaxis(down_full, 0, 1).reshape(conv_down.shape[0], width)

    def half_of(whole):
        blocks = whole.reshape((2, 2, row_count) + whole.shape[1:])
        return pick(blocks, 1, low_bit).reshape((2 * row_count,) + whole.shape[1:])

    valid = [places < lengths[b] for b in each]
    valid_col = [valid[b].astype(F32)[:, None] for b in each]
    masked, masked_half = [], []
    for b in each:
        starts = span_starts[b]
        covered = jnp.any(
            (starts[:, None] <= places[None, :]) & (places[None, :] < starts[:, None] + SPAN),
            axis=0,
        )
        masked.append(covered & valid[b])
        masked_half.append(half_of(masked[b]))

    unit_in, inv_in, gathered_one, hidden_one, active_one, stream_one = [], [], [], [], [], []
    for b in each:
        inputs = jnp.where(masked[b][:, None], mask_full[None, :], wholes[b].astype(F32))
        unit_rows, inverse = norm_unit(inputs)
        gathered_one.append((unit_rows * gain_one).astype(BF))
        inputs_half = half_of(inputs)
        hidden_one.append(product(gathered_one[b], ffn1_up))
        active_one.append(jax.nn.silu(hidden_one[b]).astype(BF))
        branch = narrow_sum(product(active_one[b], ffn1_down))
        stream_one.append(inputs_half + 0.5 * branch)

    unit_attn, inv_attn, gathered_attn, kept_attn, context, stream_two = [], [], [], [], [], []
    for b in each:
        unit_rows, inverse = norm_unit(stream_one[b])
        unit_attn.append(unit_rows)
        inv_attn.append(inverse)
        gathered_attn.append(widen((unit_rows * gain_attn).astype(BF)))
        rows, kept = attend(
            gathered_attn[b], query_weight, key_weight, value_weight, rel_slope, relative, valid[b]
        )
        context.append(rows)
        kept_attn.append(kept)
        stream_two.append(stream_one[b] + narrow_sum(product(rows, output_weight)))

    unit_conv, inv_conv, gathered_conv, value_half, gate, padded, convolved = (
        [], [], [], [], [], [], []
    )
    stats = []
    for b in each:
        unit_rows, inverse = norm_unit(stream_two[b])
        unit_conv.append(unit_rows)
        inv_conv.append(inverse)
        gathered_conv.append(widen((unit_rows * gain_conv).astype(BF)))
        mixed = product(gathered_conv[b], up_full)
        value_half.append(mixed[:, :channels])
        gate.append(jax.nn.sigmoid(mixed[:, channels:]))
        gated = value_half[b] * gate[b] * valid_col[b]
        padded.append(jnp.pad(gated, ((KW // 2, KW // 2), (0, 0))))
        convolved.append(depthwise(padded[b], conv_depth, length))
        count = lengths[b].astype(F32)
        mean = jnp.sum(convolved[b] * valid_col[b], axis=0) / count
        centred = (convolved[b] - mean) * valid_col[b]
        spread = jnp.sum(centred * centred, axis=0)
        held = jnp.stack([jnp.broadcast_to(count, mean.shape), mean, spread])
        bit = 1
        while bit < lax.axis_size("dp"):
            theirs = swap(held, "dp", bit)
            total = held[0] + theirs[0]
            apart = held[1] - theirs[1]
            held = jnp.stack(
                [
                    total,
                    (held[0] * held[1] + theirs[0] * theirs[1]) / total,
                    held[2] + theirs[2] + apart * apart * (held[0] * theirs[0] / total),
                ]
            )
            bit *= 2
        stats.append((held[0], held[1], lax.rsqrt(held[2] / held[0] + EPSILON)))

    unit_bn, centred_conv, shaped, activated, stream_three = [], [], [], [], []
    for b in each:
        count, centre, bn_inverse = stats[b]
        centred_conv.append(convolved[b] - centre)
        unit_bn.append(centred_conv[b] * bn_inverse)
        shaped.append(unit_bn[b] * bn_scale + bn_shift)
        activated.append(jax.nn.silu(shaped[b]).astype(BF))
        stream_three.append(stream_two[b] + narrow_sum(product(activated[b], down_full)))

    unit_two, inv_two, gathered_two, hidden_two, active_two = [], [], [], [], []
    outputs, grad_four, grad_final = [], [], []
    for b in each:
        unit_rows, inverse = norm_unit(stream_three[b])
        unit_two.append(unit_rows)
        inv_two.append(inverse)
        gathered_two.append(widen((unit_rows * gain_two).astype(BF)))
        hidden_two.append(product(gathered_two[b], ffn2_up))
        active_two.append(jax.nn.silu(hidden_two[b]).astype(BF))
        branch = narrow_sum(product(active_two[b], ffn2_down))
        stream_four = stream_three[b] + 0.5 * branch
        unit_rows, inverse = norm_unit(stream_four)
        rows_out = (unit_rows * gain_final).astype(BF)
        outputs.append(pick(rows_out.reshape(2, row_count, width), 0, high_bit))
        grad, gain_sum = norm_back(grads_out[b].astype(F32), unit_rows, inverse, gain_final)
        grad_four.append(grad)
        grad_final.append(gain_sum)

    grad_three, grad_gain_two, branch_grads, hidden_grads = [], [], [], []
    for b in each:
        grad_branch = widen((0.5 * grad_four[b]).astype(BF))
        branch_grads.append(grad_branch)
        grad_hidden = (times_back(grad_branch, ffn2_down) * silu_slope(hidden_two[b])).astype(BF)
        hidden_grads.append(grad_hidden)
        grad_normed = narrow_sum(times_back(grad_hidden, ffn2_up))
        grad, gain_sum = norm_back(grad_normed, unit_two[b], inv_two[b], gain_two)
        grad_three.append(grad_four[b] + grad)
        grad_gain_two.append(gain_sum)
    ffn2_down_grad = scatter_rows(inner_rows(both(branch_grads), both(active_two))).T
    ffn2_up_grad = scatter_rows(inner_rows(both(gathered_two), both(hidden_grads)))

    grad_shaped, sums_bn, branch_grads = [], [], []
    for b in each:
        grad_branch = widen(grad_three[b].astype(BF))
        branch_grads.append(grad_branch)
        grad_shaped.append(times_back(grad_branch, down_full) * silu_slope(shaped[b]))
        sums_bn.append(
            sum_axis(
                jnp.stack(
                    [
                        jnp.sum(grad_shaped[b], axis=0),
                        jnp.sum(grad_shaped[b] * unit_bn[b], axis=0),
                    ]
                ),
                "dp",
            )
        )
    conv_down_grad = scatter_rows(inner_rows(both(branch_grads), both(activated))).T
    grad_two, grad_gain_conv, mixed_grads, grad_depth = [], [], [], None
    for b in each:
        count, centre, bn_inverse = stats[b]
        sum_shift, sum_scale = sums_bn[b][0], sums_bn[b][1]
        grad_centre = -bn_inverse * bn_scale * sum_shift
        grad_spread = -bn_inverse * bn_inverse * bn_scale * sum_scale
        grad_conv = (
            grad_shaped[b] * bn_scale * bn_inverse
            + valid_col[b] * (grad_centre + grad_spread * centred_conv[b]) / count
        )
        grad_padded = jnp.pad(grad_conv, ((KW // 2, KW // 2), (0, 0)))
        grad_gated = conv_depth[0] * grad_padded[2 * (KW // 2) : 2 * (KW // 2) + length]
        for offset in range(1, KW):
            begin = 2 * (KW // 2) - offset
            grad_gated = grad_gated + conv_depth[offset] * grad_padded[begin : begin + length]
        fresh = jnp.stack(
            [
                jnp.sum(grad_conv * padded[b][offset : offset + length], axis=0)
                for offset in range(KW)
            ]
        )
        grad_depth = fresh if grad_depth is None else grad_depth + fresh
        grad_gated = grad_gated * valid_col[b]
        grad_mixed = jnp.concatenate(
            [
                grad_gated * gate[b],
                grad_gated * value_half[b] * gate[b] * (1.0 - gate[b]),
            ],
            axis=1,
        ).astype(BF)
        mixed_grads.append(grad_mixed)
        grad_normed = narrow_sum(times_back(grad_mixed, up_full))
        grad, gain_sum = norm_back(grad_normed, unit_conv[b], inv_conv[b], gain_conv)
        grad_two.append(grad_three[b] + grad)
        grad_gain_conv.append(gain_sum)
    conv_up_grad = scatter_rows(inner_rows(both(gathered_conv), both(mixed_grads)))

    grad_one, grad_gain_attn, branch_grads, three_grads, grad_slopes = [], [], [], [], None
    for b in each:
        grad_branch = widen(grad_two[b].astype(BF))
        branch_grads.append(grad_branch)
        grad_context = times_back(grad_branch, output_weight).astype(BF)
        (grad_query, grad_key, grad_value), fresh = attend_back(
            grad_context, kept_attn[b], relative
        )
        grad_slopes = fresh if grad_slopes is None else grad_slopes + fresh
        three_grads.append(jnp.concatenate([grad_query, grad_key, grad_value], axis=1))
        grad_normed = narrow_sum(
            times_back(grad_query, query_weight)
            + times_back(grad_key, key_weight)
            + times_back(grad_value, value_weight)
        )
        grad, gain_sum = norm_back(grad_normed, unit_attn[b], inv_attn[b], gain_attn)
        grad_one.append(grad_two[b] + grad)
        grad_gain_attn.append(gain_sum)
    output_grad = scatter_rows(inner_rows(both(branch_grads), both(context))).T
    qkv_grad = scatter_rows(inner_rows(both(gathered_attn), both(three_grads)))

    branch_grads, hidden_grads, last_normed = [], [], []
    for b in each:
        grad_branch = widen((0.5 * grad_one[b]).astype(BF))
        branch_grads.append(grad_branch)
        grad_hidden = (times_back(grad_branch, ffn1_down) * silu_slope(hidden_one[b])).astype(BF)
        hidden_grads.append(grad_hidden)
        last_normed.append(narrow_last(times_back(grad_hidden, ffn1_up)))
    ffn1_down_grad = scatter_rows(inner_rows(both(branch_grads), both(active_one))).T
    ffn1_up_grad = scatter_rows(inner_rows(both(gathered_one), both(hidden_grads)))
    frames_grad, grad_mask, grad_gain_one = [], [], []
    for b in each:
        hit = pick(masked_half[b].reshape(2, row_count), 0, high_bit)
        inputs = jnp.where(hit[:, None], mask_full[None, :], frames[b].astype(F32))
        unit_rows, inverse = norm_unit(inputs)
        grad, gain_sum = norm_back(last_normed[b], unit_rows, inverse, gain_one)
        grad = pick(grad_one[b].reshape(2, row_count, width), 0, high_bit) + grad
        frames_grad.append(jnp.where(hit[:, None], 0.0, grad))
        grad_mask.append(jnp.sum(jnp.where(hit[:, None], grad, 0.0), axis=0))
        grad_gain_one.append(gain_sum)

    gains = jnp.stack(
        [
            sum(grad_mask),
            sum(grad_gain_one),
            0.5 * sum(grad_gain_attn),
            0.5 * sum(grad_gain_conv),
            0.5 * sum(grad_gain_two),
            0.5 * sum(grad_final),
        ]
    )
    gains = sum_axis(sum_axis(gains, "tensor"), "dp")
    part = mask_vector.shape[0]
    place = lax.axis_index("dp") * lax.axis_size("tensor") + lax.axis_index("tensor")
    gains = lax.dynamic_slice_in_dim(gains, place * part, part, axis=1)

    head_count = rel_slope.shape[0]
    depth_slope = jnp.concatenate(
        [grad_depth, jnp.pad(grad_slopes[None], ((0, 0), (0, channels - head_count)))]
    )
    depth_slope = sum_axis(depth_slope, "dp")
    wide = query_weight.shape[1]

    return (
        jnp.stack(outputs),
        jnp.stack(frames_grad),
        gains[0],
        gains[1],
        ffn1_up_grad,
        ffn1_down_grad,
        gains[2],
        qkv_grad[:, :wide],
        qkv_grad[:, wide : 2 * wide],
        qkv_grad[:, 2 * wide :],
        output_grad,
        depth_slope[KW, :head_count],
        gains[3],
        conv_up_grad.reshape(conv_up.shape),
        depth_slope[:KW],
        sums_bn[0][1] + sums_bn[1][1],
        sums_bn[0][0] + sums_bn[1][0],
        conv_down_grad,
        gains[4],
        ffn2_up_grad,
        ffn2_down_grad,
        gains[5],
    )


def solution(mesh):
    every, split, columns = P(("dp", "tensor")), P("tensor"), P(None, "tensor")
    rows_by = P("dp", "tensor", None)
    return jax.shard_map(
        per_device,
        mesh=mesh,
        in_specs=(
            rows_by,
            P("dp"),
            P("dp", None),
            every,
            every,
            columns,
            P("tensor", None),
            every,
            columns,
            columns,
            columns,
            P("tensor", None),
            split,
            every,
            P("dp", None, "tensor"),
            columns,
            split,
            split,
            P("tensor", "dp"),
            every,
            columns,
            P("tensor", None),
            every,
            rows_by,
        ),
        out_specs=(
            rows_by,
            rows_by,
            every,
            every,
            P("dp", "tensor"),
            P("tensor", "dp"),
            every,
            P("dp", "tensor"),
            P("dp", "tensor"),
            P("dp", "tensor"),
            P("tensor", "dp"),
            split,
            every,
            P("dp", None, "tensor"),
            columns,
            split,
            split,
            P("tensor", "dp"),
            every,
            P("dp", "tensor"),
            P("tensor", "dp"),
            every,
        ),
        check_vma=False,
    )
```

```python
import functools

import jax
import jax.numpy as jnp
from jax import lax
from jax.experimental import pallas as pl
from jax.experimental.pallas import tpu as pltpu
from jax.sharding import PartitionSpec as P

DH = 128
KW = 5
SPAN = 10
REACH = 128
EPSILON = 1e-05
MASKED_SCORE = -1000000000.0
BF = jnp.bfloat16
F32 = jnp.float32
STEP = 32
TILE = 256
EDGE = 8
MIB = 1024 * 1024
COST = 30_000_000

VMEM_SPEC = pl.BlockSpec(memory_space=pltpu.VMEM)
SMEM_SPEC = pl.BlockSpec(memory_space=pltpu.SMEM)


def product(left, right):
    return jnp.dot(left, right, preferred_element_type=F32)


def inner_rows(left, right):
    return lax.dot_general(left, right, (((0,), (0,)), ((), ())), preferred_element_type=F32)


def times_back(left, right):
    return lax.dot_general(left, right, (((1,), (1,)), ((), ())), preferred_element_type=F32)


def sigmoid(values):
    return 0.5 * jnp.tanh(0.5 * values) + 0.5


def norm_unit(values):
    centre = jnp.mean(values, axis=-1, keepdims=True)
    centred = values - centre
    inverse = lax.rsqrt(jnp.mean(centred * centred, axis=-1, keepdims=True) + EPSILON)
    return centred * inverse, inverse


def norm_back(grad_out, unit_rows, inverse, norm_gain):
    grad_unit = grad_out * norm_gain
    first_mean = jnp.mean(grad_unit, axis=-1, keepdims=True)
    second_mean = jnp.mean(grad_unit * unit_rows, axis=-1, keepdims=True)
    return (
        inverse * (grad_unit - first_mean - unit_rows * second_mean),
        jnp.sum(grad_out * unit_rows, axis=0, keepdims=True),
    )


def silu_slope(values):
    gate_value = sigmoid(values)
    return gate_value * (1.0 + values * (1.0 - gate_value))


def over_rows(count, body, init=0, step=STEP):
    def one(index, carry):
        return body(pl.ds(pl.multiple_of(index * step, step), step), index * step, carry)

    return lax.fori_loop(0, count // step, one, init)


def row_iota(first, rows, columns):
    return first + lax.broadcasted_iota(jnp.int32, (rows, columns), 0)


def mask_col(starts_ref, first, rows, length):
    starts = starts_ref[...]
    at = row_iota(first, rows, starts.shape[1])
    hit = (starts <= at) & (at < starts + SPAN) & (at < length)
    return jnp.max(jnp.where(hit, 1.0, 0.0), axis=1, keepdims=True)


def valid_col(first, rows, columns, length):
    return jnp.where(row_iota(first, rows, columns) < length, 1.0, 0.0)


def masked_rows(frame_rows, mask, mask_row):
    return jnp.where(
        jnp.broadcast_to(mask, frame_rows.shape) > 0.5, mask_row, frame_rows.astype(F32)
    )


def pair_sum(mine, theirs, rows):
    return mine[rows, :].astype(F32) + theirs[rows, :].astype(F32)


class Late:
    def __init__(self, source, held, semaphore):
        self.copy = pltpu.make_async_copy(source, held, semaphore)
        self.copy.start()
        self.held, self.shape, self.dtype, self.waited = held, held.shape, held.dtype, False

    def arrive(self):
        if not self.waited:
            self.copy.wait()
            self.waited = True

    def __getitem__(self, index):
        assert self.waited
        return self.held[index]


class Leaving:
    def __init__(self, target, held, semaphore):
        self.copy = pltpu.make_async_copy(held, target, semaphore)
        self.held, self.shape, self.dtype, self.started = held, held.shape, held.dtype, False

    def leave(self):
        if not self.started:
            self.copy.start()
            self.started = True

    def finish(self):
        self.leave()
        self.copy.wait()

    def __getitem__(self, index):
        return self.held[index]

    def __setitem__(self, index, value):
        assert not self.started
        self.held[index] = value


def arrive(*refs):
    for ref in refs:
        if isinstance(ref, Late):
            ref.arrive()


def leave(*refs):
    for ref in refs:
        if isinstance(ref, Leaving):
            ref.leave()


def columns(index, size=TILE):
    return slice(index * size, (index + 1) * size)


def ffn_up(branch, ups, hidden, active_own, active_cross):
    normed = branch[...]
    for shard, weight in enumerate(ups):
        arrive(weight)
        tiles = weight.shape[1] // TILE
        for index in range(tiles):
            at = columns(index)
            values = product(normed, weight[:, at])
            hidden[:, columns(index + shard * tiles)] = values
            (active_own, active_cross)[shard][:, at] = (values * sigmoid(values)).astype(BF)


def ffn_down(active_own, active_cross, downs, part):
    width = downs[0].shape[1]
    own, cross = active_own[...], active_cross[...]
    arrive(*downs)
    for index in range(width // TILE):
        at = columns(index)
        part[:, at] = (product(own, downs[0][:, at]) + product(cross, downs[1][:, at])).astype(BF)


def ffn_grad_hidden(branch, downs, hidden, grad_own, grad_cross):
    grad_branch = branch[...]
    for shard, weight in enumerate(downs):
        arrive(weight)
        tiles = weight.shape[0] // TILE
        for index in range(tiles):
            at = columns(index)
            slope = silu_slope(hidden[:, columns(index + shard * tiles)])
            grad = (times_back(grad_branch, weight[at, :]) * slope).astype(BF)
            (grad_own, grad_cross)[shard][:, at] = grad


def ffn_grad_input(grad_own, grad_cross, ups, store):
    own, cross = grad_own[...], grad_cross[...]
    arrive(*ups)
    for index in range(ups[0].shape[0] // TILE):
        at = columns(index)
        store(at, times_back(own, ups[0][at, :]) + times_back(cross, ups[1][at, :]))


def k_pick(info, block, across_block, sent):
    core = info[0]
    sent[0] = block[pl.ds(1 - core, 1)][0]
    sent[1] = across_block[pl.ds(1 - core, 1)][0]


def place_rows(info, block, across_block, arrived, whole):
    core, high = info[0], info[1]
    rows = block.shape[1]
    places = (
        (2 * high + core, block[pl.ds(core, 1)][0]),
        (2 * (1 - high) + core, across_block[pl.ds(core, 1)][0]),
        (2 * high + 1 - core, arrived[0]),
        (2 * (1 - high) + 1 - core, arrived[1]),
    )
    for place, value in places:
        whole[pl.ds(pl.multiple_of(place * rows, rows), rows), :] = value


def k_ffn_one(
    info, starts, block, across_block, arrived, small, up_o, up_t, down_o, down_t,
    frames, branch, active_cross, active_own, hidden, part, whole,
):
    length = info[2]
    rows, width = whole.shape
    place_rows(info, block, across_block, arrived, whole)
    frames[...] = whole[...]

    def normalise(at, first, carry):
        mask = mask_col(starts, first, STEP, length)
        unit_rows, _ = norm_unit(masked_rows(whole[at, :], mask, small[0:1, :]))
        branch[at, :] = (unit_rows * small[1:2, :]).astype(BF)
        return carry

    over_rows(rows, normalise)
    ffn_up(branch, (up_o, up_t), hidden, active_own, active_cross)
    ffn_down(active_own, active_cross, (down_o, down_t), part)


def k_attn(
    info, starts, slopes, mine, theirs, frames, small, qkv_o, qkv_t, out_o, out_t,
    stream, branch, context_cross, context_own, qkv, weights, part,
):
    length = info[2]
    rows, width = frames.shape
    arrive(frames)

    def normalise(at, first, carry):
        mask = mask_col(starts, first, STEP, length)
        inputs = masked_rows(frames[at, :], mask, small[0:1, :])
        values = inputs + 0.5 * pair_sum(mine, theirs, at)
        stream[at, :] = values
        unit_rows, _ = norm_unit(values)
        branch[at, :] = (unit_rows * small[2:3, :]).astype(BF)
        return carry

    over_rows(rows, normalise)
    normed = branch[...]
    third = qkv_o.shape[1] // 3
    for shard, weight in enumerate((qkv_o, qkv_t)):
        arrive(weight)
        for index in range(3):
            at = columns(index, third)
            qkv[:, columns(3 * shard + index, third)] = product(normed, weight[:, at]).astype(BF)
    heads = third // DH
    span = rows // 2
    for shard in range(2):
        base = 3 * third * shard
        for head in range(heads):
            place = shard * heads + head
            key = qkv[:, base + third + head * DH : base + third + (head + 1) * DH]
            value = qkv[:, base + 2 * third + head * DH : base + 2 * third + (head + 1) * DH]
            for part_index in range(2):
                at = columns(part_index, span)
                query = qkv[at, base + head * DH : base + (head + 1) * DH]
                scores = times_back(query, key) * DH ** (-0.5)
                key_place = lax.broadcasted_iota(jnp.int32, (span, rows), 1)
                away = key_place - row_iota(part_index * span, span, rows)
                relative = jnp.clip(away, -REACH, REACH).astype(F32) * (1.0 / REACH)
                scores = scores + slopes[place] * relative
                scores = jnp.where(key_place < length, scores, MASKED_SCORE)
                raised = jnp.exp(scores - jnp.max(scores, axis=-1, keepdims=True))
                soft = raised * (1.0 / jnp.sum(raised, axis=-1, keepdims=True))
                weights[place, at, :] = soft
                context = product(soft.astype(BF), value).astype(BF)
                if shard == 0:
                    context_own[at, columns(head, DH)] = context
                else:
                    context_cross[at, columns(head, DH)] = context
    arrive(out_o, out_t)
    own = context_own[...]
    other = context_cross[...]
    for index in range(width // TILE):
        at = columns(index)
        part[:, at] = (product(own, out_o[:, at]) + product(other, out_t[:, at])).astype(BF)


def k_conv_front(
    info, mine, theirs, stream_in, small, params, conv_o, conv_t,
    stream, normed, value, gate, padded, convolved, stats,
):
    length = info[2]
    rows, width = stream_in.shape
    channels = params.shape[1] // 2
    arrive(stream_in)

    def normalise(at, first, carry):
        values = stream_in[at, :] + pair_sum(mine, theirs, at)
        stream[at, :] = values
        unit_rows, _ = norm_unit(values)
        normed[at, :] = (unit_rows * small[3:4, :]).astype(BF)
        return carry

    over_rows(rows, normalise)
    normed_rows = normed[...]
    edge = jnp.zeros((EDGE, 2 * channels), F32)
    padded[:EDGE, :] = edge
    padded[EDGE + rows :, :] = edge
    for shard, weight in enumerate((conv_o, conv_t)):
        arrive(weight)
        at = columns(shard, channels)
        value_rows = product(normed_rows, weight[:, :channels])
        value[:, at] = value_rows
        gate_rows = sigmoid(product(normed_rows, weight[:, channels : 2 * channels]))
        gate[:, at] = gate_rows
        padded[EDGE : EDGE + rows, at] = (
            value_rows * gate_rows * valid_col(0, rows, channels, length)
        )
    count = length.astype(F32)
    for tile in range(2 * channels // DH):
        at = columns(tile, DH)
        total = params[0:1, at] * padded[EDGE - 2 : EDGE - 2 + rows, at]
        for offset in range(1, KW):
            begin = EDGE - 2 + offset
            total = total + params[offset : offset + 1, at] * padded[begin : begin + rows, at]
        convolved[:, at] = total
        keep = valid_col(0, rows, DH, length)
        mean = jnp.sum(total * keep, axis=0, keepdims=True) / count
        centred = (total - mean) * keep
        stats[0:1, at] = jnp.full((1, DH), count, F32)
        stats[1:2, at] = mean
        stats[2:3, at] = jnp.sum(centred * centred, axis=0, keepdims=True)
        stats[3:8, at] = jnp.zeros((5, DH), F32)


def merged(mine, theirs):
    total = mine[0:1, :] + theirs[0:1, :]
    apart = mine[1:2, :] - theirs[1:2, :]
    mean = (mine[0:1, :] * mine[1:2, :] + theirs[0:1, :] * theirs[1:2, :]) / total
    share = mine[0:1, :] * theirs[0:1, :] / total
    spread = mine[2:3, :] + theirs[2:3, :] + apart * apart * share
    return total, mean, spread


def k_merge(mine, theirs, result):
    total, mean, spread = merged(mine, theirs)
    result[0:1, :] = total
    result[1:2, :] = mean
    result[2:3, :] = spread
    result[3:8, :] = jnp.zeros((5, result.shape[1]), F32)


def k_add(mine, theirs, result):
    result[...] = mine[...] + theirs[...]


def shaped_rows(convolved, stats, params, at):
    unit_bn = (convolved[at, :] - stats[1:2, :]) * stats[2:3, :]
    return unit_bn, unit_bn * params[5:6, :] + params[6:7, :]


def k_conv_rear(
    mine, theirs, convolved, params, normed, conv_o, conv_t,
    stats, active_own, active_cross, part,
):
    rows, width = normed.shape
    channels = params.shape[1] // 2
    total, mean, spread = merged(mine, theirs)
    arrive(convolved)
    stats[0:1, :] = total
    stats[1:2, :] = mean
    stats[2:3, :] = lax.rsqrt(spread / total + EPSILON)
    stats[3:8, :] = jnp.zeros((5, stats.shape[1]), F32)

    def activate(at, first, carry):
        _, shaped = shaped_rows(convolved, stats, params, at)
        active = (shaped * sigmoid(shaped)).astype(BF)
        active_own[at, :] = active[:, :channels]
        active_cross[at, :] = active[:, channels:]
        return carry

    over_rows(rows, activate)
    arrive(conv_o, conv_t)
    own = active_own[...]
    other = active_cross[...]
    for index in range(width // TILE):
        at = columns(index)
        part[:, at] = (
            times_back(own, conv_o[at, 2 * channels :])
            + times_back(other, conv_t[at, 2 * channels :])
        ).astype(BF)


def k_ffn_two(
    mine, theirs, stream_in, small, up_o, up_t, down_o, down_t,
    stream, branch, active_cross, active_own, hidden, part,
):
    rows, width = stream_in.shape
    arrive(stream_in)

    def normalise(at, first, carry):
        values = stream_in[at, :] + pair_sum(mine, theirs, at)
        stream[at, :] = values
        unit_rows, _ = norm_unit(values)
        branch[at, :] = (unit_rows * small[4:5, :]).astype(BF)
        return carry

    over_rows(rows, normalise)
    ffn_up(branch, (up_o, up_t), hidden, active_own, active_cross)
    ffn_down(active_own, active_cross, (down_o, down_t), part)


def split_blocks(info, rows, source, own, sent):
    core, high = info[0], info[1]
    own[...] = source[pl.ds((2 * high + core) * rows, rows), :]
    sent[...] = source[pl.ds((2 * high + 1 - core) * rows, rows), :]


def k_ffn_two_back(
    info, mine, theirs, stream, small, block, across_block, arrived, hidden,
    up_o, up_t, down_o, down_t,
    out_own, out_sent, grad_four, gain_sum, branch, grad_cross, grad_own, part, out_rows, grads,
):
    rows, width = stream.shape
    arrive(block, across_block, arrived)
    place_rows(info, block, across_block, arrived, grads)
    arrive(stream)

    def pass_back(at, first, carry):
        values = stream[at, :] + 0.5 * pair_sum(mine, theirs, at)
        unit_rows, inverse = norm_unit(values)
        out_rows[at, :] = (unit_rows * small[5:6, :]).astype(BF)
        grad, fresh = norm_back(grads[at, :].astype(F32), unit_rows, inverse, small[5:6, :])
        grad_four[at, :] = grad
        branch[at, :] = (0.5 * grad).astype(BF)
        return carry + fresh

    gain_sum[...] = over_rows(rows, pass_back, jnp.zeros((1, width), F32))
    split_blocks(info, rows // 4, out_rows, out_own, out_sent)
    ffn_grad_hidden(branch, (down_o, down_t), hidden, grad_own, grad_cross)

    def store(at, values):
        part[:, at] = values.astype(BF)

    ffn_grad_input(grad_own, grad_cross, (up_o, up_t), store)


def k_conv_back_front(
    mine, theirs, stream, small, grad_in, convolved, stats, params, conv_o, conv_t,
    grad_out, gain_sum, branch, grad_shaped, sums,
):
    rows, width = stream.shape
    channels = params.shape[1] // 2
    arrive(stream)

    def pass_back(at, first, carry):
        unit_rows, inverse = norm_unit(stream[at, :])
        grad, fresh = norm_back(pair_sum(mine, theirs, at), unit_rows, inverse, small[4:5, :])
        grad = grad_in[at, :] + grad
        grad_out[at, :] = grad
        branch[at, :] = grad.astype(BF)
        return carry + fresh

    gain_sum[...] = over_rows(rows, pass_back, jnp.zeros((1, width), F32))
    branch_rows = branch[...]
    arrive(convolved)
    for shard, weight in enumerate((conv_o, conv_t)):
        arrive(weight)
        grad_shaped[:, columns(shard, channels)] = product(branch_rows, weight[:, 2 * channels :])

    def slope(at, first, carry):
        unit_bn, shaped = shaped_rows(convolved, stats, params, at)
        grad = grad_shaped[at, :] * silu_slope(shaped)
        grad_shaped[at, :] = grad
        return (
            carry[0] + jnp.sum(grad, axis=0, keepdims=True),
            carry[1] + jnp.sum(grad * unit_bn, axis=0, keepdims=True),
        )

    zero = jnp.zeros((1, 2 * channels), F32)
    shift_sum, scale_sum = over_rows(rows, slope, (zero, zero))
    sums[0:1, :] = shift_sum
    sums[1:2, :] = scale_sum
    sums[2:8, :] = jnp.zeros((6, 2 * channels), F32)


def k_conv_back_rear(
    info, sums_mine, sums_theirs, grad_shaped, convolved, stats, params, padded, value, gate, branch,
    conv_o, conv_t,
    small_sums, mixed_own, mixed_cross, part, grad_padded,
):
    length = info[2]
    rows, width = branch.shape
    channels = params.shape[1] // 2
    sums = sums_mine[0:2, :] + sums_theirs[0:2, :]
    small_sums[5:6, :] = sums[0:1, :]
    small_sums[6:7, :] = sums[1:2, :]
    small_sums[7:8, :] = jnp.zeros((1, 2 * channels), F32)
    edge = jnp.zeros((EDGE, 2 * channels), F32)
    grad_padded[:EDGE, :] = edge
    grad_padded[EDGE + rows :, :] = edge
    arrive(convolved)
    count, bn_inverse, scale_row = stats[0:1, :], stats[2:3, :], params[5:6, :]
    grad_centre = -bn_inverse * scale_row * sums[0:1, :]
    grad_spread = -bn_inverse * bn_inverse * scale_row * sums[1:2, :]

    def spread(at, first, carry):
        centred = convolved[at, :] - stats[1:2, :]
        keep = valid_col(first, STEP, 2 * channels, length)
        grad = grad_shaped[at, :] * scale_row * bn_inverse + keep * (
            grad_centre + grad_spread * centred
        ) * (1.0 / count)
        grad_padded[pl.ds(pl.multiple_of(EDGE + first, EDGE), STEP), :] = grad
        return carry

    over_rows(rows, spread)
    arrive(padded, gate, value)
    for tile in range(2 * channels // DH):
        at = columns(tile, DH)
        grad = grad_padded[EDGE : EDGE + rows, at]
        back = None
        for offset in range(KW):
            begin = EDGE + 2 - offset
            term = params[offset : offset + 1, at] * grad_padded[begin : begin + rows, at]
            back = term if back is None else back + term
            begin = EDGE - 2 + offset
            small_sums[offset : offset + 1, at] = jnp.sum(
                grad * padded[begin : begin + rows, at], axis=0, keepdims=True
            )
        back = back * valid_col(0, rows, DH, length)
        gate_rows = gate[:, at]
        first_grad = (back * gate_rows).astype(BF)
        second_grad = (back * value[:, at] * gate_rows * (1.0 - gate_rows)).astype(BF)
        inner = (tile * DH) % channels
        if tile * DH < channels:
            mixed_own[:, inner : inner + DH] = first_grad
            mixed_own[:, channels + inner : channels + inner + DH] = second_grad
        else:
            mixed_cross[:, inner : inner + DH] = first_grad
            mixed_cross[:, channels + inner : channels + inner + DH] = second_grad
    arrive(conv_o, conv_t)
    own = mixed_own[...]
    other = mixed_cross[...]
    for index in range(width // TILE):
        at = columns(index)
        part[:, at] = (
            times_back(own, conv_o[at, : 2 * channels])
            + times_back(other, conv_t[at, : 2 * channels])
        ).astype(BF)


def k_attn_back(
    mine, theirs, stream, small, grad_in, sums_in, qkv, weights, qkv_o, qkv_t, out_o, out_t,
    grad_out, gain_sum, branch, three_cross, three_own, small_sums, part, grad_context,
):
    rows, width = stream.shape
    arrive(stream)
    third = qkv_o.shape[1] // 3
    heads = third // DH

    def pass_back(at, first, carry):
        unit_rows, inverse = norm_unit(stream[at, :])
        grad, fresh = norm_back(pair_sum(mine, theirs, at), unit_rows, inverse, small[3:4, :])
        grad = grad_in[at, :] + grad
        grad_out[at, :] = grad
        branch[at, :] = grad.astype(BF)
        return carry + fresh

    gain_sum[...] = over_rows(rows, pass_back, jnp.zeros((1, width), F32))
    branch_rows = branch[...]
    for shard, weight in enumerate((out_o, out_t)):
        arrive(weight)
        grad_context[:, columns(shard, third)] = times_back(branch_rows, weight[...]).astype(BF)
    away = lax.broadcasted_iota(jnp.int32, (rows, rows), 1) - row_iota(0, rows, rows)
    relative = jnp.clip(away, -REACH, REACH).astype(F32) * (1.0 / REACH)
    scale = DH ** (-0.5)
    arrive(qkv, weights)
    lanes = small_sums.shape[1]
    lane = lax.broadcasted_iota(jnp.int32, (1, lanes), 1)
    slope_row = jnp.zeros((1, lanes), F32)
    for shard in range(2):
        base = 3 * third * shard
        for head in range(heads):
            place = shard * heads + head
            query = qkv[:, base + head * DH : base + (head + 1) * DH]
            key = qkv[:, base + third + head * DH : base + third + (head + 1) * DH]
            value = qkv[:, base + 2 * third + head * DH : base + 2 * third + (head + 1) * DH]
            grad_head = grad_context[:, place * DH : (place + 1) * DH]
            soft = weights[place]
            grad_soft = times_back(grad_head, value)
            grad_value = inner_rows(soft.astype(BF), grad_head)
            dots = jnp.sum(soft * grad_soft, axis=-1, keepdims=True)
            grad_scores = (soft * (grad_soft - dots)).astype(BF)
            tilted = jnp.sum(grad_scores.astype(F32) * relative, axis=0, keepdims=True)
            slope = jnp.broadcast_to(jnp.sum(tilted, axis=1, keepdims=True), (1, lanes))
            slope_row = jnp.where(lane == shard * (lanes // 2) + head, slope, slope_row)
            grads = (
                product(grad_scores, key) * scale,
                inner_rows(grad_scores, query) * scale,
                grad_value,
            )
            for index, grad in enumerate(grads):
                begin = index * third + head * DH
                if shard == 0:
                    three_own[:, begin : begin + DH] = grad.astype(BF)
                else:
                    three_cross[:, begin : begin + DH] = grad.astype(BF)
    small_sums[:7, :] = sums_in[:7, :]
    small_sums[7:8, :] = slope_row
    arrive(qkv_o, qkv_t)
    own = three_own[...]
    other = three_cross[...]
    for index in range(width // TILE):
        at = columns(index)
        part[:, at] = (times_back(own, qkv_o[at, :]) + times_back(other, qkv_t[at, :])).astype(BF)


def k_ffn_one_back(
    info, mine, theirs, stream, small, grad_in, hidden, up_o, up_t, down_o, down_t,
    grad_out, gain_sum, branch, grad_cross, grad_own, part_own, part_sent, whole,
):
    high = info[1]
    rows, width = stream.shape
    span = rows // 2
    arrive(stream)

    def pass_back(at, first, carry):
        unit_rows, inverse = norm_unit(stream[at, :])
        grad, fresh = norm_back(pair_sum(mine, theirs, at), unit_rows, inverse, small[2:3, :])
        grad = grad_in[at, :] + grad
        grad_out[at, :] = grad
        branch[at, :] = (0.5 * grad).astype(BF)
        return carry + fresh

    gain_sum[...] = over_rows(rows, pass_back, jnp.zeros((1, width), F32))
    ffn_grad_hidden(branch, (down_o, down_t), hidden, grad_own, grad_cross)

    def store(at, values):
        whole[:, at] = values

    ffn_grad_input(grad_own, grad_cross, (up_o, up_t), store)
    part_own[...] = whole[pl.ds(high * span, span), :]
    part_sent[...] = whole[pl.ds((1 - high) * span, span), :].astype(BF)


def k_last(
    info, starts, part_own, arrived, frames, small, grad_in,
    grad_own, grad_sent, sums, grads,
):
    core, high, length = info[0], info[1], info[2]
    span, width = part_own.shape
    arrive(frames)

    def pass_back(at, first, carry):
        begin = pl.multiple_of(high * span + first, STEP)
        mask = mask_col(starts, begin, STEP, length)
        unit_rows, inverse = norm_unit(
            masked_rows(frames[pl.ds(begin, STEP), :], mask, small[0:1, :])
        )
        grad_normed = part_own[at, :] + arrived[at, :].astype(F32)
        grad, fresh = norm_back(grad_normed, unit_rows, inverse, small[1:2, :])
        grad = grad_in[pl.ds(begin, STEP), :] + grad
        hit = jnp.broadcast_to(mask, grad.shape) > 0.5
        grads[at, :] = jnp.where(hit, 0.0, grad)
        masked_part = jnp.sum(jnp.where(hit, grad, 0.0), axis=0, keepdims=True)
        return carry[0] + masked_part, carry[1] + fresh

    zero = jnp.zeros((1, width), F32)
    mask_sum, gain_sum = over_rows(span, pass_back, (zero, zero))
    sums[0:1, :] = mask_sum
    sums[1:2, :] = gain_sum
    rows = span // 2
    grad_own[...] = grads[pl.ds(core * rows, rows), :]
    grad_sent[...] = grads[pl.ds((1 - core) * rows, rows), :]


def k_weights(pairs, bit, tiles, info, *refs):
    count = 1 + max(max(pair[place] for place in (0, 1, 2, 4)) for pair in pairs)
    inputs, kept, sent = refs[:count], refs[count], refs[count + 1 :]
    mine = (info[3] >> bit) & 1
    low = bit - tiles
    rows = kept.shape[1]
    cut = sent[0].shape[2]
    for index in range(kept.shape[0]):
        high_part, low_part = index >> low, index & ((1 << low) - 1)
        for side in range(2):
            tile = (high_part * 2 + (mine ^ side)) * (1 << low) + low_part
            at = pl.ds(pl.multiple_of(tile * rows, rows), rows)
            begin = 0
            for left, left_too, right, shift, right_too, shift_too, size in pairs:
                for piece in range(0, size, TILE):
                    grad = inner_rows(
                        inputs[left][:, at],
                        inputs[right][:, shift + piece : shift + piece + TILE],
                    ) + inner_rows(
                        inputs[left_too][:, at],
                        inputs[right_too][:, shift_too + piece : shift_too + piece + TILE],
                    )
                    place = begin + piece
                    if side == 0:
                        kept[index, :, place : place + TILE] = grad
                    else:
                        inside = place % cut
                        sent[place // cut][index, :, inside : inside + TILE] = grad.astype(BF)
                begin += size


def k_fold(bit, count, info, held, *refs):
    arrivals, kept, sent = refs[:count], refs[count], refs[count + 1 :]
    mine = (info[3] >> bit) & 1
    cut_in, cut_out = arrivals[0].shape[3], sent[0].shape[2]
    size = min(cut_in, cut_out)
    for index in range(held.shape[0]):
        for side in range(2):
            at = pl.ds(mine ^ side, 1)
            for begin in range(0, held.shape[3], size):
                spot = slice(begin, begin + size)
                inside = slice(begin % cut_in, begin % cut_in + size)
                total = held[index, at, :, spot][0]
                total = total + arrivals[begin // cut_in][index, at, :, inside][0].astype(F32)
                if side == 0:
                    kept[index, :, spot] = total
                else:
                    inside = slice(begin % cut_out, begin % cut_out + size)
                    sent[begin // cut_out][index, :, inside] = total.astype(BF)


def k_finish(turned, count, info, kept, *refs):
    arrivals, results = refs[:count], refs[count:]
    cut = arrivals[0].shape[1]
    begin = 0
    for result, turn in zip(results, turned):
        size = result.shape[0] if turn else result.size // result.shape[0]
        for piece in range(begin, begin + size, DH):
            spot = slice(piece, piece + DH)
            at = piece - begin
            inside = slice(piece % cut, piece % cut + DH)
            total = kept[:, spot] + arrivals[piece // cut][:, inside].astype(F32)
            if turn:
                result[at : at + DH, :] = total.T
            elif len(result.shape) == 3:
                result[:, at // result.shape[2], pl.ds(at % result.shape[2], DH)] = total
            else:
                result[:, at : at + DH] = total
        begin += size


def k_in_order(info, own, other, result):
    core = info[0]
    result[pl.ds(core, 1)] = own[...][None]
    result[pl.ds(1 - core, 1)] = other[...][None]


def k_gather(bit, info, held, arrived, result):
    mine = (info[3] >> bit) & 1
    result[:, pl.ds(mine, 1)] = held[...][:, None]
    result[:, pl.ds(1 - mine, 1)] = arrived[...][:, None]


def k_smalls(last, attn, conv, two, final, channel_sums, result):
    width = attn.shape[1]
    result[0:2, :width] = last[...]
    for place, entry in enumerate((attn, conv, two, final), 2):
        result[place : place + 1, :width] = 0.5 * entry[...]
    result[6:8, :width] = jnp.zeros((2, width), F32)
    result[:, width:] = channel_sums[...]


def k_smalls_cross(smalls, result):
    width = smalls.shape[1] - 2 * (smalls.shape[1] - result.shape[1])
    channels = result.shape[1] - width
    result[:, :width] = smalls[:, :width]
    result[:, width:] = smalls[:, width + channels :]


def k_gains(mine, theirs, channel_sums, result):
    width = mine.shape[1]
    result[:, :width] = mine[...] + theirs[...]
    result[:, width:] = channel_sums[...]


def k_smalls_add(smalls, arrived, result):
    size = result.shape[1]
    result[...] = smalls[:, :size] + arrived[...]


def run(kernel, results, arguments, scalars=1, scratch=(), late=(), leaving=(), cost=1):
    given, made = len(arguments), len(results)
    hbm_shapes = [(arguments[place].shape, arguments[place].dtype) for place in late]
    hbm_shapes += [results[place] for place in leaving]
    buffers = [pltpu.VMEM(shape, kind) for shape, kind in hbm_shapes]
    own = [pltpu.VMEM(shape, kind) for shape, kind in scratch]
    hbm = pl.BlockSpec(memory_space=pltpu.HBM)

    def body(*refs):
        ins, outs = list(refs[:given]), list(refs[given : given + made])
        rest = refs[given + made :]
        extra, held, semaphores = rest[: len(own)], rest[len(own) : -1], rest[-1]
        for index, place in enumerate(late):
            ins[place] = Late(ins[place], held[index], semaphores.at[index])
        for index, place in enumerate(leaving, len(late)):
            outs[place] = Leaving(outs[place], held[index], semaphores.at[index])
        kernel(*ins, *outs, *extra)
        arrive(*ins)
        for place in leaving:
            outs[place].finish()

    def plain(*refs):
        kernel(*refs)

    held_bytes = sum(
        functools.reduce(lambda a, b: a * b, shape) * jnp.dtype(kind).itemsize
        for shape, kind in [*scratch, *hbm_shapes]
    )
    specs = [SMEM_SPEC] * scalars + [VMEM_SPEC] * (given - scalars)
    out_specs = [VMEM_SPEC] * made
    for place in late:
        specs[place] = hbm
    for place in leaving:
        out_specs[place] = hbm
    many = len(hbm_shapes)
    return pl.pallas_call(
        body if many else plain,
        out_shape=[
            pltpu.HBM(shape, kind) if place in leaving else pltpu.VMEM(shape, kind)
            for place, (shape, kind) in enumerate(results)
        ],
        in_specs=specs,
        out_specs=out_specs,
        scratch_shapes=own + buffers + ([pltpu.SemaphoreType.DMA((many,))] if many else []),
        compiler_params=pltpu.CompilerParams(vmem_limit_bytes=held_bytes + 8 * MIB),
        cost_estimate=pl.CostEstimate(flops=cost, bytes_accessed=cost, transcendentals=0),
    )(*(
        entry if place < scalars else pltpu.with_memory_space_constraint(
            entry, pltpu.HBM if place in late else pltpu.VMEM
        )
        for place, entry in enumerate(arguments)
    ))


def swap(value, axis, bit):
    size = lax.axis_size(axis)
    return lax.ppermute(value, axis, [(place, place ^ bit) for place in range(size)])


def across(value):
    return swap(value, "tensor", 2)


def beside(value):
    return swap(value, "tensor", 1)


def bit_of(axis, bit):
    return (lax.axis_index(axis) & bit) != 0


def tie(*values):
    return lax.optimization_barrier(values)


class RowSum:
    def __init__(self, info, inputs, pairs, width, first_bits, cuts=1, cost=1):
        size = lax.axis_size("dp")
        levels = size.bit_length() - 1
        tiles = max(levels - 3, 0)
        order = [tiles + bit for bit in first_bits]
        self.order = order + [bit for bit in range(levels - 1, -1, -1) if bit not in order]
        self.left = list(range(levels - 1, -1, -1))
        self.total = sum(pair[-1] for pair in pairs)
        self.block = width // size
        self.info = info
        count = size >> tiles
        shape = (count // 2, width // count)
        self.kept, *self.sent = run(
            functools.partial(k_weights, pairs, self.order[0], tiles),
            [((*shape, self.total), F32)] + [((*shape, self.total // cuts), BF)] * cuts,
            [info] + inputs,
            cost=cost,
        )
        self.begin()

    def begin(self):
        self.bit = self.order.pop(0)
        self.left.remove(self.bit)
        self.arrived = []

    def send(self, chain=None):
        piece = self.sent.pop(0)
        if chain is not None:
            (piece,) = chain.after(piece)
        self.arrived.append(swap(piece, "dp", 1 << self.bit))

    def here(self, chain):
        (self.arrived[-1],) = chain.after(self.arrived[-1])

    def fold(self, chain, cuts=1):
        bit = self.order[0]
        place = self.left.index(bit)
        inner = self.block << (len(self.left) - 1 - place)
        outer = 1 << place
        kept, *arrived = chain.after(self.kept, *self.arrived)
        self.kept, *self.sent = run(
            functools.partial(k_fold, bit, len(arrived)),
            [((outer, inner, self.total), F32)] + [((outer, inner, self.total // cuts), BF)] * cuts,
            [self.info, kept.reshape(outer, 2, inner, self.total)]
            + [entry.reshape(outer, 2, inner, -1) for entry in arrived],
        )
        self.kept, chain.last = tie(self.kept, chain.last)
        self.begin()

    def step(self, chain):
        self.fold(chain)
        self.send()

    def finish(self, chain, *results):
        while self.order:
            self.step(chain)
        shape = (self.block, self.total)
        kept, *arrived = chain.after(
            self.kept.reshape(shape), *(entry.reshape(self.block, -1) for entry in self.arrived)
        )
        sums = run(
            functools.partial(k_finish, tuple(turn for _, turn in results), len(arrived)),
            [(size, F32) for size, _ in results],
            [self.info, kept, *arrived],
        )
        *sums, chain.last = tie(*sums, chain.last)
        return sums


class Chain:
    def __init__(self, last):
        self.last = last

    def after(self, *values):
        *values, self.last = tie(*values, self.last)
        return values


class Gather:
    def __init__(self, info, block):
        self.info, self.held = info, block.reshape(1, *block.shape)
        self.bit = lax.axis_size("dp") // 2
        self.shape = (lax.axis_size("dp") * block.shape[0], block.shape[1])

    def send(self):
        self.arrived = swap(self.held, "dp", self.bit)

    def take(self):
        outer, rows, width = self.held.shape
        (held,) = run(
            functools.partial(k_gather, self.bit.bit_length() - 1),
            [((outer, 2, rows, width), self.held.dtype)],
            [self.info, self.held, self.arrived],
        )
        self.held = held.reshape(outer * 2, rows, width)
        self.bit //= 2

    def whole(self):
        while self.bit:
            self.send()
            self.take()
        return self.held.reshape(self.shape)


def sum_pair(value, axis, merge=None):
    bit, size = 1, lax.axis_size(axis)
    while bit * 2 < size:
        (value,) = run(
            merge or k_add, [(value.shape, F32)], [value, swap(value, axis, bit)], scalars=0
        )
        bit *= 2
    return value, swap(value, axis, bit)


def per_device(
    frames,
    lengths,
    span_starts,
    mask_vector,
    ffn1_gain,
    ffn1_up,
    ffn1_down,
    attn_gain,
    query_weight,
    key_weight,
    value_weight,
    output_weight,
    rel_slope,
    conv_gain,
    conv_up,
    conv_depth,
    bn_scale,
    bn_shift,
    conv_down,
    ffn2_gain,
    ffn2_up,
    ffn2_down,
    final_gain,
    cotangent,
):
    batches, row_count, width = frames.shape
    length = row_count * lax.axis_size("tensor")
    span = 2 * row_count
    channels = conv_depth.shape[1]
    hidden_width = ffn1_up.shape[1]
    heads = rel_slope.shape[0]
    third = query_weight.shape[1]
    core = lax.axis_index("tensor") & 1
    high = (lax.axis_index("tensor") >> 1) & 1
    group = lax.axis_index("dp")
    on_first = core == 0
    own_length = jnp.where(on_first, lengths[0], lengths[1])
    info = jnp.stack([core, high, own_length, group]).astype(jnp.int32)
    starts = jnp.where(on_first, span_starts[0:1], span_starts[1:2])

    def gather_rows(block):
        across_block = across(block)
        (sent,) = run(k_pick, [(block.shape, BF)], [info, block, across_block])
        return [block, across_block, beside(sent)]

    conv_block = jnp.concatenate(
        [conv_up.reshape(conv_up.shape[0], 2 * channels), conv_down.T], axis=1
    )
    conv_weights = Gather(info, conv_block)
    conv_weights.send()
    frame_parts = gather_rows(frames)
    part = mask_vector.shape[0]
    place = (group * lax.axis_size("tensor") + lax.axis_index("tensor")) * part
    vectors = jnp.stack(
        [mask_vector.astype(F32), ffn1_gain, attn_gain, conv_gain, ffn2_gain, final_gain,
         jnp.zeros_like(ffn1_gain), jnp.zeros_like(ffn1_gain)]
    )
    small = lax.dynamic_update_slice(jnp.zeros((8, width), F32), vectors, (0, place))
    hops = [("tensor", 1), ("dp", 2), ("dp", 1), ("tensor", 2)]
    bit = 4
    while bit < lax.axis_size("dp"):
        hops.append(("dp", bit))
        bit *= 2
    for step, (axis, bit) in enumerate(hops):
        if step == 3:
            conv_weights.arrived, small = tie(conv_weights.arrived, small)
            conv_weights.take()
            if conv_weights.bit:
                conv_weights.send()
        if bit < lax.axis_size(axis):
            (small,) = run(
                k_add, [(small.shape, F32)], [small, swap(small, axis, bit)], scalars=0
            )
    if conv_weights.bit:
        conv_weights.arrived, small = tie(conv_weights.arrived, small)
        conv_weights.take()
    conv_weights.held, small = tie(conv_weights.held, small)
    if conv_weights.bit:
        conv_weights.send()
    up_one, down_one = beside(ffn1_up), beside(ffn1_down)

    wide = (length, width)
    ffn_outs = [
        (wide, BF),
        ((length, hidden_width), BF),
        ((length, hidden_width), BF),
        ((length, 2 * hidden_width), F32),
        (wide, BF),
    ]
    whole, norm_one, cross_one, active_one, hidden_one, partial = run(
        k_ffn_one,
        [(wide, BF)] + ffn_outs,
        [info, starts, *frame_parts, small, ffn1_up, up_one, ffn1_down, down_one],
        scratch=[(wide, BF)], late=(6, 7, 8, 9),
    )
    query_weight, key_weight, value_weight, output_weight, rel_slope, active_one = tie(
        query_weight, key_weight, value_weight, output_weight, rel_slope, active_one
    )
    own_qkv = jnp.concatenate([query_weight, key_weight, value_weight], axis=1)
    other_qkv, other_out = beside(own_qkv), beside(output_weight)
    slope_row = jnp.pad(rel_slope[None], ((0, 0), (0, channels - heads)))
    own_params = jnp.concatenate([conv_depth, bn_scale[None], bn_shift[None], slope_row])
    other_params = beside(own_params)
    params = jnp.concatenate([own_params, other_params], axis=1)
    slopes = jnp.concatenate([rel_slope, other_params[KW + 2, :heads]])
    stream_one, norm_attn, context_cross, context_own, qkv, weights, partial = run(
        k_attn_wrapped,
        [
            (wide, F32),
            (wide, BF),
            ((length, third), BF),
            ((length, third), BF),
            ((length, 6 * third), BF),
            ((2 * heads, length, length), F32),
            (wide, BF),
        ],
        [info, slopes, starts, partial, across(partial), whole, small, own_qkv, other_qkv,
         output_weight, other_out],
        scalars=2, late=(7, 8, 9, 10),
    )
    conv_weights.arrived, norm_one, cross_one, context_own = tie(
        conv_weights.arrived, norm_one, cross_one, context_own
    )
    conv_weights.take()
    own_conv = conv_weights.whole()
    other_conv = beside(own_conv)
    norm_one_too, cross_one_too = beside(norm_one), beside(cross_one)
    norm_one_too, cross_one_too, params = tie(norm_one_too, cross_one_too, params)
    both_channels = (length, 2 * channels)
    stat_shape = ((8, 2 * channels), F32)
    stream_two, norm_conv, value, gate, padded, convolved, stats = run(
        k_conv_front,
        [
            (wide, F32),
            (wide, BF),
            (both_channels, F32),
            (both_channels, F32),
            ((length + 2 * EDGE, 2 * channels), F32),
            (both_channels, F32),
            stat_shape,
        ],
        [info, partial, across(partial), stream_one, small, params, own_conv, other_conv],
        late=(6, 7),
    )
    norm_attn, context_cross, cotangent, ffn2_up, ffn2_down, value = tie(
        norm_attn, context_cross, cotangent, ffn2_up, ffn2_down, value
    )
    stats, stats_too = sum_pair(stats, "dp", k_merge)
    grad_across = across(cotangent)
    up_two, down_two = beside(ffn2_up), beside(ffn2_down)
    norm_attn_too, context_cross_too = beside(norm_attn), beside(context_cross)
    norm_attn_too, context_cross_too, params, grad_across = tie(
        norm_attn_too, context_cross_too, params, grad_across
    )
    stats, active_conv, cross_conv, partial = run(
        k_conv_rear,
        [stat_shape, ((length, channels), BF), ((length, channels), BF), (wide, BF)],
        [stats, stats_too, convolved, params, norm_conv, own_conv, other_conv],
        scalars=0, late=(5, 6),
    )
    grad_across, active_conv = tie(grad_across, active_conv)
    (sent,) = run(k_pick, [(cotangent.shape, BF)], [info, cotangent, grad_across])
    grad_parts = [cotangent, grad_across, beside(sent)]
    grad_parts[2], small = tie(grad_parts[2], small)
    stream_three, norm_two, cross_two, active_two, hidden_two, partial = run(
        k_ffn_two,
        [(wide, F32)] + ffn_outs,
        [partial, across(partial), stream_two, small, ffn2_up, up_two, ffn2_down, down_two],
        scalars=0, late=(4, 5, 6, 7),
    )
    norm_two, cross_two, norm_conv, cross_conv, active_two = tie(
        norm_two, cross_two, norm_conv, cross_conv, active_two
    )
    norm_two_too, cross_two_too = beside(norm_two), beside(cross_two)
    norm_conv_too, cross_conv_too = beside(norm_conv), beside(cross_conv)
    norm_two_too, cross_two_too, norm_conv_too, cross_conv_too, small = tie(
        norm_two_too, cross_two_too, norm_conv_too, cross_conv_too, small
    )

    row_shape = ((1, width), F32)
    block_shape = (row_count, width)
    out_own, out_sent, grad_four, sum_final, back_two, hid_cross_two, hid_two, partial = run(
        k_ffn_two_back,
        [
            (block_shape, BF),
            (block_shape, BF),
            (wide, F32),
            row_shape,
            (wide, BF),
            ((length, hidden_width), BF),
            ((length, hidden_width), BF),
            (wide, BF),
        ],
        [info, partial, across(partial), stream_three, small, *grad_parts, hidden_two,
         ffn2_up, up_two, ffn2_down, down_two],
        scratch=[(wide, BF), (wide, BF)], late=(9, 10, 11, 12),
    )
    back_two_too, hid_cross_two_too = beside(back_two), beside(hid_cross_two)
    ffn_pair = ((0, 1, 2, 0, 3, 0, hidden_width),)
    two_up = RowSum(
        info, [norm_two, norm_two_too, hid_two, hid_cross_two_too], ffn_pair, width, (0, 1, 2)
    )
    two_down = RowSum(
        info, [back_two, back_two_too, active_two, cross_two_too], ffn_pair, width, (1, 2, 0)
    )
    grad_four, two_up.sent[0], two_down.sent[0] = tie(
        grad_four, two_up.sent[0], two_down.sent[0]
    )
    grad_three, sum_two, back_conv, grad_shaped, sums = run(
        k_conv_back_front,
        [(wide, F32), row_shape, (wide, BF), (both_channels, F32), stat_shape],
        [partial, across(partial), stream_three, small, grad_four, convolved, stats, params,
         own_conv, other_conv],
        scalars=0, late=(8, 9),
    )
    out_sent, sum_two, back_conv = tie(out_sent, sum_two, back_conv)
    out_other, back_conv_too = beside(out_sent), beside(back_conv)
    sums, sums_too = sum_pair(sums, "dp")
    sums_too, out_other, back_conv_too = tie(sums_too, out_other, back_conv_too)
    chain = Chain(sums_too)
    two_up.send(chain)
    two_down.send(chain)
    sums_too = chain.last
    small_sums, mixed_own, mixed_cross, partial = run(
        k_conv_back_rear,
        [
            stat_shape,
            ((length, 2 * channels), BF),
            ((length, 2 * channels), BF),
            (wide, BF),
        ],
        [info, sums, sums_too, grad_shaped, convolved, stats, params, padded, value, gate,
         back_conv, own_conv, other_conv],
        scratch=[((length + 2 * EDGE, 2 * channels), F32)], late=(11, 12),
    )
    mixed_cross_too = beside(mixed_cross)
    mixed_cross_too, grad_three = tie(mixed_cross_too, grad_three)
    grad_two, sum_conv, back_attn, three_cross, three_own, small_sums, partial = run(
        k_attn_back,
        [
            (wide, F32),
            row_shape,
            (wide, BF),
            ((length, 3 * third), BF),
            ((length, 3 * third), BF),
            stat_shape,
            (wide, BF),
        ],
        [partial, across(partial), stream_two, small, grad_three, small_sums, qkv, weights,
         own_qkv, other_qkv, output_weight, other_out],
        scalars=0,
        scratch=[((length, 2 * third), BF)], late=(8, 9, 10, 11),
    )
    back_attn_too, three_cross_too = beside(back_attn), beside(three_cross)
    chain = Chain(small_sums)
    for entry in (two_up, two_down):
        entry.step(chain)
    back_attn, three_own = chain.after(back_attn, three_own)
    small_sums = chain.last
    middle = RowSum(
        info,
        [norm_conv, norm_conv_too, mixed_own, mixed_cross_too,
         back_conv, back_conv_too, active_conv, cross_conv_too,
         norm_attn, norm_attn_too, three_own, three_cross_too,
         back_attn, back_attn_too, context_own, context_cross_too],
        (
            (0, 1, 2, 0, 3, 0, 2 * channels),
            (4, 5, 6, 0, 7, 0, channels),
            (8, 9, 10, 0, 11, 0, 3 * third),
            (12, 13, 14, 0, 15, 0, third),
        ),
        width, (0, 1, 2),
    )
    middle.send()
    middle.kept, grad_two = tie(middle.kept, grad_two)
    grad_one, sum_attn, back_one, hid_cross_one, hid_one, last_own, last_sent = run(
        k_ffn_one_back,
        [
            (wide, F32),
            row_shape,
            (wide, BF),
            ((length, hidden_width), BF),
            ((length, hidden_width), BF),
            ((span, width), F32),
            ((span, width), BF),
        ],
        [info, partial, across(partial), stream_one, small, grad_two, hidden_one,
         ffn1_up, up_one, ffn1_down, down_one],
        scratch=[(wide, F32)], late=(7, 8, 9, 10),
    )
    back_one_too, hid_cross_one_too = beside(back_one), beside(hid_cross_one)
    one_up = RowSum(
        info, [norm_one, norm_one_too, hid_one, hid_cross_one_too], ffn_pair, width, (0, 1, 2),
        cost=COST,
    )
    one_down = RowSum(
        info, [back_one, back_one_too, active_one, cross_one_too], ffn_pair, width, (0, 1, 2),
        cost=COST,
    )
    chain = Chain(sum_attn)
    for entry in (one_up, one_down):
        entry.send(chain)
        entry.kept, chain.last = tie(entry.kept, chain.last)
    for entry in (middle, two_up, two_down):
        entry.step(chain)
    (starts,) = chain.after(starts)
    sum_attn = chain.last
    frames_own, frames_sent, last_sums = run(
        k_last,
        [(block_shape, F32), (block_shape, F32), ((2, width), F32)],
        [info, starts, last_own, across(last_sent), whole, small, grad_one],
        scratch=[((span, width), F32)],
    )
    frames_other = beside(frames_sent)
    (smalls,) = run(
        k_smalls, [((8, width + 2 * channels), F32)],
        [last_sums, sum_attn, sum_conv, sum_two, sum_final, small_sums], scalars=0,
    )
    (smalls_sent,) = run(k_smalls_cross, [((8, width + channels), F32)], [smalls], scalars=0)
    (smalls,) = run(
        k_smalls_add, [((8, width + channels), F32)], [smalls, beside(smalls_sent)], scalars=0
    )
    gains, gains_too = smalls[:, :width], across(smalls[:, :width])
    block = width // lax.axis_size("dp")
    (gains,) = run(
        k_gains, [(smalls.shape, F32)], [gains, gains_too, smalls[:, width:]], scalars=0
    )
    chain = Chain(frames_own)
    one_up.step(chain)
    (two_up,) = two_up.finish(chain, ((block, hidden_width), False))
    middle.step(chain)
    one_up.step(chain)
    one_down.step(chain)
    (gains,) = chain.after(gains)
    gains_too = swap(gains, "dp", 1)
    conv_up_grad, conv_down_grad, query_grad, key_grad, value_grad, output_grad = middle.finish(
        chain,
        (conv_up.shape, False), ((channels, block), True),
        *[((block, third), False)] * 3, ((third, block), True),
    )
    (two_down,) = two_down.finish(chain, ((hidden_width, block), True))
    one_down.step(chain)
    (one_up,) = one_up.finish(chain, ((block, hidden_width), False))
    gains, gains_too = chain.after(gains, gains_too)
    (gains,) = run(k_add, [(gains.shape, F32)], [gains, gains_too], scalars=0)
    bit = 2
    while bit < lax.axis_size("dp"):
        (gains,) = run(
            k_add, [(gains.shape, F32)], [gains, swap(gains, "dp", bit)], scalars=0
        )
        bit *= 2
    (one_down,) = one_down.finish(chain, ((hidden_width, block), True))
    frames_own = chain.last

    channel_sums = gains[:, width:]
    scale_grad = channel_sums[KW + 1] * (1.0 / lax.axis_size("dp"))
    shift_grad = channel_sums[KW] * (1.0 / lax.axis_size("dp"))
    gains = lax.dynamic_slice_in_dim(gains, place, part, axis=1)

    def in_order(own, other):
        return run(k_in_order, [((2, *own.shape), own.dtype)], [info, own, other])[0]

    return (
        in_order(out_own, out_other),
        in_order(frames_own, frames_other),
        gains[0],
        gains[1],
        one_up,
        one_down,
        gains[2],
        query_grad,
        key_grad,
        value_grad,
        output_grad,
        channel_sums[KW + 2, :heads],
        gains[3],
        conv_up_grad,
        channel_sums[:KW],
        scale_grad,
        shift_grad,
        conv_down_grad,
        gains[4],
        two_up,
        two_down,
        gains[5],
    )


def k_attn_wrapped(info, slopes, starts, *refs):
    k_attn(info, starts, slopes, *refs)


def solution(mesh):
    every, split, by_column = P(("dp", "tensor")), P("tensor"), P(None, "tensor")
    rows_by = P("dp", "tensor", None)
    return jax.shard_map(
        per_device,
        mesh=mesh,
        in_specs=(
            rows_by,
            P("dp"),
            P("dp", None),
            every,
            every,
            by_column,
            P("tensor", None),
            every,
            by_column,
            by_column,
            by_column,
            P("tensor", None),
            split,
            every,
            P("dp", None, "tensor"),
            by_column,
            split,
            split,
            P("tensor", "dp"),
            every,
            by_column,
            P("tensor", None),
            every,
            rows_by,
        ),
        out_specs=(
            rows_by,
            rows_by,
            every,
            every,
            P("dp", "tensor"),
            P("tensor", "dp"),
            every,
            P("dp", "tensor"),
            P("dp", "tensor"),
            P("dp", "tensor"),
            P("tensor", "dp"),
            split,
            every,
            P("dp", None, "tensor"),
            by_column,
            split,
            split,
            P("tensor", "dp"),
            every,
            P("dp", "tensor"),
            P("tensor", "dp"),
            every,
        ),
        check_vma=False,
    )
```

```python
import functools

import jax
import jax.numpy as jnp
from jax import lax
from jax.experimental import pallas as pl
from jax.experimental.pallas import tpu as pltpu
from jax.sharding import PartitionSpec as P

DH = 128
KW = 5
SPAN = 10
REACH = 128
EPSILON = 1e-05
MASKED_SCORE = -1000000000.0
BF = jnp.bfloat16
F32 = jnp.float32
STEP = 32
TILE = 256
EDGE = 8
MIB = 1024 * 1024
COST = 30_000_000

VMEM_SPEC = pl.BlockSpec(memory_space=pltpu.VMEM)
SMEM_SPEC = pl.BlockSpec(memory_space=pltpu.SMEM)


def product(left, right):
    return jnp.dot(left, right, preferred_element_type=F32)


def inner_rows(left, right):
    return lax.dot_general(left, right, (((0,), (0,)), ((), ())), preferred_element_type=F32)


def times_back(left, right):
    return lax.dot_general(left, right, (((1,), (1,)), ((), ())), preferred_element_type=F32)


def sigmoid(values):
    return 0.5 * jnp.tanh(0.5 * values) + 0.5


def norm_unit(values):
    centre = jnp.mean(values, axis=-1, keepdims=True)
    centred = values - centre
    inverse = lax.rsqrt(jnp.mean(centred * centred, axis=-1, keepdims=True) + EPSILON)
    return centred * inverse, inverse


def norm_back(grad_out, unit_rows, inverse, norm_gain):
    grad_unit = grad_out * norm_gain
    first_mean = jnp.mean(grad_unit, axis=-1, keepdims=True)
    second_mean = jnp.mean(grad_unit * unit_rows, axis=-1, keepdims=True)
    return (
        inverse * (grad_unit - first_mean - unit_rows * second_mean),
        jnp.sum(grad_out * unit_rows, axis=0, keepdims=True),
    )


def silu_slope(values):
    gate_value = sigmoid(values)
    return gate_value * (1.0 + values * (1.0 - gate_value))


def over_rows(count, body, init=0, step=STEP):
    def one(index, carry):
        return body(pl.ds(pl.multiple_of(index * step, step), step), index * step, carry)

    return lax.fori_loop(0, count // step, one, init)


def row_iota(first, rows, columns):
    return first + lax.broadcasted_iota(jnp.int32, (rows, columns), 0)


def mask_col(starts_ref, first, rows, length):
    starts = starts_ref[...]
    at = row_iota(first, rows, starts.shape[1])
    hit = (starts <= at) & (at < starts + SPAN) & (at < length)
    return jnp.max(jnp.where(hit, 1.0, 0.0), axis=1, keepdims=True)


def valid_col(first, rows, columns, length):
    return jnp.where(row_iota(first, rows, columns) < length, 1.0, 0.0)


def masked_rows(frame_rows, mask, mask_row):
    return jnp.where(
        jnp.broadcast_to(mask, frame_rows.shape) > 0.5, mask_row, frame_rows.astype(F32)
    )


def pair_sum(mine, theirs, rows):
    return mine[rows, :].astype(F32) + theirs[rows, :].astype(F32)


class Late:
    def __init__(self, source, held, semaphore):
        self.copy = pltpu.make_async_copy(source, held, semaphore)
        self.copy.start()
        self.held, self.shape, self.dtype, self.waited = held, held.shape, held.dtype, False

    def arrive(self):
        if not self.waited:
            self.copy.wait()
            self.waited = True

    def __getitem__(self, index):
        assert self.waited
        return self.held[index]


class Leaving:
    def __init__(self, target, held, semaphore):
        self.copy = pltpu.make_async_copy(held, target, semaphore)
        self.held, self.shape, self.dtype, self.started = held, held.shape, held.dtype, False

    def leave(self):
        if not self.started:
            self.copy.start()
            self.started = True

    def finish(self):
        self.leave()
        self.copy.wait()

    def __getitem__(self, index):
        return self.held[index]

    def __setitem__(self, index, value):
        assert not self.started
        self.held[index] = value


def arrive(*refs):
    for ref in refs:
        if isinstance(ref, Late):
            ref.arrive()


def leave(*refs):
    for ref in refs:
        if isinstance(ref, Leaving):
            ref.leave()


def columns(index, size=TILE):
    return slice(index * size, (index + 1) * size)


def ffn_up(branch, ups, hidden, active_own, active_cross):
    normed = branch[...]
    for shard, weight in enumerate(ups):
        arrive(weight)
        tiles = weight.shape[1] // TILE
        for index in range(tiles):
            at = columns(index)
            values = product(normed, weight[:, at])
            hidden[:, columns(index + shard * tiles)] = values
            (active_own, active_cross)[shard][:, at] = (values * sigmoid(values)).astype(BF)


def ffn_down(active_own, active_cross, downs, part):
    width = downs[0].shape[1]
    own, cross = active_own[...], active_cross[...]
    arrive(*downs)
    for index in range(width // TILE):
        at = columns(index)
        part[:, at] = (product(own, downs[0][:, at]) + product(cross, downs[1][:, at])).astype(BF)


def ffn_grad_hidden(branch, downs, hidden, grad_own, grad_cross):
    grad_branch = branch[...]
    for shard, weight in enumerate(downs):
        arrive(weight)
        tiles = weight.shape[0] // TILE
        for index in range(tiles):
            at = columns(index)
            slope = silu_slope(hidden[:, columns(index + shard * tiles)])
            grad = (times_back(grad_branch, weight[at, :]) * slope).astype(BF)
            (grad_own, grad_cross)[shard][:, at] = grad


def ffn_grad_input(grad_own, grad_cross, ups, store):
    own, cross = grad_own[...], grad_cross[...]
    arrive(*ups)
    for index in range(ups[0].shape[0] // TILE):
        at = columns(index)
        store(at, times_back(own, ups[0][at, :]) + times_back(cross, ups[1][at, :]))


def k_pick(info, block, across_block, sent):
    core = info[0]
    sent[0] = block[pl.ds(1 - core, 1)][0]
    sent[1] = across_block[pl.ds(1 - core, 1)][0]


def place_rows(info, block, across_block, arrived, whole):
    core, high = info[0], info[1]
    rows = block.shape[1]
    places = (
        (2 * high + core, block[pl.ds(core, 1)][0]),
        (2 * (1 - high) + core, across_block[pl.ds(core, 1)][0]),
        (2 * high + 1 - core, arrived[0]),
        (2 * (1 - high) + 1 - core, arrived[1]),
    )
    for place, value in places:
        whole[pl.ds(pl.multiple_of(place * rows, rows), rows), :] = value


def k_ffn_one(
    info, starts, block, across_block, arrived, small, up_o, up_t, down_o, down_t,
    frames, branch, active_cross, active_own, hidden, part, whole,
):
    length = info[2]
    rows, width = whole.shape
    place_rows(info, block, across_block, arrived, whole)
    frames[...] = whole[...]

    def normalise(at, first, carry):
        mask = mask_col(starts, first, STEP, length)
        unit_rows, _ = norm_unit(masked_rows(whole[at, :], mask, small[0:1, :]))
        branch[at, :] = (unit_rows * small[1:2, :]).astype(BF)
        return carry

    over_rows(rows, normalise)
    ffn_up(branch, (up_o, up_t), hidden, active_own, active_cross)
    ffn_down(active_own, active_cross, (down_o, down_t), part)


def k_attn(
    info, starts, slopes, mine, theirs, frames, small, qkv_o, qkv_t, out_o, out_t,
    stream, branch, context_cross, context_own, qkv, weights, part,
):
    length = info[2]
    rows, width = frames.shape
    arrive(frames)

    def normalise(at, first, carry):
        mask = mask_col(starts, first, STEP, length)
        inputs = masked_rows(frames[at, :], mask, small[0:1, :])
        values = inputs + 0.5 * pair_sum(mine, theirs, at)
        stream[at, :] = values
        unit_rows, _ = norm_unit(values)
        branch[at, :] = (unit_rows * small[2:3, :]).astype(BF)
        return carry

    over_rows(rows, normalise)
    normed = branch[...]
    third = qkv_o.shape[1] // 3
    for shard, weight in enumerate((qkv_o, qkv_t)):
        arrive(weight)
        for index in range(3):
            at = columns(index, third)
            qkv[:, columns(3 * shard + index, third)] = product(normed, weight[:, at]).astype(BF)
    heads = third // DH
    span = rows // 2
    for shard in range(2):
        base = 3 * third * shard
        for head in range(heads):
            place = shard * heads + head
            key = qkv[:, base + third + head * DH : base + third + (head + 1) * DH]
            value = qkv[:, base + 2 * third + head * DH : base + 2 * third + (head + 1) * DH]
            for part_index in range(2):
                at = columns(part_index, span)
                query = qkv[at, base + head * DH : base + (head + 1) * DH]
                scores = times_back(query, key) * DH ** (-0.5)
                key_place = lax.broadcasted_iota(jnp.int32, (span, rows), 1)
                away = key_place - row_iota(part_index * span, span, rows)
                relative = jnp.clip(away, -REACH, REACH).astype(F32) * (1.0 / REACH)
                scores = scores + slopes[place] * relative
                scores = jnp.where(key_place < length, scores, MASKED_SCORE)
                raised = jnp.exp(scores - jnp.max(scores, axis=-1, keepdims=True))
                soft = raised * (1.0 / jnp.sum(raised, axis=-1, keepdims=True))
                weights[place, at, :] = soft
                context = product(soft.astype(BF), value).astype(BF)
                if shard == 0:
                    context_own[at, columns(head, DH)] = context
                else:
                    context_cross[at, columns(head, DH)] = context
    arrive(out_o, out_t)
    own = context_own[...]
    other = context_cross[...]
    for index in range(width // TILE):
        at = columns(index)
        part[:, at] = (product(own, out_o[:, at]) + product(other, out_t[:, at])).astype(BF)


def k_conv_front(
    info, mine, theirs, stream_in, small, params, conv_o, conv_t,
    stream, normed, value, gate, padded, convolved, stats,
):
    length = info[2]
    rows, width = stream_in.shape
    channels = params.shape[1] // 2
    arrive(stream_in)

    def normalise(at, first, carry):
        values = stream_in[at, :] + pair_sum(mine, theirs, at)
        stream[at, :] = values
        unit_rows, _ = norm_unit(values)
        normed[at, :] = (unit_rows * small[3:4, :]).astype(BF)
        return carry

    over_rows(rows, normalise)
    normed_rows = normed[...]
    edge = jnp.zeros((EDGE, 2 * channels), F32)
    padded[:EDGE, :] = edge
    padded[EDGE + rows :, :] = edge
    for shard, weight in enumerate((conv_o, conv_t)):
        arrive(weight)
        at = columns(shard, channels)
        value_rows = product(normed_rows, weight[:, :channels])
        value[:, at] = value_rows
        gate_rows = sigmoid(product(normed_rows, weight[:, channels : 2 * channels]))
        gate[:, at] = gate_rows
        padded[EDGE : EDGE + rows, at] = (
            value_rows * gate_rows * valid_col(0, rows, channels, length)
        )
    count = length.astype(F32)
    for tile in range(2 * channels // DH):
        at = columns(tile, DH)
        total = params[0:1, at] * padded[EDGE - 2 : EDGE - 2 + rows, at]
        for offset in range(1, KW):
            begin = EDGE - 2 + offset
            total = total + params[offset : offset + 1, at] * padded[begin : begin + rows, at]
        convolved[:, at] = total
        keep = valid_col(0, rows, DH, length)
        mean = jnp.sum(total * keep, axis=0, keepdims=True) / count
        centred = (total - mean) * keep
        stats[0:1, at] = jnp.full((1, DH), count, F32)
        stats[1:2, at] = mean
        stats[2:3, at] = jnp.sum(centred * centred, axis=0, keepdims=True)
        stats[3:8, at] = jnp.zeros((5, DH), F32)


def merged(mine, theirs):
    total = mine[0:1, :] + theirs[0:1, :]
    apart = mine[1:2, :] - theirs[1:2, :]
    mean = (mine[0:1, :] * mine[1:2, :] + theirs[0:1, :] * theirs[1:2, :]) / total
    share = mine[0:1, :] * theirs[0:1, :] / total
    spread = mine[2:3, :] + theirs[2:3, :] + apart * apart * share
    return total, mean, spread


def k_merge(mine, theirs, result):
    total, mean, spread = merged(mine, theirs)
    result[0:1, :] = total
    result[1:2, :] = mean
    result[2:3, :] = spread
    result[3:8, :] = jnp.zeros((5, result.shape[1]), F32)


def k_add(mine, theirs, result):
    result[...] = mine[...] + theirs[...]


def shaped_rows(convolved, stats, params, at):
    unit_bn = (convolved[at, :] - stats[1:2, :]) * stats[2:3, :]
    return unit_bn, unit_bn * params[5:6, :] + params[6:7, :]


def k_conv_rear(
    mine, theirs, convolved, params, normed, conv_o, conv_t,
    stats, active_own, active_cross, part,
):
    rows, width = normed.shape
    channels = params.shape[1] // 2
    total, mean, spread = merged(mine, theirs)
    arrive(convolved)
    stats[0:1, :] = total
    stats[1:2, :] = mean
    stats[2:3, :] = lax.rsqrt(spread / total + EPSILON)
    stats[3:8, :] = jnp.zeros((5, stats.shape[1]), F32)

    def activate(at, first, carry):
        _, shaped = shaped_rows(convolved, stats, params, at)
        active = (shaped * sigmoid(shaped)).astype(BF)
        active_own[at, :] = active[:, :channels]
        active_cross[at, :] = active[:, channels:]
        return carry

    over_rows(rows, activate)
    arrive(conv_o, conv_t)
    own = active_own[...]
    other = active_cross[...]
    for index in range(width // TILE):
        at = columns(index)
        part[:, at] = (
            times_back(own, conv_o[at, 2 * channels :])
            + times_back(other, conv_t[at, 2 * channels :])
        ).astype(BF)


def k_ffn_two(
    mine, theirs, stream_in, small, up_o, up_t, down_o, down_t,
    stream, branch, active_cross, active_own, hidden, part,
):
    rows, width = stream_in.shape
    arrive(stream_in)

    def normalise(at, first, carry):
        values = stream_in[at, :] + pair_sum(mine, theirs, at)
        stream[at, :] = values
        unit_rows, _ = norm_unit(values)
        branch[at, :] = (unit_rows * small[4:5, :]).astype(BF)
        return carry

    over_rows(rows, normalise)
    ffn_up(branch, (up_o, up_t), hidden, active_own, active_cross)
    ffn_down(active_own, active_cross, (down_o, down_t), part)


def split_blocks(info, rows, source, own, sent):
    core, high = info[0], info[1]
    own[...] = source[pl.ds((2 * high + core) * rows, rows), :]
    sent[...] = source[pl.ds((2 * high + 1 - core) * rows, rows), :]


def k_ffn_two_back(
    info, mine, theirs, stream, small, block, across_block, arrived, hidden,
    up_o, up_t, down_o, down_t,
    out_own, out_sent, grad_four, gain_sum, branch, grad_cross, grad_own, part, out_rows, grads,
):
    rows, width = stream.shape
    arrive(block, across_block, arrived)
    place_rows(info, block, across_block, arrived, grads)
    arrive(stream)

    def pass_back(at, first, carry):
        values = stream[at, :] + 0.5 * pair_sum(mine, theirs, at)
        unit_rows, inverse = norm_unit(values)
        out_rows[at, :] = (unit_rows * small[5:6, :]).astype(BF)
        grad, fresh = norm_back(grads[at, :].astype(F32), unit_rows, inverse, small[5:6, :])
        grad_four[at, :] = grad
        branch[at, :] = (0.5 * grad).astype(BF)
        return carry + fresh

    gain_sum[...] = over_rows(rows, pass_back, jnp.zeros((1, width), F32))
    split_blocks(info, rows // 4, out_rows, out_own, out_sent)
    ffn_grad_hidden(branch, (down_o, down_t), hidden, grad_own, grad_cross)

    def store(at, values):
        part[:, at] = values.astype(BF)

    ffn_grad_input(grad_own, grad_cross, (up_o, up_t), store)


def k_conv_back_front(
    mine, theirs, stream, small, grad_in, convolved, stats, params, conv_o, conv_t,
    grad_out, gain_sum, branch, grad_shaped, sums,
):
    rows, width = stream.shape
    channels = params.shape[1] // 2
    arrive(stream)

    def pass_back(at, first, carry):
        unit_rows, inverse = norm_unit(stream[at, :])
        grad, fresh = norm_back(pair_sum(mine, theirs, at), unit_rows, inverse, small[4:5, :])
        grad = grad_in[at, :] + grad
        grad_out[at, :] = grad
        branch[at, :] = grad.astype(BF)
        return carry + fresh

    gain_sum[...] = over_rows(rows, pass_back, jnp.zeros((1, width), F32))
    branch_rows = branch[...]
    arrive(convolved)
    for shard, weight in enumerate((conv_o, conv_t)):
        arrive(weight)
        grad_shaped[:, columns(shard, channels)] = product(branch_rows, weight[:, 2 * channels :])

    def slope(at, first, carry):
        unit_bn, shaped = shaped_rows(convolved, stats, params, at)
        grad = grad_shaped[at, :] * silu_slope(shaped)
        grad_shaped[at, :] = grad
        return (
            carry[0] + jnp.sum(grad, axis=0, keepdims=True),
            carry[1] + jnp.sum(grad * unit_bn, axis=0, keepdims=True),
        )

    zero = jnp.zeros((1, 2 * channels), F32)
    shift_sum, scale_sum = over_rows(rows, slope, (zero, zero))
    sums[0:1, :] = shift_sum
    sums[1:2, :] = scale_sum
    sums[2:8, :] = jnp.zeros((6, 2 * channels), F32)


def k_conv_back_rear(
    info, sums_mine, sums_theirs, grad_shaped, convolved, stats, params, padded, value, gate, branch,
    conv_o, conv_t,
    small_sums, mixed_own, mixed_cross, part, grad_padded,
):
    length = info[2]
    rows, width = branch.shape
    channels = params.shape[1] // 2
    sums = sums_mine[0:2, :] + sums_theirs[0:2, :]
    small_sums[5:6, :] = sums[0:1, :]
    small_sums[6:7, :] = sums[1:2, :]
    small_sums[7:8, :] = jnp.zeros((1, 2 * channels), F32)
    edge = jnp.zeros((EDGE, 2 * channels), F32)
    grad_padded[:EDGE, :] = edge
    grad_padded[EDGE + rows :, :] = edge
    arrive(convolved)
    count, bn_inverse, scale_row = stats[0:1, :], stats[2:3, :], params[5:6, :]
    grad_centre = -bn_inverse * scale_row * sums[0:1, :]
    grad_spread = -bn_inverse * bn_inverse * scale_row * sums[1:2, :]

    def spread(at, first, carry):
        centred = convolved[at, :] - stats[1:2, :]
        keep = valid_col(first, STEP, 2 * channels, length)
        grad = grad_shaped[at, :] * scale_row * bn_inverse + keep * (
            grad_centre + grad_spread * centred
        ) * (1.0 / count)
        grad_padded[pl.ds(pl.multiple_of(EDGE + first, EDGE), STEP), :] = grad
        return carry

    over_rows(rows, spread)
    arrive(padded, gate, value)
    for tile in range(2 * channels // DH):
        at = columns(tile, DH)
        grad = grad_padded[EDGE : EDGE + rows, at]
        back = None
        for offset in range(KW):
            begin = EDGE + 2 - offset
            term = params[offset : offset + 1, at] * grad_padded[begin : begin + rows, at]
            back = term if back is None else back + term
            begin = EDGE - 2 + offset
            small_sums[offset : offset + 1, at] = jnp.sum(
                grad * padded[begin : begin + rows, at], axis=0, keepdims=True
            )
        back = back * valid_col(0, rows, DH, length)
        gate_rows = gate[:, at]
        first_grad = (back * gate_rows).astype(BF)
        second_grad = (back * value[:, at] * gate_rows * (1.0 - gate_rows)).astype(BF)
        inner = (tile * DH) % channels
        if tile * DH < channels:
            mixed_own[:, inner : inner + DH] = first_grad
            mixed_own[:, channels + inner : channels + inner + DH] = second_grad
        else:
            mixed_cross[:, inner : inner + DH] = first_grad
            mixed_cross[:, channels + inner : channels + inner + DH] = second_grad
    arrive(conv_o, conv_t)
    own = mixed_own[...]
    other = mixed_cross[...]
    for index in range(width // TILE):
        at = columns(index)
        part[:, at] = (
            times_back(own, conv_o[at, : 2 * channels])
            + times_back(other, conv_t[at, : 2 * channels])
        ).astype(BF)


def k_attn_back(
    mine, theirs, stream, small, grad_in, sums_in, qkv, weights, qkv_o, qkv_t, out_o, out_t,
    grad_out, gain_sum, branch, three_cross, three_own, small_sums, part, grad_context,
):
    rows, width = stream.shape
    arrive(stream)
    third = qkv_o.shape[1] // 3
    heads = third // DH

    def pass_back(at, first, carry):
        unit_rows, inverse = norm_unit(stream[at, :])
        grad, fresh = norm_back(pair_sum(mine, theirs, at), unit_rows, inverse, small[3:4, :])
        grad = grad_in[at, :] + grad
        grad_out[at, :] = grad
        branch[at, :] = grad.astype(BF)
        return carry + fresh

    gain_sum[...] = over_rows(rows, pass_back, jnp.zeros((1, width), F32))
    branch_rows = branch[...]
    for shard, weight in enumerate((out_o, out_t)):
        arrive(weight)
        grad_context[:, columns(shard, third)] = times_back(branch_rows, weight[...]).astype(BF)
    away = lax.broadcasted_iota(jnp.int32, (rows, rows), 1) - row_iota(0, rows, rows)
    relative = jnp.clip(away, -REACH, REACH).astype(F32) * (1.0 / REACH)
    scale = DH ** (-0.5)
    arrive(qkv, weights)
    lanes = small_sums.shape[1]
    lane = lax.broadcasted_iota(jnp.int32, (1, lanes), 1)
    slope_row = jnp.zeros((1, lanes), F32)
    for shard in range(2):
        base = 3 * third * shard
        for head in range(heads):
            place = shard * heads + head
            query = qkv[:, base + head * DH : base + (head + 1) * DH]
            key = qkv[:, base + third + head * DH : base + third + (head + 1) * DH]
            value = qkv[:, base + 2 * third + head * DH : base + 2 * third + (head + 1) * DH]
            grad_head = grad_context[:, place * DH : (place + 1) * DH]
            soft = weights[place]
            grad_soft = times_back(grad_head, value)
            grad_value = inner_rows(soft.astype(BF), grad_head)
            dots = jnp.sum(soft * grad_soft, axis=-1, keepdims=True)
            grad_scores = (soft * (grad_soft - dots)).astype(BF)
            tilted = jnp.sum(grad_scores.astype(F32) * relative, axis=0, keepdims=True)
            slope = jnp.broadcast_to(jnp.sum(tilted, axis=1, keepdims=True), (1, lanes))
            slope_row = jnp.where(lane == shard * (lanes // 2) + head, slope, slope_row)
            grads = (
                product(grad_scores, key) * scale,
                inner_rows(grad_scores, query) * scale,
                grad_value,
            )
            for index, grad in enumerate(grads):
                begin = index * third + head * DH
                if shard == 0:
                    three_own[:, begin : begin + DH] = grad.astype(BF)
                else:
                    three_cross[:, begin : begin + DH] = grad.astype(BF)
    small_sums[:7, :] = sums_in[:7, :]
    small_sums[7:8, :] = slope_row
    arrive(qkv_o, qkv_t)
    own = three_own[...]
    other = three_cross[...]
    for index in range(width // TILE):
        at = columns(index)
        part[:, at] = (times_back(own, qkv_o[at, :]) + times_back(other, qkv_t[at, :])).astype(BF)


def k_ffn_one_back(
    info, mine, theirs, stream, small, grad_in, hidden, up_o, up_t, down_o, down_t,
    grad_out, gain_sum, branch, grad_cross, grad_own, part_own, part_sent, whole,
):
    high = info[1]
    rows, width = stream.shape
    span = rows // 2
    arrive(stream)

    def pass_back(at, first, carry):
        unit_rows, inverse = norm_unit(stream[at, :])
        grad, fresh = norm_back(pair_sum(mine, theirs, at), unit_rows, inverse, small[2:3, :])
        grad = grad_in[at, :] + grad
        grad_out[at, :] = grad
        branch[at, :] = (0.5 * grad).astype(BF)
        return carry + fresh

    gain_sum[...] = over_rows(rows, pass_back, jnp.zeros((1, width), F32))
    ffn_grad_hidden(branch, (down_o, down_t), hidden, grad_own, grad_cross)

    def store(at, values):
        whole[:, at] = values

    ffn_grad_input(grad_own, grad_cross, (up_o, up_t), store)
    part_own[...] = whole[pl.ds(high * span, span), :]
    part_sent[...] = whole[pl.ds((1 - high) * span, span), :].astype(BF)


def k_last(
    info, starts, part_own, arrived, frames, small, grad_in,
    grad_own, grad_sent, sums, grads,
):
    core, high, length = info[0], info[1], info[2]
    span, width = part_own.shape
    arrive(frames)

    def pass_back(at, first, carry):
        begin = pl.multiple_of(high * span + first, STEP)
        mask = mask_col(starts, begin, STEP, length)
        unit_rows, inverse = norm_unit(
            masked_rows(frames[pl.ds(begin, STEP), :], mask, small[0:1, :])
        )
        grad_normed = part_own[at, :] + arrived[at, :].astype(F32)
        grad, fresh = norm_back(grad_normed, unit_rows, inverse, small[1:2, :])
        grad = grad_in[pl.ds(begin, STEP), :] + grad
        hit = jnp.broadcast_to(mask, grad.shape) > 0.5
        grads[at, :] = jnp.where(hit, 0.0, grad)
        masked_part = jnp.sum(jnp.where(hit, grad, 0.0), axis=0, keepdims=True)
        return carry[0] + masked_part, carry[1] + fresh

    zero = jnp.zeros((1, width), F32)
    mask_sum, gain_sum = over_rows(span, pass_back, (zero, zero))
    sums[0:1, :] = mask_sum
    sums[1:2, :] = gain_sum
    rows = span // 2
    grad_own[...] = grads[pl.ds(core * rows, rows), :]
    grad_sent[...] = grads[pl.ds((1 - core) * rows, rows), :]


def k_weights(pairs, bit, tiles, info, *refs):
    count = 1 + max(max(pair[place] for place in (0, 1, 2, 4)) for pair in pairs)
    inputs, kept, sent = refs[:count], refs[count], refs[count + 1 :]
    mine = (info[3] >> bit) & 1
    low = bit - tiles
    rows = kept.shape[1]
    cut = sent[0].shape[2]
    for index in range(kept.shape[0]):
        high_part, low_part = index >> low, index & ((1 << low) - 1)
        for side in range(2):
            tile = (high_part * 2 + (mine ^ side)) * (1 << low) + low_part
            at = pl.ds(pl.multiple_of(tile * rows, rows), rows)
            begin = 0
            for left, left_too, right, shift, right_too, shift_too, size in pairs:
                for piece in range(0, size, TILE):
                    grad = inner_rows(
                        inputs[left][:, at],
                        inputs[right][:, shift + piece : shift + piece + TILE],
                    ) + inner_rows(
                        inputs[left_too][:, at],
                        inputs[right_too][:, shift_too + piece : shift_too + piece + TILE],
                    )
                    place = begin + piece
                    if side == 0:
                        kept[index, :, place : place + TILE] = grad
                    else:
                        inside = place % cut
                        sent[place // cut][index, :, inside : inside + TILE] = grad.astype(BF)
                begin += size


def k_fold(bit, count, info, held, *refs):
    arrivals, kept, sent = refs[:count], refs[count], refs[count + 1 :]
    mine = (info[3] >> bit) & 1
    cut_in, cut_out = arrivals[0].shape[3], sent[0].shape[2]
    size = min(cut_in, cut_out)
    for index in range(held.shape[0]):
        for side in range(2):
            at = pl.ds(mine ^ side, 1)
            for begin in range(0, held.shape[3], size):
                spot = slice(begin, begin + size)
                inside = slice(begin % cut_in, begin % cut_in + size)
                total = held[index, at, :, spot][0]
                total = total + arrivals[begin // cut_in][index, at, :, inside][0].astype(F32)
                if side == 0:
                    kept[index, :, spot] = total
                else:
                    inside = slice(begin % cut_out, begin % cut_out + size)
                    sent[begin // cut_out][index, :, inside] = total.astype(BF)


def k_finish(turned, count, info, kept, *refs):
    arrivals, results = refs[:count], refs[count:]
    cut = arrivals[0].shape[1]
    begin = 0
    for result, turn in zip(results, turned):
        size = result.shape[0] if turn else result.size // result.shape[0]
        for piece in range(begin, begin + size, DH):
            spot = slice(piece, piece + DH)
            at = piece - begin
            inside = slice(piece % cut, piece % cut + DH)
            total = kept[:, spot] + arrivals[piece // cut][:, inside].astype(F32)
            if turn:
                result[at : at + DH, :] = total.T
            elif len(result.shape) == 3:
                result[:, at // result.shape[2], pl.ds(at % result.shape[2], DH)] = total
            else:
                result[:, at : at + DH] = total
        begin += size


def k_in_order(info, own, other, result):
    core = info[0]
    result[pl.ds(core, 1)] = own[...][None]
    result[pl.ds(1 - core, 1)] = other[...][None]


def k_gather(bit, info, held, arrived, result):
    mine = (info[3] >> bit) & 1
    result[:, pl.ds(mine, 1)] = held[...][:, None]
    result[:, pl.ds(1 - mine, 1)] = arrived[...][:, None]


def k_smalls(last, attn, conv, two, final, channel_sums, result):
    width = attn.shape[1]
    result[0:2, :width] = last[...]
    for place, entry in enumerate((attn, conv, two, final), 2):
        result[place : place + 1, :width] = 0.5 * entry[...]
    result[6:8, :width] = jnp.zeros((2, width), F32)
    result[:, width:] = channel_sums[...]


def k_smalls_cross(smalls, result):
    width = smalls.shape[1] - 2 * (smalls.shape[1] - result.shape[1])
    channels = result.shape[1] - width
    result[:, :width] = smalls[:, :width]
    result[:, width:] = smalls[:, width + channels :]


def k_gains(mine, theirs, channel_sums, result):
    width = mine.shape[1]
    result[:, :width] = mine[...] + theirs[...]
    result[:, width:] = channel_sums[...]


def k_smalls_add(smalls, arrived, result):
    size = result.shape[1]
    result[...] = smalls[:, :size] + arrived[...]


def run(kernel, results, arguments, scalars=1, scratch=(), late=(), leaving=(), cost=1):
    given, made = len(arguments), len(results)
    hbm_shapes = [(arguments[place].shape, arguments[place].dtype) for place in late]
    hbm_shapes += [results[place] for place in leaving]
    buffers = [pltpu.VMEM(shape, kind) for shape, kind in hbm_shapes]
    own = [pltpu.VMEM(shape, kind) for shape, kind in scratch]
    hbm = pl.BlockSpec(memory_space=pltpu.HBM)

    def body(*refs):
        ins, outs = list(refs[:given]), list(refs[given : given + made])
        rest = refs[given + made :]
        extra, held, semaphores = rest[: len(own)], rest[len(own) : -1], rest[-1]
        for index, place in enumerate(late):
            ins[place] = Late(ins[place], held[index], semaphores.at[index])
        for index, place in enumerate(leaving, len(late)):
            outs[place] = Leaving(outs[place], held[index], semaphores.at[index])
        kernel(*ins, *outs, *extra)
        arrive(*ins)
        for place in leaving:
            outs[place].finish()

    def plain(*refs):
        kernel(*refs)

    held_bytes = sum(
        functools.reduce(lambda a, b: a * b, shape) * jnp.dtype(kind).itemsize
        for shape, kind in [*scratch, *hbm_shapes]
    )
    specs = [SMEM_SPEC] * scalars + [VMEM_SPEC] * (given - scalars)
    out_specs = [VMEM_SPEC] * made
    for place in late:
        specs[place] = hbm
    for place in leaving:
        out_specs[place] = hbm
    many = len(hbm_shapes)
    return pl.pallas_call(
        body if many else plain,
        out_shape=[
            pltpu.HBM(shape, kind) if place in leaving else pltpu.VMEM(shape, kind)
            for place, (shape, kind) in enumerate(results)
        ],
        in_specs=specs,
        out_specs=out_specs,
        scratch_shapes=own + buffers + ([pltpu.SemaphoreType.DMA((many,))] if many else []),
        compiler_params=pltpu.CompilerParams(vmem_limit_bytes=held_bytes + 8 * MIB),
        cost_estimate=pl.CostEstimate(flops=cost, bytes_accessed=cost, transcendentals=0),
    )(*(
        entry if place < scalars else pltpu.with_memory_space_constraint(
            entry, pltpu.HBM if place in late else pltpu.VMEM
        )
        for place, entry in enumerate(arguments)
    ))


def swap(value, axis, bit):
    size = lax.axis_size(axis)
    return lax.ppermute(value, axis, [(place, place ^ bit) for place in range(size)])


def across(value):
    return swap(value, "tensor", 2)


def beside(value):
    return swap(value, "tensor", 1)


def bit_of(axis, bit):
    return (lax.axis_index(axis) & bit) != 0


def tie(*values):
    return lax.optimization_barrier(values)


class RowSum:
    def __init__(self, info, inputs, pairs, width, first_bits, cuts=1, cost=1):
        size = lax.axis_size("dp")
        levels = size.bit_length() - 1
        tiles = max(levels - 3, 0)
        order = [tiles + bit for bit in first_bits]
        self.order = order + [bit for bit in range(levels - 1, -1, -1) if bit not in order]
        self.left = list(range(levels - 1, -1, -1))
        self.total = sum(pair[-1] for pair in pairs)
        self.block = width // size
        self.info = info
        count = size >> tiles
        shape = (count // 2, width // count)
        self.kept, *self.sent = run(
            functools.partial(k_weights, pairs, self.order[0], tiles),
            [((*shape, self.total), F32)] + [((*shape, self.total // cuts), BF)] * cuts,
            [info] + inputs,
            cost=cost,
        )
        self.begin()

    def begin(self):
        self.bit = self.order.pop(0)
        self.left.remove(self.bit)
        self.arrived = []

    def send(self, chain=None):
        piece = self.sent.pop(0)
        if chain is not None:
            (piece,) = chain.after(piece)
        self.arrived.append(swap(piece, "dp", 1 << self.bit))

    def here(self, chain):
        (self.arrived[-1],) = chain.after(self.arrived[-1])

    def fold(self, chain, cuts=1, cost=1):
        bit = self.order[0]
        place = self.left.index(bit)
        inner = self.block << (len(self.left) - 1 - place)
        outer = 1 << place
        kept, *arrived = chain.after(self.kept, *self.arrived)
        self.kept, *self.sent = run(
            functools.partial(k_fold, bit, len(arrived)),
            [((outer, inner, self.total), F32)] + [((outer, inner, self.total // cuts), BF)] * cuts,
            [self.info, kept.reshape(outer, 2, inner, self.total)]
            + [entry.reshape(outer, 2, inner, -1) for entry in arrived],
            cost=cost,
        )
        self.kept, chain.last = tie(self.kept, chain.last)
        self.begin()

    def step(self, chain, cost=1):
        self.fold(chain, cost=cost)
        self.send()

    def finish(self, chain, *results):
        while self.order:
            self.step(chain)
        shape = (self.block, self.total)
        kept, *arrived = chain.after(
            self.kept.reshape(shape), *(entry.reshape(self.block, -1) for entry in self.arrived)
        )
        sums = run(
            functools.partial(k_finish, tuple(turn for _, turn in results), len(arrived)),
            [(size, F32) for size, _ in results],
            [self.info, kept, *arrived],
        )
        *sums, chain.last = tie(*sums, chain.last)
        return sums


class Chain:
    def __init__(self, last):
        self.last = last

    def after(self, *values):
        *values, self.last = tie(*values, self.last)
        return values


class Gather:
    def __init__(self, info, block):
        self.info, self.held = info, block.reshape(1, *block.shape)
        self.bit = lax.axis_size("dp") // 2
        self.shape = (lax.axis_size("dp") * block.shape[0], block.shape[1])

    def send(self):
        self.arrived = swap(self.held, "dp", self.bit)

    def take(self):
        outer, rows, width = self.held.shape
        (held,) = run(
            functools.partial(k_gather, self.bit.bit_length() - 1),
            [((outer, 2, rows, width), self.held.dtype)],
            [self.info, self.held, self.arrived],
        )
        self.held = held.reshape(outer * 2, rows, width)
        self.bit //= 2

    def whole(self):
        while self.bit:
            self.send()
            self.take()
        return self.held.reshape(self.shape)


def sum_pair(value, axis, merge=None):
    bit, size = 1, lax.axis_size(axis)
    while bit * 2 < size:
        (value,) = run(
            merge or k_add, [(value.shape, F32)], [value, swap(value, axis, bit)], scalars=0
        )
        bit *= 2
    return value, swap(value, axis, bit)


def per_device(
    frames,
    lengths,
    span_starts,
    mask_vector,
    ffn1_gain,
    ffn1_up,
    ffn1_down,
    attn_gain,
    query_weight,
    key_weight,
    value_weight,
    output_weight,
    rel_slope,
    conv_gain,
    conv_up,
    conv_depth,
    bn_scale,
    bn_shift,
    conv_down,
    ffn2_gain,
    ffn2_up,
    ffn2_down,
    final_gain,
    cotangent,
):
    batches, row_count, width = frames.shape
    length = row_count * lax.axis_size("tensor")
    span = 2 * row_count
    channels = conv_depth.shape[1]
    hidden_width = ffn1_up.shape[1]
    heads = rel_slope.shape[0]
    third = query_weight.shape[1]
    core = lax.axis_index("tensor") & 1
    high = (lax.axis_index("tensor") >> 1) & 1
    group = lax.axis_index("dp")
    on_first = core == 0
    own_length = jnp.where(on_first, lengths[0], lengths[1])
    info = jnp.stack([core, high, own_length, group]).astype(jnp.int32)
    starts = jnp.where(on_first, span_starts[0:1], span_starts[1:2])

    frames_across = across(frames)
    conv_block = jnp.concatenate(
        [conv_up.reshape(conv_up.shape[0], 2 * channels), conv_down.T], axis=1
    )
    conv_weights = Gather(info, conv_block)
    conv_weights.send()

    part = mask_vector.shape[0]
    place = (group * lax.axis_size("tensor") + lax.axis_index("tensor")) * part
    vectors = jnp.stack(
        [mask_vector.astype(F32), ffn1_gain, attn_gain, conv_gain, ffn2_gain, final_gain,
         jnp.zeros_like(ffn1_gain), jnp.zeros_like(ffn1_gain)]
    )
    small = lax.dynamic_update_slice(jnp.zeros((8, width), F32), vectors, (0, place))
    hops = [("tensor", 1), ("dp", 2), ("dp", 1), ("tensor", 2)]
    bit = 4
    while bit < lax.axis_size("dp"):
        hops.append(("dp", bit))
        bit *= 2
    for step, (axis, bit) in enumerate(hops):
        if step == 4:
            (sent,) = run(k_pick, [(frames.shape, BF)], [info, frames, frames_across])
            sent, small = tie(sent, small)
        if step == 3:
            query_weight, key_weight, conv_depth, rel_slope, small = tie(
                query_weight, key_weight, conv_depth, rel_slope, small
            )
            own_qkv = jnp.concatenate([query_weight, key_weight, value_weight], axis=1)
            slope_row = jnp.pad(rel_slope[None], ((0, 0), (0, channels - heads)))
            own_params = jnp.concatenate([conv_depth, bn_scale[None], bn_shift[None], slope_row])
            other_params = beside(own_params)
            conv_weights.arrived, small = tie(conv_weights.arrived, small)
            conv_weights.take()
            if conv_weights.bit:
                conv_weights.send()
        if bit < lax.axis_size(axis):
            (small,) = run(
                k_add, [(small.shape, F32)], [small, swap(small, axis, bit)], scalars=0
            )
    if conv_weights.bit:
        conv_weights.arrived, small = tie(conv_weights.arrived, small)
        conv_weights.take()
    frame_parts = [frames, frames_across, beside(sent)]
    own_qkv, other_params, conv_weights.held, small = tie(
        own_qkv, other_params, conv_weights.held, small
    )
    params = jnp.concatenate([own_params, other_params], axis=1)
    slopes = jnp.concatenate([rel_slope, other_params[KW + 2, :heads]])
    if conv_weights.bit:
        conv_weights.send()
    up_one, down_one = beside(ffn1_up), beside(ffn1_down)

    wide = (length, width)
    ffn_outs = [
        (wide, BF),
        ((length, hidden_width), BF),
        ((length, hidden_width), BF),
        ((length, 2 * hidden_width), F32),
        (wide, BF),
    ]
    whole, norm_one, cross_one, active_one, hidden_one, partial = run(
        k_ffn_one,
        [(wide, BF)] + ffn_outs,
        [info, starts, *frame_parts, small, ffn1_up, up_one, ffn1_down, down_one],
        scratch=[(wide, BF)], late=(6, 8),
    )
    output_weight, active_one = tie(output_weight, active_one)
    other_qkv, other_out = beside(own_qkv), beside(output_weight)
    stream_one, norm_attn, context_cross, context_own, qkv, weights, partial = run(
        k_attn_wrapped,
        [
            (wide, F32),
            (wide, BF),
            ((length, third), BF),
            ((length, third), BF),
            ((length, 6 * third), BF),
            ((2 * heads, length, length), F32),
            (wide, BF),
        ],
        [info, slopes, starts, partial, across(partial), whole, small, own_qkv, other_qkv,
         output_weight, other_out],
        scalars=2, late=(7, 9),
    )
    conv_weights.arrived, norm_one, cross_one, context_own = tie(
        conv_weights.arrived, norm_one, cross_one, context_own
    )
    conv_weights.take()
    own_conv = conv_weights.whole()
    other_conv = beside(own_conv)
    norm_one_too, cross_one_too = beside(norm_one), beside(cross_one)
    norm_one_too, cross_one_too, params = tie(norm_one_too, cross_one_too, params)
    both_channels = (length, 2 * channels)
    stat_shape = ((8, 2 * channels), F32)
    stream_two, norm_conv, value, gate, padded, convolved, stats = run(
        k_conv_front,
        [
            (wide, F32),
            (wide, BF),
            (both_channels, F32),
            (both_channels, F32),
            ((length + 2 * EDGE, 2 * channels), F32),
            (both_channels, F32),
            stat_shape,
        ],
        [info, partial, across(partial), stream_one, small, params, own_conv, other_conv],
        late=(6,),
    )
    norm_attn, context_cross, cotangent, ffn2_up, ffn2_down, value = tie(
        norm_attn, context_cross, cotangent, ffn2_up, ffn2_down, value
    )
    stats, stats_too = sum_pair(stats, "dp", k_merge)
    grad_across = across(cotangent)
    up_two, down_two = beside(ffn2_up), beside(ffn2_down)
    norm_attn_too, context_cross_too = beside(norm_attn), beside(context_cross)
    norm_attn_too, context_cross_too, params, grad_across = tie(
        norm_attn_too, context_cross_too, params, grad_across
    )
    stats, active_conv, cross_conv, partial = run(
        k_conv_rear,
        [stat_shape, ((length, channels), BF), ((length, channels), BF), (wide, BF)],
        [stats, stats_too, convolved, params, norm_conv, own_conv, other_conv],
        scalars=0, late=(5,),
    )
    grad_across, active_conv = tie(grad_across, active_conv)
    (sent,) = run(k_pick, [(cotangent.shape, BF)], [info, cotangent, grad_across])
    grad_parts = [cotangent, grad_across, beside(sent)]
    grad_parts[2], small = tie(grad_parts[2], small)
    stream_three, norm_two, cross_two, active_two, hidden_two, partial = run(
        k_ffn_two,
        [(wide, F32)] + ffn_outs,
        [partial, across(partial), stream_two, small, ffn2_up, up_two, ffn2_down, down_two],
        scalars=0, late=(4, 6),
    )
    norm_two, cross_two, norm_conv, cross_conv, active_two = tie(
        norm_two, cross_two, norm_conv, cross_conv, active_two
    )
    norm_two_too, cross_two_too = beside(norm_two), beside(cross_two)
    norm_conv_too, cross_conv_too = beside(norm_conv), beside(cross_conv)
    norm_two_too, cross_two_too, norm_conv_too, cross_conv_too, small = tie(
        norm_two_too, cross_two_too, norm_conv_too, cross_conv_too, small
    )

    row_shape = ((1, width), F32)
    block_shape = (row_count, width)
    out_own, out_sent, grad_four, sum_final, back_two, hid_cross_two, hid_two, partial = run(
        k_ffn_two_back,
        [
            (block_shape, BF),
            (block_shape, BF),
            (wide, F32),
            row_shape,
            (wide, BF),
            ((length, hidden_width), BF),
            ((length, hidden_width), BF),
            (wide, BF),
        ],
        [info, partial, across(partial), stream_three, small, *grad_parts, hidden_two,
         ffn2_up, up_two, ffn2_down, down_two],
        scratch=[(wide, BF), (wide, BF)], late=(9, 11),
    )
    back_two_too, hid_cross_two_too = beside(back_two), beside(hid_cross_two)
    ffn_pair = ((0, 1, 2, 0, 3, 0, hidden_width),)
    two_up = RowSum(
        info, [norm_two, norm_two_too, hid_two, hid_cross_two_too], ffn_pair, width, (0, 1, 2)
    )
    two_down = RowSum(
        info, [back_two, back_two_too, active_two, cross_two_too], ffn_pair, width, (1, 2, 0)
    )
    grad_four, two_up.sent[0], two_down.sent[0] = tie(
        grad_four, two_up.sent[0], two_down.sent[0]
    )
    grad_three, sum_two, back_conv, grad_shaped, sums = run(
        k_conv_back_front,
        [(wide, F32), row_shape, (wide, BF), (both_channels, F32), stat_shape],
        [partial, across(partial), stream_three, small, grad_four, convolved, stats, params,
         own_conv, other_conv],
        scalars=0, late=(8,),
    )
    out_sent, sum_two, back_conv = tie(out_sent, sum_two, back_conv)
    out_other, back_conv_too = beside(out_sent), beside(back_conv)
    sums, sums_too = sum_pair(sums, "dp")
    sums_too, out_other, back_conv_too = tie(sums_too, out_other, back_conv_too)
    chain = Chain(sums_too)
    two_up.send(chain)
    two_down.send(chain)
    sums_too = chain.last
    small_sums, mixed_own, mixed_cross, partial = run(
        k_conv_back_rear,
        [
            stat_shape,
            ((length, 2 * channels), BF),
            ((length, 2 * channels), BF),
            (wide, BF),
        ],
        [info, sums, sums_too, grad_shaped, convolved, stats, params, padded, value, gate,
         back_conv, own_conv, other_conv],
        scratch=[((length + 2 * EDGE, 2 * channels), F32)], late=(11,),
    )
    mixed_cross_too = beside(mixed_cross)
    mixed_cross_too, grad_three = tie(mixed_cross_too, grad_three)
    grad_two, sum_conv, back_attn, three_cross, three_own, small_sums, partial = run(
        k_attn_back,
        [
            (wide, F32),
            row_shape,
            (wide, BF),
            ((length, 3 * third), BF),
            ((length, 3 * third), BF),
            stat_shape,
            (wide, BF),
        ],
        [partial, across(partial), stream_two, small, grad_three, small_sums, qkv, weights,
         own_qkv, other_qkv, output_weight, other_out],
        scalars=0,
        scratch=[((length, 2 * third), BF)], late=(8, 10),
    )
    back_attn_too, three_cross_too = beside(back_attn), beside(three_cross)
    chain = Chain(small_sums)
    for entry in (two_up, two_down):
        entry.step(chain)
    back_attn, three_own = chain.after(back_attn, three_own)
    small_sums = chain.last
    middle = RowSum(
        info,
        [norm_conv, norm_conv_too, mixed_own, mixed_cross_too,
         back_conv, back_conv_too, active_conv, cross_conv_too,
         norm_attn, norm_attn_too, three_own, three_cross_too,
         back_attn, back_attn_too, context_own, context_cross_too],
        (
            (0, 1, 2, 0, 3, 0, 2 * channels),
            (4, 5, 6, 0, 7, 0, channels),
            (8, 9, 10, 0, 11, 0, 3 * third),
            (12, 13, 14, 0, 15, 0, third),
        ),
        width, (0, 1, 2),
    )
    middle.send()
    middle.kept, grad_two = tie(middle.kept, grad_two)
    grad_one, sum_attn, back_one, hid_cross_one, hid_one, last_own, last_sent = run(
        k_ffn_one_back,
        [
            (wide, F32),
            row_shape,
            (wide, BF),
            ((length, hidden_width), BF),
            ((length, hidden_width), BF),
            ((span, width), F32),
            ((span, width), BF),
        ],
        [info, partial, across(partial), stream_one, small, grad_two, hidden_one,
         ffn1_up, up_one, ffn1_down, down_one],
        scratch=[(wide, F32)], late=(7, 9),
    )
    back_one_too, hid_cross_one_too = beside(back_one), beside(hid_cross_one)
    chain = Chain(sum_attn)
    for entry in (two_up, two_down):
        entry.step(chain, cost=COST)
    hid_one, active_one = chain.after(hid_one, active_one)
    one_up = RowSum(
        info, [norm_one, norm_one_too, hid_one, hid_cross_one_too], ffn_pair, width, (0, 1, 2),
        cost=COST,
    )
    one_down = RowSum(
        info, [back_one, back_one_too, active_one, cross_one_too], ffn_pair, width, (0, 1, 2),
        cost=COST,
    )
    one_up.send(chain)
    one_up.kept, chain.last = tie(one_up.kept, chain.last)
    one_down.send(chain)
    one_down.kept, chain.last = tie(one_down.kept, chain.last)
    block = width // lax.axis_size("dp")
    (starts,) = chain.after(starts)
    sum_attn = chain.last
    frames_own, frames_sent, last_sums = run(
        k_last,
        [(block_shape, F32), (block_shape, F32), ((2, width), F32)],
        [info, starts, last_own, across(last_sent), whole, small, grad_one],
        scratch=[((span, width), F32)],
    )
    frames_other = beside(frames_sent)
    (smalls,) = run(
        k_smalls, [((8, width + 2 * channels), F32)],
        [last_sums, sum_attn, sum_conv, sum_two, sum_final, small_sums], scalars=0,
    )
    (smalls_sent,) = run(k_smalls_cross, [((8, width + channels), F32)], [smalls], scalars=0)
    (smalls,) = run(
        k_smalls_add, [((8, width + channels), F32)], [smalls, beside(smalls_sent)], scalars=0
    )
    gains, gains_too = smalls[:, :width], across(smalls[:, :width])
    (gains,) = run(
        k_gains, [(smalls.shape, F32)], [gains, gains_too, smalls[:, width:]], scalars=0
    )

    def in_order(own, other):
        return run(k_in_order, [((2, *own.shape), own.dtype)], [info, own, other])[0]

    chain = Chain(in_order(out_own, out_other))

    def hop(value, bit):
        (value,) = chain.after(value)
        return value, swap(value, "dp", bit)

    def add(value, other):
        (total,) = run(k_add, [(value.shape, F32)], chain.after(value, other), scalars=0)
        return total

    first, *between = [1 << level for level in range(1, lax.axis_size("dp").bit_length() - 1)]
    gains = add(*hop(gains, first))
    gains, chain.last = tie(gains, chain.last)
    (two_up,) = two_up.finish(chain, ((block, hidden_width), False))
    middle.step(chain)
    for bit in between:
        gains = add(*hop(gains, bit))
    gains, chain.last = tie(gains, chain.last)
    middle.step(chain)
    one_up.step(chain)
    one_down.step(chain)
    one_up.step(chain)
    conv_up_grad, conv_down_grad, query_grad, key_grad, value_grad, output_grad = middle.finish(
        chain,
        (conv_up.shape, False), ((channels, block), True),
        *[((block, third), False)] * 3, ((third, block), True),
    )
    gains, gains_too = hop(gains, 1)
    (one_up,) = one_up.finish(chain, ((block, hidden_width), False))
    gains = add(gains, gains_too)
    one_down.step(chain)
    (two_down,) = two_down.finish(chain, ((hidden_width, block), True))
    channel_sums = gains[:, width:]
    scale_grad = channel_sums[KW + 1] * (1.0 / lax.axis_size("dp"))
    shift_grad = channel_sums[KW] * (1.0 / lax.axis_size("dp"))
    gains = lax.dynamic_slice_in_dim(gains, place, part, axis=1)

    frames_grad = in_order(frames_own, frames_other)
    smallest = [
        *(gains[index] for index in range(6)),
        channel_sums[KW + 2, :heads],
        channel_sums[:KW],
        scale_grad,
        shift_grad,
    ]
    frames_grad, *smallest = chain.after(frames_grad, *smallest)
    (one_down,) = one_down.finish(chain, ((hidden_width, block), True))

    return (
        chain.last,
        frames_grad,
        smallest[0],
        smallest[1],
        one_up,
        one_down,
        smallest[2],
        query_grad,
        key_grad,
        value_grad,
        output_grad,
        smallest[6],
        smallest[3],
        conv_up_grad,
        smallest[7],
        smallest[8],
        smallest[9],
        conv_down_grad,
        smallest[4],
        two_up,
        two_down,
        smallest[5],
    )


def k_attn_wrapped(info, slopes, starts, *refs):
    k_attn(info, starts, slopes, *refs)


def solution(mesh):
    every, split, by_column = P(("dp", "tensor")), P("tensor"), P(None, "tensor")
    rows_by = P("dp", "tensor", None)
    return jax.shard_map(
        per_device,
        mesh=mesh,
        in_specs=(
            rows_by,
            P("dp"),
            P("dp", None),
            every,
            every,
            by_column,
            P("tensor", None),
            every,
            by_column,
            by_column,
            by_column,
            P("tensor", None),
            split,
            every,
            P("dp", None, "tensor"),
            by_column,
            split,
            split,
            P("tensor", "dp"),
            every,
            by_column,
            P("tensor", None),
            every,
            rows_by,
        ),
        out_specs=(
            rows_by,
            rows_by,
            every,
            every,
            P("dp", "tensor"),
            P("tensor", "dp"),
            every,
            P("dp", "tensor"),
            P("dp", "tensor"),
            P("dp", "tensor"),
            P("tensor", "dp"),
            split,
            every,
            P("dp", None, "tensor"),
            by_column,
            split,
            split,
            P("tensor", "dp"),
            every,
            P("dp", "tensor"),
            P("tensor", "dp"),
            every,
        ),
        check_vma=False,
    )
```

```python
import functools

import jax
import jax.numpy as jnp
from jax import lax
from jax.experimental import pallas as pl
from jax.experimental.pallas import tpu as pltpu
from jax.sharding import PartitionSpec as P

DH = 128
KW = 5
SPAN = 10
REACH = 128
EPSILON = 1e-05
MASKED_SCORE = -1000000000.0
BF = jnp.bfloat16
F32 = jnp.float32
STEP = 32
TILE = 256
EDGE = 8
MIB = 1024 * 1024
COST = 30_000_000

VMEM_SPEC = pl.BlockSpec(memory_space=pltpu.VMEM)
SMEM_SPEC = pl.BlockSpec(memory_space=pltpu.SMEM)


def product(left, right):
    return jnp.dot(left, right, preferred_element_type=F32)


def inner_rows(left, right):
    return lax.dot_general(left, right, (((0,), (0,)), ((), ())), preferred_element_type=F32)


def times_back(left, right):
    return lax.dot_general(left, right, (((1,), (1,)), ((), ())), preferred_element_type=F32)


def sigmoid(values):
    return 0.5 * jnp.tanh(0.5 * values) + 0.5


def norm_unit(values):
    centre = jnp.mean(values, axis=-1, keepdims=True)
    centred = values - centre
    inverse = lax.rsqrt(jnp.mean(centred * centred, axis=-1, keepdims=True) + EPSILON)
    return centred * inverse, inverse


def norm_back(grad_out, unit_rows, inverse, norm_gain):
    grad_unit = grad_out * norm_gain
    first_mean = jnp.mean(grad_unit, axis=-1, keepdims=True)
    second_mean = jnp.mean(grad_unit * unit_rows, axis=-1, keepdims=True)
    return (
        inverse * (grad_unit - first_mean - unit_rows * second_mean),
        jnp.sum(grad_out * unit_rows, axis=0, keepdims=True),
    )


def silu_slope(values):
    gate_value = sigmoid(values)
    return gate_value * (1.0 + values * (1.0 - gate_value))


def over_rows(count, body, init=0, step=STEP):
    def one(index, carry):
        return body(pl.ds(pl.multiple_of(index * step, step), step), index * step, carry)

    return lax.fori_loop(0, count // step, one, init, unroll=True)


def row_iota(first, rows, columns):
    return first + lax.broadcasted_iota(jnp.int32, (rows, columns), 0)


def mask_col(starts_ref, first, rows, length):
    starts = starts_ref[...]
    at = row_iota(first, rows, starts.shape[1])
    hit = (starts <= at) & (at < starts + SPAN) & (at < length)
    return jnp.max(jnp.where(hit, 1.0, 0.0), axis=1, keepdims=True)


def valid_col(first, rows, columns, length):
    return jnp.where(row_iota(first, rows, columns) < length, 1.0, 0.0)


def masked_rows(frame_rows, mask, mask_row):
    return jnp.where(
        jnp.broadcast_to(mask, frame_rows.shape) > 0.5, mask_row, frame_rows.astype(F32)
    )


def pair_sum(mine, theirs, rows):
    return mine[rows, :].astype(F32) + theirs[rows, :].astype(F32)


class Late:
    def __init__(self, source, held, semaphore):
        self.copy = pltpu.make_async_copy(source, held, semaphore)
        self.copy.start()
        self.held, self.shape, self.dtype, self.waited = held, held.shape, held.dtype, False

    def arrive(self):
        if not self.waited:
            self.copy.wait()
            self.waited = True

    def __getitem__(self, index):
        assert self.waited
        return self.held[index]


class Leaving:
    def __init__(self, target, held, semaphore):
        self.copy = pltpu.make_async_copy(held, target, semaphore)
        self.held, self.shape, self.dtype, self.started = held, held.shape, held.dtype, False

    def leave(self):
        if not self.started:
            self.copy.start()
            self.started = True

    def finish(self):
        self.leave()
        self.copy.wait()

    def __getitem__(self, index):
        return self.held[index]

    def __setitem__(self, index, value):
        assert not self.started
        self.held[index] = value


def arrive(*refs):
    for ref in refs:
        if isinstance(ref, Late):
            ref.arrive()


def leave(*refs):
    for ref in refs:
        if isinstance(ref, Leaving):
            ref.leave()


def columns(index, size=TILE):
    return slice(index * size, (index + 1) * size)


def ffn_up(branch, ups, hidden, active_own, active_cross):
    normed = branch[...]
    for shard, weight in enumerate(ups):
        arrive(weight)
        tiles = weight.shape[1] // TILE
        for index in range(tiles):
            at = columns(index)
            values = product(normed, weight[:, at])
            hidden[:, columns(index + shard * tiles)] = values
            (active_own, active_cross)[shard][:, at] = (values * sigmoid(values)).astype(BF)


def ffn_down(active_own, active_cross, downs, part):
    width = downs[0].shape[1]
    own, cross = active_own[...], active_cross[...]
    arrive(*downs)
    for index in range(width // TILE):
        at = columns(index)
        part[:, at] = (product(own, downs[0][:, at]) + product(cross, downs[1][:, at])).astype(BF)


def ffn_grad_hidden(branch, downs, hidden, grad_own, grad_cross):
    grad_branch = branch[...]
    for shard, weight in enumerate(downs):
        arrive(weight)
        tiles = weight.shape[0] // TILE
        for index in range(tiles):
            at = columns(index)
            slope = silu_slope(hidden[:, columns(index + shard * tiles)])
            grad = (times_back(grad_branch, weight[at, :]) * slope).astype(BF)
            (grad_own, grad_cross)[shard][:, at] = grad


def ffn_grad_input(grad_own, grad_cross, ups, store):
    own, cross = grad_own[...], grad_cross[...]
    arrive(*ups)
    for index in range(ups[0].shape[0] // TILE):
        at = columns(index)
        store(at, times_back(own, ups[0][at, :]) + times_back(cross, ups[1][at, :]))


def k_pick(info, block, across_block, sent):
    core = info[0]
    sent[0] = block[pl.ds(1 - core, 1)][0]
    sent[1] = across_block[pl.ds(1 - core, 1)][0]


def place_rows(info, block, across_block, arrived, whole):
    core, high = info[0], info[1]
    rows = block.shape[1]
    places = (
        (2 * high + core, block[pl.ds(core, 1)][0]),
        (2 * (1 - high) + core, across_block[pl.ds(core, 1)][0]),
        (2 * high + 1 - core, arrived[0]),
        (2 * (1 - high) + 1 - core, arrived[1]),
    )
    for place, value in places:
        whole[pl.ds(pl.multiple_of(place * rows, rows), rows), :] = value


def k_ffn_one(
    info, starts, block, across_block, arrived, small, up_o, up_t, down_o, down_t,
    frames, branch, active_cross, active_own, hidden, part, whole,
):
    length = info[2]
    rows, width = whole.shape
    place_rows(info, block, across_block, arrived, whole)
    frames[...] = whole[...]

    def normalise(at, first, carry):
        mask = mask_col(starts, first, STEP, length)
        unit_rows, _ = norm_unit(masked_rows(whole[at, :], mask, small[0:1, :]))
        branch[at, :] = (unit_rows * small[1:2, :]).astype(BF)
        return carry

    over_rows(rows, normalise)
    ffn_up(branch, (up_o, up_t), hidden, active_own, active_cross)
    ffn_down(active_own, active_cross, (down_o, down_t), part)


def k_attn(
    info, starts, slopes, mine, theirs, frames, small, qkv_o, qkv_t, out_o, out_t,
    stream, branch, context_cross, context_own, qkv, weights, part,
):
    length = info[2]
    rows, width = frames.shape
    arrive(frames)

    def normalise(at, first, carry):
        mask = mask_col(starts, first, STEP, length)
        inputs = masked_rows(frames[at, :], mask, small[0:1, :])
        values = inputs + 0.5 * pair_sum(mine, theirs, at)
        stream[at, :] = values
        unit_rows, _ = norm_unit(values)
        branch[at, :] = (unit_rows * small[2:3, :]).astype(BF)
        return carry

    over_rows(rows, normalise)
    normed = branch[...]
    third = qkv_o.shape[1] // 3
    for shard, weight in enumerate((qkv_o, qkv_t)):
        arrive(weight)
        for index in range(3):
            at = columns(index, third)
            qkv[:, columns(3 * shard + index, third)] = product(normed, weight[:, at]).astype(BF)
    heads = third // DH
    span = rows // 2
    for shard in range(2):
        base = 3 * third * shard
        for head in range(heads):
            place = shard * heads + head
            key = qkv[:, base + third + head * DH : base + third + (head + 1) * DH]
            value = qkv[:, base + 2 * third + head * DH : base + 2 * third + (head + 1) * DH]
            for part_index in range(2):
                at = columns(part_index, span)
                query = qkv[at, base + head * DH : base + (head + 1) * DH]
                scores = times_back(query, key) * DH ** (-0.5)
                key_place = lax.broadcasted_iota(jnp.int32, (span, rows), 1)
                away = key_place - row_iota(part_index * span, span, rows)
                relative = jnp.clip(away, -REACH, REACH).astype(F32) * (1.0 / REACH)
                scores = scores + slopes[place] * relative
                scores = jnp.where(key_place < length, scores, MASKED_SCORE)
                raised = jnp.exp(scores - jnp.max(scores, axis=-1, keepdims=True))
                soft = raised * (1.0 / jnp.sum(raised, axis=-1, keepdims=True))
                weights[place, at, :] = soft
                context = product(soft.astype(BF), value).astype(BF)
                if shard == 0:
                    context_own[at, columns(head, DH)] = context
                else:
                    context_cross[at, columns(head, DH)] = context
    arrive(out_o, out_t)
    own = context_own[...]
    other = context_cross[...]
    for index in range(width // TILE):
        at = columns(index)
        part[:, at] = (product(own, out_o[:, at]) + product(other, out_t[:, at])).astype(BF)


def k_conv_front(
    info, mine, theirs, stream_in, small, params, conv_o, conv_t,
    stream, normed, value, gate, padded, convolved, stats,
):
    length = info[2]
    rows, width = stream_in.shape
    channels = params.shape[1] // 2
    arrive(stream_in)

    def normalise(at, first, carry):
        values = stream_in[at, :] + pair_sum(mine, theirs, at)
        stream[at, :] = values
        unit_rows, _ = norm_unit(values)
        normed[at, :] = (unit_rows * small[3:4, :]).astype(BF)
        return carry

    over_rows(rows, normalise)
    normed_rows = normed[...]
    edge = jnp.zeros((EDGE, 2 * channels), F32)
    padded[:EDGE, :] = edge
    padded[EDGE + rows :, :] = edge
    for shard, weight in enumerate((conv_o, conv_t)):
        arrive(weight)
        at = columns(shard, channels)
        value_rows = product(normed_rows, weight[:, :channels])
        value[:, at] = value_rows
        gate_rows = sigmoid(product(normed_rows, weight[:, channels : 2 * channels]))
        gate[:, at] = gate_rows
        padded[EDGE : EDGE + rows, at] = (
            value_rows * gate_rows * valid_col(0, rows, channels, length)
        )
    count = length.astype(F32)
    for tile in range(2 * channels // DH):
        at = columns(tile, DH)
        total = params[0:1, at] * padded[EDGE - 2 : EDGE - 2 + rows, at]
        for offset in range(1, KW):
            begin = EDGE - 2 + offset
            total = total + params[offset : offset + 1, at] * padded[begin : begin + rows, at]
        convolved[:, at] = total
        keep = valid_col(0, rows, DH, length)
        mean = jnp.sum(total * keep, axis=0, keepdims=True) / count
        centred = (total - mean) * keep
        stats[0:1, at] = jnp.full((1, DH), count, F32)
        stats[1:2, at] = mean
        stats[2:3, at] = jnp.sum(centred * centred, axis=0, keepdims=True)
        stats[3:8, at] = jnp.zeros((5, DH), F32)


def merged(mine, theirs):
    total = mine[0:1, :] + theirs[0:1, :]
    apart = mine[1:2, :] - theirs[1:2, :]
    mean = (mine[0:1, :] * mine[1:2, :] + theirs[0:1, :] * theirs[1:2, :]) / total
    share = mine[0:1, :] * theirs[0:1, :] / total
    spread = mine[2:3, :] + theirs[2:3, :] + apart * apart * share
    return total, mean, spread


def k_merge(mine, theirs, result):
    total, mean, spread = merged(mine, theirs)
    result[0:1, :] = total
    result[1:2, :] = mean
    result[2:3, :] = spread
    result[3:8, :] = jnp.zeros((5, result.shape[1]), F32)


def k_add(mine, theirs, result):
    result[...] = mine[...] + theirs[...]


def shaped_rows(convolved, stats, params, at):
    unit_bn = (convolved[at, :] - stats[1:2, :]) * stats[2:3, :]
    return unit_bn, unit_bn * params[5:6, :] + params[6:7, :]


def k_conv_rear(
    mine, theirs, convolved, params, normed, conv_o, conv_t,
    stats, active_own, active_cross, part,
):
    rows, width = normed.shape
    channels = params.shape[1] // 2
    total, mean, spread = merged(mine, theirs)
    arrive(convolved)
    stats[0:1, :] = total
    stats[1:2, :] = mean
    stats[2:3, :] = lax.rsqrt(spread / total + EPSILON)
    stats[3:8, :] = jnp.zeros((5, stats.shape[1]), F32)

    def activate(at, first, carry):
        _, shaped = shaped_rows(convolved, stats, params, at)
        active = (shaped * sigmoid(shaped)).astype(BF)
        active_own[at, :] = active[:, :channels]
        active_cross[at, :] = active[:, channels:]
        return carry

    over_rows(rows, activate)
    arrive(conv_o, conv_t)
    own = active_own[...]
    other = active_cross[...]
    for index in range(width // TILE):
        at = columns(index)
        part[:, at] = (
            times_back(own, conv_o[at, 2 * channels :])
            + times_back(other, conv_t[at, 2 * channels :])
        ).astype(BF)


def k_ffn_two(
    mine, theirs, stream_in, small, up_o, up_t, down_o, down_t,
    stream, branch, active_cross, active_own, hidden, part,
):
    rows, width = stream_in.shape
    arrive(stream_in)

    def normalise(at, first, carry):
        values = stream_in[at, :] + pair_sum(mine, theirs, at)
        stream[at, :] = values
        unit_rows, _ = norm_unit(values)
        branch[at, :] = (unit_rows * small[4:5, :]).astype(BF)
        return carry

    over_rows(rows, normalise)
    ffn_up(branch, (up_o, up_t), hidden, active_own, active_cross)
    ffn_down(active_own, active_cross, (down_o, down_t), part)


def split_blocks(info, rows, source, own, sent):
    core, high = info[0], info[1]
    own[...] = source[pl.ds((2 * high + core) * rows, rows), :]
    sent[...] = source[pl.ds((2 * high + 1 - core) * rows, rows), :]


def k_ffn_two_back(
    info, mine, theirs, stream, small, block, across_block, arrived, hidden,
    up_o, up_t, down_o, down_t,
    out_own, out_sent, grad_four, gain_sum, branch, grad_cross, grad_own, part, out_rows, grads,
):
    rows, width = stream.shape
    arrive(block, across_block, arrived)
    place_rows(info, block, across_block, arrived, grads)
    arrive(stream)

    def pass_back(at, first, carry):
        values = stream[at, :] + 0.5 * pair_sum(mine, theirs, at)
        unit_rows, inverse = norm_unit(values)
        out_rows[at, :] = (unit_rows * small[5:6, :]).astype(BF)
        grad, fresh = norm_back(grads[at, :].astype(F32), unit_rows, inverse, small[5:6, :])
        grad_four[at, :] = grad
        branch[at, :] = (0.5 * grad).astype(BF)
        return carry + fresh

    gain_sum[...] = over_rows(rows, pass_back, jnp.zeros((1, width), F32))
    split_blocks(info, rows // 4, out_rows, out_own, out_sent)
    ffn_grad_hidden(branch, (down_o, down_t), hidden, grad_own, grad_cross)

    def store(at, values):
        part[:, at] = values.astype(BF)

    ffn_grad_input(grad_own, grad_cross, (up_o, up_t), store)


def k_conv_back_front(
    mine, theirs, stream, small, grad_in, convolved, stats, params, conv_o, conv_t,
    grad_out, gain_sum, branch, grad_shaped, sums,
):
    rows, width = stream.shape
    channels = params.shape[1] // 2
    arrive(stream)

    def pass_back(at, first, carry):
        unit_rows, inverse = norm_unit(stream[at, :])
        grad, fresh = norm_back(pair_sum(mine, theirs, at), unit_rows, inverse, small[4:5, :])
        grad = grad_in[at, :] + grad
        grad_out[at, :] = grad
        branch[at, :] = grad.astype(BF)
        return carry + fresh

    gain_sum[...] = over_rows(rows, pass_back, jnp.zeros((1, width), F32))
    branch_rows = branch[...]
    arrive(convolved)
    for shard, weight in enumerate((conv_o, conv_t)):
        arrive(weight)
        grad_shaped[:, columns(shard, channels)] = product(branch_rows, weight[:, 2 * channels :])

    def slope(at, first, carry):
        unit_bn, shaped = shaped_rows(convolved, stats, params, at)
        grad = grad_shaped[at, :] * silu_slope(shaped)
        grad_shaped[at, :] = grad
        return (
            carry[0] + jnp.sum(grad, axis=0, keepdims=True),
            carry[1] + jnp.sum(grad * unit_bn, axis=0, keepdims=True),
        )

    zero = jnp.zeros((1, 2 * channels), F32)
    shift_sum, scale_sum = over_rows(rows, slope, (zero, zero))
    sums[0:1, :] = shift_sum
    sums[1:2, :] = scale_sum
    sums[2:8, :] = jnp.zeros((6, 2 * channels), F32)


def k_conv_back_rear(
    info, sums_mine, sums_theirs, grad_shaped, convolved, stats, params, padded, value, gate, branch,
    conv_o, conv_t,
    small_sums, mixed_own, mixed_cross, part, grad_padded,
):
    length = info[2]
    rows, width = branch.shape
    channels = params.shape[1] // 2
    sums = sums_mine[0:2, :] + sums_theirs[0:2, :]
    small_sums[5:6, :] = sums[0:1, :]
    small_sums[6:7, :] = sums[1:2, :]
    small_sums[7:8, :] = jnp.zeros((1, 2 * channels), F32)
    edge = jnp.zeros((EDGE, 2 * channels), F32)
    grad_padded[:EDGE, :] = edge
    grad_padded[EDGE + rows :, :] = edge
    arrive(convolved)
    count, bn_inverse, scale_row = stats[0:1, :], stats[2:3, :], params[5:6, :]
    grad_centre = -bn_inverse * scale_row * sums[0:1, :]
    grad_spread = -bn_inverse * bn_inverse * scale_row * sums[1:2, :]

    def spread(at, first, carry):
        centred = convolved[at, :] - stats[1:2, :]
        keep = valid_col(first, STEP, 2 * channels, length)
        grad = grad_shaped[at, :] * scale_row * bn_inverse + keep * (
            grad_centre + grad_spread * centred
        ) * (1.0 / count)
        grad_padded[pl.ds(pl.multiple_of(EDGE + first, EDGE), STEP), :] = grad
        return carry

    over_rows(rows, spread)
    arrive(padded, gate, value)
    for tile in range(2 * channels // DH):
        at = columns(tile, DH)
        grad = grad_padded[EDGE : EDGE + rows, at]
        back = None
        for offset in range(KW):
            begin = EDGE + 2 - offset
            term = params[offset : offset + 1, at] * grad_padded[begin : begin + rows, at]
            back = term if back is None else back + term
            begin = EDGE - 2 + offset
            small_sums[offset : offset + 1, at] = jnp.sum(
                grad * padded[begin : begin + rows, at], axis=0, keepdims=True
            )
        back = back * valid_col(0, rows, DH, length)
        gate_rows = gate[:, at]
        first_grad = (back * gate_rows).astype(BF)
        second_grad = (back * value[:, at] * gate_rows * (1.0 - gate_rows)).astype(BF)
        inner = (tile * DH) % channels
        if tile * DH < channels:
            mixed_own[:, inner : inner + DH] = first_grad
            mixed_own[:, channels + inner : channels + inner + DH] = second_grad
        else:
            mixed_cross[:, inner : inner + DH] = first_grad
            mixed_cross[:, channels + inner : channels + inner + DH] = second_grad
    arrive(conv_o, conv_t)
    own = mixed_own[...]
    other = mixed_cross[...]
    for index in range(width // TILE):
        at = columns(index)
        part[:, at] = (
            times_back(own, conv_o[at, : 2 * channels])
            + times_back(other, conv_t[at, : 2 * channels])
        ).astype(BF)


def k_attn_back(
    mine, theirs, stream, small, grad_in, sums_in, qkv, weights, qkv_o, qkv_t, out_o, out_t,
    grad_out, gain_sum, branch, three_cross, three_own, small_sums, part, grad_context,
):
    rows, width = stream.shape
    arrive(stream)
    third = qkv_o.shape[1] // 3
    heads = third // DH

    def pass_back(at, first, carry):
        unit_rows, inverse = norm_unit(stream[at, :])
        grad, fresh = norm_back(pair_sum(mine, theirs, at), unit_rows, inverse, small[3:4, :])
        grad = grad_in[at, :] + grad
        grad_out[at, :] = grad
        branch[at, :] = grad.astype(BF)
        return carry + fresh

    gain_sum[...] = over_rows(rows, pass_back, jnp.zeros((1, width), F32))
    branch_rows = branch[...]
    for shard, weight in enumerate((out_o, out_t)):
        arrive(weight)
        grad_context[:, columns(shard, third)] = times_back(branch_rows, weight[...]).astype(BF)
    away = lax.broadcasted_iota(jnp.int32, (rows, rows), 1) - row_iota(0, rows, rows)
    relative = jnp.clip(away, -REACH, REACH).astype(F32) * (1.0 / REACH)
    scale = DH ** (-0.5)
    arrive(qkv, weights)
    lanes = small_sums.shape[1]
    lane = lax.broadcasted_iota(jnp.int32, (1, lanes), 1)
    slope_row = jnp.zeros((1, lanes), F32)
    for shard in range(2):
        base = 3 * third * shard
        for head in range(heads):
            place = shard * heads + head
            query = qkv[:, base + head * DH : base + (head + 1) * DH]
            key = qkv[:, base + third + head * DH : base + third + (head + 1) * DH]
            value = qkv[:, base + 2 * third + head * DH : base + 2 * third + (head + 1) * DH]
            grad_head = grad_context[:, place * DH : (place + 1) * DH]
            soft = weights[place]
            grad_soft = times_back(grad_head, value)
            grad_value = inner_rows(soft.astype(BF), grad_head)
            dots = jnp.sum(soft * grad_soft, axis=-1, keepdims=True)
            grad_scores = (soft * (grad_soft - dots)).astype(BF)
            tilted = jnp.sum(grad_scores.astype(F32) * relative, axis=0, keepdims=True)
            slope = jnp.broadcast_to(jnp.sum(tilted, axis=1, keepdims=True), (1, lanes))
            slope_row = jnp.where(lane == shard * (lanes // 2) + head, slope, slope_row)
            grads = (
                product(grad_scores, key) * scale,
                inner_rows(grad_scores, query) * scale,
                grad_value,
            )
            for index, grad in enumerate(grads):
                begin = index * third + head * DH
                if shard == 0:
                    three_own[:, begin : begin + DH] = grad.astype(BF)
                else:
                    three_cross[:, begin : begin + DH] = grad.astype(BF)
    small_sums[:7, :] = sums_in[:7, :]
    small_sums[7:8, :] = slope_row
    arrive(qkv_o, qkv_t)
    own = three_own[...]
    other = three_cross[...]
    for index in range(width // TILE):
        at = columns(index)
        part[:, at] = (times_back(own, qkv_o[at, :]) + times_back(other, qkv_t[at, :])).astype(BF)


def k_ffn_one_back(
    info, mine, theirs, stream, small, grad_in, hidden, up_o, up_t, down_o, down_t,
    grad_out, gain_sum, branch, grad_cross, grad_own, part_own, part_sent, whole,
):
    high = info[1]
    rows, width = stream.shape
    span = rows // 2
    arrive(stream)

    def pass_back(at, first, carry):
        unit_rows, inverse = norm_unit(stream[at, :])
        grad, fresh = norm_back(pair_sum(mine, theirs, at), unit_rows, inverse, small[2:3, :])
        grad = grad_in[at, :] + grad
        grad_out[at, :] = grad
        branch[at, :] = (0.5 * grad).astype(BF)
        return carry + fresh

    gain_sum[...] = over_rows(rows, pass_back, jnp.zeros((1, width), F32))
    ffn_grad_hidden(branch, (down_o, down_t), hidden, grad_own, grad_cross)

    def store(at, values):
        whole[:, at] = values

    ffn_grad_input(grad_own, grad_cross, (up_o, up_t), store)
    part_own[...] = whole[pl.ds(high * span, span), :]
    part_sent[...] = whole[pl.ds((1 - high) * span, span), :].astype(BF)


def k_last(
    info, starts, part_own, arrived, frames, small, grad_in,
    grad_own, grad_sent, sums, grads,
):
    core, high, length = info[0], info[1], info[2]
    span, width = part_own.shape
    arrive(frames)

    def pass_back(at, first, carry):
        begin = pl.multiple_of(high * span + first, STEP)
        mask = mask_col(starts, begin, STEP, length)
        unit_rows, inverse = norm_unit(
            masked_rows(frames[pl.ds(begin, STEP), :], mask, small[0:1, :])
        )
        grad_normed = part_own[at, :] + arrived[at, :].astype(F32)
        grad, fresh = norm_back(grad_normed, unit_rows, inverse, small[1:2, :])
        grad = grad_in[pl.ds(begin, STEP), :] + grad
        hit = jnp.broadcast_to(mask, grad.shape) > 0.5
        grads[at, :] = jnp.where(hit, 0.0, grad)
        masked_part = jnp.sum(jnp.where(hit, grad, 0.0), axis=0, keepdims=True)
        return carry[0] + masked_part, carry[1] + fresh

    zero = jnp.zeros((1, width), F32)
    mask_sum, gain_sum = over_rows(span, pass_back, (zero, zero))
    sums[0:1, :] = mask_sum
    sums[1:2, :] = gain_sum
    rows = span // 2
    grad_own[...] = grads[pl.ds(core * rows, rows), :]
    grad_sent[...] = grads[pl.ds((1 - core) * rows, rows), :]


def k_weights(pairs, bit, tiles, info, *refs):
    count = 1 + max(max(pair[place] for place in (0, 1, 2, 4)) for pair in pairs)
    inputs, kept, sent = refs[:count], refs[count], refs[count + 1 :]
    mine = (info[3] >> bit) & 1
    low = bit - tiles
    rows = kept.shape[1]
    ends = [sum(entry.shape[2] for entry in sent[: place + 1]) for place in range(len(sent))]
    for index in range(kept.shape[0]):
        high_part, low_part = index >> low, index & ((1 << low) - 1)
        for side in range(2):
            tile = (high_part * 2 + (mine ^ side)) * (1 << low) + low_part
            at = pl.ds(pl.multiple_of(tile * rows, rows), rows)
            begin = 0
            for left, left_too, right, shift, right_too, shift_too, size in pairs:
                for piece in range(0, size, TILE):
                    grad = inner_rows(
                        inputs[left][:, at],
                        inputs[right][:, shift + piece : shift + piece + TILE],
                    ) + inner_rows(
                        inputs[left_too][:, at],
                        inputs[right_too][:, shift_too + piece : shift_too + piece + TILE],
                    )
                    place = begin + piece
                    if side == 0:
                        kept[index, :, place : place + TILE] = grad
                        continue
                    for half in range(0, TILE, DH):
                        which = sum(place + half >= end for end in ends)
                        inside = place + half - (ends[which - 1] if which else 0)
                        sent[which][index, :, inside : inside + DH] = grad[
                            :, half : half + DH
                        ].astype(BF)
                begin += size


def k_fold(bit, count, info, held, *refs):
    arrivals, kept, sent = refs[:count], refs[count], refs[count + 1]
    mine = (info[3] >> bit) & 1
    for index in range(held.shape[0]):
        for side in range(2):
            at = pl.ds(mine ^ side, 1)
            begin = 0
            for entry in arrivals:
                spot = slice(begin, begin + entry.shape[3])
                total = held[index, at, :, spot][0] + entry[index, at][0].astype(F32)
                if side == 0:
                    kept[index, :, spot] = total
                else:
                    sent[index, :, spot] = total.astype(BF)
                begin = spot.stop


def k_finish(turned, count, info, kept, *refs):
    arrivals, results = refs[:count], refs[count:]
    cut = arrivals[0].shape[1]
    begin = 0
    for result, turn in zip(results, turned):
        size = result.shape[0] if turn else result.size // result.shape[0]
        for piece in range(begin, begin + size, DH):
            spot = slice(piece, piece + DH)
            at = piece - begin
            inside = slice(piece % cut, piece % cut + DH)
            total = kept[:, spot] + arrivals[piece // cut][:, inside].astype(F32)
            if turn:
                result[at : at + DH, :] = total.T
            elif len(result.shape) == 3:
                result[:, at // result.shape[2], pl.ds(at % result.shape[2], DH)] = total
            else:
                result[:, at : at + DH] = total
        begin += size


def k_in_order(info, own, other, result):
    core = info[0]
    result[pl.ds(core, 1)] = own[...][None]
    result[pl.ds(1 - core, 1)] = other[...][None]


def k_gather(bit, info, held, arrived, result):
    mine = (info[3] >> bit) & 1
    result[:, pl.ds(mine, 1)] = held[...][:, None]
    result[:, pl.ds(1 - mine, 1)] = arrived[...][:, None]


def k_smalls(last, attn, conv, two, final, channel_sums, result):
    width = attn.shape[1]
    result[0:2, :width] = last[...]
    for place, entry in enumerate((attn, conv, two, final), 2):
        result[place : place + 1, :width] = 0.5 * entry[...]
    result[6:8, :width] = jnp.zeros((2, width), F32)
    result[:, width:] = channel_sums[...]


def k_smalls_cross(smalls, result):
    width = smalls.shape[1] - 2 * (smalls.shape[1] - result.shape[1])
    channels = result.shape[1] - width
    result[:, :width] = smalls[:, :width]
    result[:, width:] = smalls[:, width + channels :]


def k_gains(mine, theirs, channel_sums, result):
    width = mine.shape[1]
    result[:, :width] = mine[...] + theirs[...]
    result[:, width:] = channel_sums[...]


def k_smalls_add(smalls, arrived, result):
    size = result.shape[1]
    result[...] = smalls[:, :size] + arrived[...]


def run(kernel, results, arguments, scalars=1, scratch=(), late=(), leaving=(), cost=1):
    given, made = len(arguments), len(results)
    hbm_shapes = [(arguments[place].shape, arguments[place].dtype) for place in late]
    hbm_shapes += [results[place] for place in leaving]
    buffers = [pltpu.VMEM(shape, kind) for shape, kind in hbm_shapes]
    own = [pltpu.VMEM(shape, kind) for shape, kind in scratch]
    hbm = pl.BlockSpec(memory_space=pltpu.HBM)

    def body(*refs):
        ins, outs = list(refs[:given]), list(refs[given : given + made])
        rest = refs[given + made :]
        extra, held, semaphores = rest[: len(own)], rest[len(own) : -1], rest[-1]
        for index, place in enumerate(late):
            ins[place] = Late(ins[place], held[index], semaphores.at[index])
        for index, place in enumerate(leaving, len(late)):
            outs[place] = Leaving(outs[place], held[index], semaphores.at[index])
        kernel(*ins, *outs, *extra)
        arrive(*ins)
        for place in leaving:
            outs[place].finish()

    def plain(*refs):
        kernel(*refs)

    held_bytes = sum(
        functools.reduce(lambda a, b: a * b, shape) * jnp.dtype(kind).itemsize
        for shape, kind in [*scratch, *hbm_shapes]
    )
    specs = [SMEM_SPEC] * scalars + [VMEM_SPEC] * (given - scalars)
    out_specs = [VMEM_SPEC] * made
    for place in late:
        specs[place] = hbm
    for place in leaving:
        out_specs[place] = hbm
    many = len(hbm_shapes)
    return pl.pallas_call(
        body if many else plain,
        out_shape=[
            pltpu.HBM(shape, kind) if place in leaving else pltpu.VMEM(shape, kind)
            for place, (shape, kind) in enumerate(results)
        ],
        in_specs=specs,
        out_specs=out_specs,
        scratch_shapes=own + buffers + ([pltpu.SemaphoreType.DMA((many,))] if many else []),
        compiler_params=pltpu.CompilerParams(vmem_limit_bytes=held_bytes + 8 * MIB),
        cost_estimate=pl.CostEstimate(flops=cost, bytes_accessed=cost, transcendentals=0),
    )(*(
        entry if place < scalars else pltpu.with_memory_space_constraint(
            entry, pltpu.HBM if place in late else pltpu.VMEM
        )
        for place, entry in enumerate(arguments)
    ))


def swap(value, axis, bit):
    size = lax.axis_size(axis)
    return lax.ppermute(value, axis, [(place, place ^ bit) for place in range(size)])


def across(value):
    return swap(value, "tensor", 2)


def beside(value):
    return swap(value, "tensor", 1)


def bit_of(axis, bit):
    return (lax.axis_index(axis) & bit) != 0


def tie(*values):
    return lax.optimization_barrier(values)


class RowSum:
    def __init__(self, info, inputs, pairs, width, first_bits, cuts=(), cost=1):
        size = lax.axis_size("dp")
        levels = size.bit_length() - 1
        tiles = max(levels - 3, 0)
        order = [tiles + bit for bit in first_bits]
        self.order = order + [bit for bit in range(levels - 1, -1, -1) if bit not in order]
        self.left = list(range(levels - 1, -1, -1))
        self.total = sum(pair[-1] for pair in pairs)
        self.block = width // size
        self.info = info
        count = size >> tiles
        shape = (count // 2, width // count)
        self.kept, *self.sent = run(
            functools.partial(k_weights, pairs, self.order[0], tiles),
            [((*shape, self.total), F32)]
            + [((*shape, size), BF) for size in (cuts or (self.total,))],
            [info] + inputs,
            cost=cost,
        )
        self.begin()

    def begin(self):
        self.bit = self.order.pop(0)
        self.left.remove(self.bit)
        self.arrived = []

    def send(self, chain=None):
        piece = self.sent.pop(0)
        if chain is not None:
            (piece,) = chain.after(piece)
        self.arrived.append(swap(piece, "dp", 1 << self.bit))

    def here(self, chain):
        (self.arrived[-1],) = chain.after(self.arrived[-1])

    def fold(self, chain, cost=1):
        bit = self.order[0]
        place = self.left.index(bit)
        inner = self.block << (len(self.left) - 1 - place)
        outer = 1 << place
        kept, *arrived = chain.after(self.kept, *self.arrived)
        self.kept, *self.sent = run(
            functools.partial(k_fold, bit, len(arrived)),
            [((outer, inner, self.total), F32), ((outer, inner, self.total), BF)],
            [self.info, kept.reshape(outer, 2, inner, self.total)]
            + [entry.reshape(outer, 2, inner, -1) for entry in arrived],
            cost=cost,
        )
        self.kept, chain.last = tie(self.kept, chain.last)
        self.begin()

    def step(self, chain, cost=1):
        self.fold(chain, cost=cost)
        self.send()

    def finish(self, chain, *results):
        while self.order:
            self.step(chain)
        shape = (self.block, self.total)
        kept, *arrived = chain.after(
            self.kept.reshape(shape), *(entry.reshape(self.block, -1) for entry in self.arrived)
        )
        sums = run(
            functools.partial(k_finish, tuple(turn for _, turn in results), len(arrived)),
            [(size, F32) for size, _ in results],
            [self.info, kept, *arrived],
        )
        *sums, chain.last = tie(*sums, chain.last)
        return sums


class Chain:
    def __init__(self, last):
        self.last = last

    def after(self, *values):
        *values, self.last = tie(*values, self.last)
        return values


class Gather:
    def __init__(self, info, block):
        self.info, self.held = info, block.reshape(1, *block.shape)
        self.bit = lax.axis_size("dp") // 2
        self.shape = (lax.axis_size("dp") * block.shape[0], block.shape[1])

    def send(self):
        self.arrived = swap(self.held, "dp", self.bit)

    def take(self):
        outer, rows, width = self.held.shape
        (held,) = run(
            functools.partial(k_gather, self.bit.bit_length() - 1),
            [((outer, 2, rows, width), self.held.dtype)],
            [self.info, self.held, self.arrived],
        )
        self.held = held.reshape(outer * 2, rows, width)
        self.bit //= 2

    def whole(self):
        while self.bit:
            self.send()
            self.take()
        return self.held.reshape(self.shape)


def sum_pair(value, axis, merge=None):
    bit, size = 1, lax.axis_size(axis)
    while bit * 2 < size:
        (value,) = run(
            merge or k_add, [(value.shape, F32)], [value, swap(value, axis, bit)], scalars=0
        )
        bit *= 2
    return value, swap(value, axis, bit)


def per_device(
    frames,
    lengths,
    span_starts,
    mask_vector,
    ffn1_gain,
    ffn1_up,
    ffn1_down,
    attn_gain,
    query_weight,
    key_weight,
    value_weight,
    output_weight,
    rel_slope,
    conv_gain,
    conv_up,
    conv_depth,
    bn_scale,
    bn_shift,
    conv_down,
    ffn2_gain,
    ffn2_up,
    ffn2_down,
    final_gain,
    cotangent,
):
    batches, row_count, width = frames.shape
    length = row_count * lax.axis_size("tensor")
    span = 2 * row_count
    channels = conv_depth.shape[1]
    hidden_width = ffn1_up.shape[1]
    heads = rel_slope.shape[0]
    third = query_weight.shape[1]
    core = lax.axis_index("tensor") & 1
    high = (lax.axis_index("tensor") >> 1) & 1
    group = lax.axis_index("dp")
    on_first = core == 0
    own_length = jnp.where(on_first, lengths[0], lengths[1])
    info = jnp.stack([core, high, own_length, group]).astype(jnp.int32)
    starts = jnp.where(on_first, span_starts[0:1], span_starts[1:2])

    frames_across = across(frames)
    conv_block = jnp.concatenate(
        [conv_up.reshape(conv_up.shape[0], 2 * channels), conv_down.T], axis=1
    )
    conv_weights = Gather(info, conv_block)
    conv_weights.send()

    part = mask_vector.shape[0]
    place = (group * lax.axis_size("tensor") + lax.axis_index("tensor")) * part
    vectors = jnp.stack(
        [mask_vector.astype(F32), ffn1_gain, attn_gain, conv_gain, ffn2_gain, final_gain,
         jnp.zeros_like(ffn1_gain), jnp.zeros_like(ffn1_gain)]
    )
    small = lax.dynamic_update_slice(jnp.zeros((8, width), F32), vectors, (0, place))
    hops = [("tensor", 1), ("dp", 2), ("dp", 1), ("tensor", 2)]
    bit = 4
    while bit < lax.axis_size("dp"):
        hops.append(("dp", bit))
        bit *= 2
    for step, (axis, bit) in enumerate(hops):
        if step == 4:
            (sent,) = run(k_pick, [(frames.shape, BF)], [info, frames, frames_across])
            sent, small = tie(sent, small)
        if step == 3:
            query_weight, key_weight, conv_depth, rel_slope, small = tie(
                query_weight, key_weight, conv_depth, rel_slope, small
            )
            own_qkv = jnp.concatenate([query_weight, key_weight, value_weight], axis=1)
            slope_row = jnp.pad(rel_slope[None], ((0, 0), (0, channels - heads)))
            own_params = jnp.concatenate([conv_depth, bn_scale[None], bn_shift[None], slope_row])
            other_params = beside(own_params)
            conv_weights.arrived, small = tie(conv_weights.arrived, small)
            conv_weights.take()
            if conv_weights.bit:
                conv_weights.send()
        if bit < lax.axis_size(axis):
            (small,) = run(
                k_add, [(small.shape, F32)], [small, swap(small, axis, bit)], scalars=0
            )
    if conv_weights.bit:
        conv_weights.arrived, small = tie(conv_weights.arrived, small)
        conv_weights.take()
    frame_parts = [frames, frames_across, beside(sent)]
    own_qkv, other_params, conv_weights.held, small = tie(
        own_qkv, other_params, conv_weights.held, small
    )
    params = jnp.concatenate([own_params, other_params], axis=1)
    slopes = jnp.concatenate([rel_slope, other_params[KW + 2, :heads]])
    if conv_weights.bit:
        conv_weights.send()
    up_one, down_one = beside(ffn1_up), beside(ffn1_down)

    wide = (length, width)
    ffn_outs = [
        (wide, BF),
        ((length, hidden_width), BF),
        ((length, hidden_width), BF),
        ((length, 2 * hidden_width), F32),
        (wide, BF),
    ]
    whole, norm_one, cross_one, active_one, hidden_one, partial = run(
        k_ffn_one,
        [(wide, BF)] + ffn_outs,
        [info, starts, *frame_parts, small, ffn1_up, up_one, ffn1_down, down_one],
        scratch=[(wide, BF)], late=(6, 8),
    )
    output_weight, active_one = tie(output_weight, active_one)
    other_qkv, other_out = beside(own_qkv), beside(output_weight)
    stream_one, norm_attn, context_cross, context_own, qkv, weights, partial = run(
        k_attn_wrapped,
        [
            (wide, F32),
            (wide, BF),
            ((length, third), BF),
            ((length, third), BF),
            ((length, 6 * third), BF),
            ((2 * heads, length, length), F32),
            (wide, BF),
        ],
        [info, slopes, starts, partial, across(partial), whole, small, own_qkv, other_qkv,
         output_weight, other_out],
        scalars=2, late=(7, 9),
    )
    conv_weights.arrived, norm_one, cross_one, context_own = tie(
        conv_weights.arrived, norm_one, cross_one, context_own
    )
    conv_weights.take()
    own_conv = conv_weights.whole()
    other_conv = beside(own_conv)
    norm_one_too, cross_one_too = beside(norm_one), beside(cross_one)
    norm_one_too, cross_one_too, params = tie(norm_one_too, cross_one_too, params)
    both_channels = (length, 2 * channels)
    stat_shape = ((8, 2 * channels), F32)
    stream_two, norm_conv, value, gate, padded, convolved, stats = run(
        k_conv_front,
        [
            (wide, F32),
            (wide, BF),
            (both_channels, F32),
            (both_channels, F32),
            ((length + 2 * EDGE, 2 * channels), F32),
            (both_channels, F32),
            stat_shape,
        ],
        [info, partial, across(partial), stream_one, small, params, own_conv, other_conv],
        late=(6,),
    )
    norm_attn, context_cross, cotangent, ffn2_up, ffn2_down, value = tie(
        norm_attn, context_cross, cotangent, ffn2_up, ffn2_down, value
    )
    stats, stats_too = sum_pair(stats, "dp", k_merge)
    grad_across = across(cotangent)
    up_two, down_two = beside(ffn2_up), beside(ffn2_down)
    norm_attn_too, context_cross_too = beside(norm_attn), beside(context_cross)
    params, grad_across = tie(params, grad_across)
    stats, active_conv, cross_conv, partial = run(
        k_conv_rear,
        [stat_shape, ((length, channels), BF), ((length, channels), BF), (wide, BF)],
        [stats, stats_too, convolved, params, norm_conv, own_conv, other_conv],
        scalars=0, late=(5,),
    )
    grad_across, active_conv = tie(grad_across, active_conv)
    (sent,) = run(k_pick, [(cotangent.shape, BF)], [info, cotangent, grad_across])
    grad_parts = [cotangent, grad_across, beside(sent)]
    grad_parts[2], small = tie(grad_parts[2], small)
    stream_three, norm_two, cross_two, active_two, hidden_two, partial = run(
        k_ffn_two,
        [(wide, F32)] + ffn_outs,
        [partial, across(partial), stream_two, small, ffn2_up, up_two, ffn2_down, down_two],
        scalars=0, late=(4, 6),
    )
    norm_two, cross_two, norm_conv, cross_conv, active_two = tie(
        norm_two, cross_two, norm_conv, cross_conv, active_two
    )
    norm_two_too, cross_two_too = beside(norm_two), beside(cross_two)
    norm_conv_too, cross_conv_too = beside(norm_conv), beside(cross_conv)
    (
        norm_two_too, cross_two_too, norm_conv_too, cross_conv_too, norm_attn_too,
        context_cross_too, small,
    ) = tie(
        norm_two_too, cross_two_too, norm_conv_too, cross_conv_too, norm_attn_too,
        context_cross_too, small,
    )

    row_shape = ((1, width), F32)
    block_shape = (row_count, width)
    out_own, out_sent, grad_four, sum_final, back_two, hid_cross_two, hid_two, partial = run(
        k_ffn_two_back,
        [
            (block_shape, BF),
            (block_shape, BF),
            (wide, F32),
            row_shape,
            (wide, BF),
            ((length, hidden_width), BF),
            ((length, hidden_width), BF),
            (wide, BF),
        ],
        [info, partial, across(partial), stream_three, small, *grad_parts, hidden_two,
         ffn2_up, up_two, ffn2_down, down_two],
        scratch=[(wide, BF), (wide, BF)], late=(9, 11),
    )
    back_two_too, hid_cross_two_too = beside(back_two), beside(hid_cross_two)
    ffn_pair = ((0, 1, 2, 0, 3, 0, hidden_width),)
    two_up = RowSum(
        info, [norm_two, norm_two_too, hid_two, hid_cross_two_too], ffn_pair, width, (0, 1, 2)
    )
    two_down = RowSum(
        info, [back_two, back_two_too, active_two, cross_two_too], ffn_pair, width, (1, 2, 0)
    )
    grad_four, two_up.sent[0], two_down.sent[0] = tie(
        grad_four, two_up.sent[0], two_down.sent[0]
    )
    grad_three, sum_two, back_conv, grad_shaped, sums = run(
        k_conv_back_front,
        [(wide, F32), row_shape, (wide, BF), (both_channels, F32), stat_shape],
        [partial, across(partial), stream_three, small, grad_four, convolved, stats, params,
         own_conv, other_conv],
        scalars=0, late=(8,),
    )
    out_sent, sum_two, back_conv = tie(out_sent, sum_two, back_conv)
    out_other, back_conv_too = beside(out_sent), beside(back_conv)
    bits = [1 << level for level in range(lax.axis_size("dp").bit_length() - 1)]
    for bit in bits[:-1]:
        (sums,) = run(
            k_add, [(sums.shape, F32)], [sums, swap(sums, "dp", bit)], scalars=0
        )
        chain = Chain(sums)
        if bit == 1:
            two_up.send(chain)
        if bit == 2:
            two_down.send(chain)
        sums = chain.last
    sums_too = swap(sums, "dp", bits[-1])
    sums_too, out_other, back_conv_too = tie(sums_too, out_other, back_conv_too)
    small_sums, mixed_own, mixed_cross, partial = run(
        k_conv_back_rear,
        [
            stat_shape,
            ((length, 2 * channels), BF),
            ((length, 2 * channels), BF),
            (wide, BF),
        ],
        [info, sums, sums_too, grad_shaped, convolved, stats, params, padded, value, gate,
         back_conv, own_conv, other_conv],
        scratch=[((length + 2 * EDGE, 2 * channels), F32)], late=(11,),
    )
    mixed_cross_too = beside(mixed_cross)
    mixed_cross_too, grad_three = tie(mixed_cross_too, grad_three)
    grad_two, sum_conv, back_attn, three_cross, three_own, small_sums, partial = run(
        k_attn_back,
        [
            (wide, F32),
            row_shape,
            (wide, BF),
            ((length, 3 * third), BF),
            ((length, 3 * third), BF),
            stat_shape,
            (wide, BF),
        ],
        [partial, across(partial), stream_two, small, grad_three, small_sums, qkv, weights,
         own_qkv, other_qkv, output_weight, other_out],
        scalars=0,
        scratch=[((length, 2 * third), BF)], late=(8, 10),
    )
    back_attn_too, three_cross_too = beside(back_attn), beside(three_cross)
    chain = Chain(small_sums)
    for entry in (two_up, two_down):
        entry.step(chain)
    back_attn, three_own = chain.after(back_attn, three_own)
    small_sums = chain.last
    middle = RowSum(
        info,
        [norm_conv, norm_conv_too, mixed_own, mixed_cross_too,
         back_conv, back_conv_too, active_conv, cross_conv_too,
         norm_attn, norm_attn_too, three_own, three_cross_too,
         back_attn, back_attn_too, context_own, context_cross_too],
        (
            (0, 1, 2, 0, 3, 0, 2 * channels),
            (4, 5, 6, 0, 7, 0, channels),
            (8, 9, 10, 0, 11, 0, 3 * third),
            (12, 13, 14, 0, 15, 0, third),
        ),
        width, (0, 1, 2),
    )
    middle.send()
    middle.kept, grad_two = tie(middle.kept, grad_two)
    grad_one, sum_attn, back_one, hid_cross_one, hid_one, last_own, last_sent = run(
        k_ffn_one_back,
        [
            (wide, F32),
            row_shape,
            (wide, BF),
            ((length, hidden_width), BF),
            ((length, hidden_width), BF),
            ((span, width), F32),
            ((span, width), BF),
        ],
        [info, partial, across(partial), stream_one, small, grad_two, hidden_one,
         ffn1_up, up_one, ffn1_down, down_one],
        scratch=[(wide, F32)], late=(7, 9),
    )
    back_one_too, hid_cross_one_too = beside(back_one), beside(hid_cross_one)
    chain = Chain(sum_attn)
    for entry in (two_up, two_down):
        entry.step(chain, cost=COST)
    hid_one, active_one = chain.after(hid_one, active_one)
    one_up = RowSum(
        info, [norm_one, norm_one_too, hid_one, hid_cross_one_too], ffn_pair, width, (0, 1, 2),
        cost=COST,
    )
    one_down = RowSum(
        info, [back_one, back_one_too, active_one, cross_one_too], ffn_pair, width, (0, 1, 2),
        cost=COST,
    )
    one_up.send(chain)
    one_up.kept, chain.last = tie(one_up.kept, chain.last)
    one_down.send(chain)
    one_down.kept, chain.last = tie(one_down.kept, chain.last)
    block = width // lax.axis_size("dp")
    (starts,) = chain.after(starts)
    sum_attn = chain.last
    frames_own, frames_sent, last_sums = run(
        k_last,
        [(block_shape, F32), (block_shape, F32), ((2, width), F32)],
        [info, starts, last_own, across(last_sent), whole, small, grad_one],
        scratch=[((span, width), F32)],
    )
    frames_other = beside(frames_sent)
    (smalls,) = run(
        k_smalls, [((8, width + 2 * channels), F32)],
        [last_sums, sum_attn, sum_conv, sum_two, sum_final, small_sums], scalars=0,
    )
    (smalls_sent,) = run(k_smalls_cross, [((8, width + channels), F32)], [smalls], scalars=0)
    (smalls,) = run(
        k_smalls_add, [((8, width + channels), F32)], [smalls, beside(smalls_sent)], scalars=0
    )
    gains, gains_too = smalls[:, :width], across(smalls[:, :width])
    (gains,) = run(
        k_gains, [(smalls.shape, F32)], [gains, gains_too, smalls[:, width:]], scalars=0
    )

    def in_order(own, other):
        return run(k_in_order, [((2, *own.shape), own.dtype)], [info, own, other])[0]

    chain = Chain(in_order(out_own, out_other))

    def hop(value, bit):
        (value,) = chain.after(value)
        return value, swap(value, "dp", bit)

    def add(value, other):
        (total,) = run(k_add, [(value.shape, F32)], chain.after(value, other), scalars=0)
        return total

    first, *between = [1 << level for level in range(1, lax.axis_size("dp").bit_length() - 1)]
    gains = add(*hop(gains, first))
    gains, chain.last = tie(gains, chain.last)
    (two_up,) = two_up.finish(chain, ((block, hidden_width), False))
    middle.step(chain)
    for bit in between:
        gains = add(*hop(gains, bit))
    gains, chain.last = tie(gains, chain.last)
    middle.step(chain)
    one_up.step(chain)
    one_down.step(chain)
    one_up.step(chain)
    conv_up_grad, conv_down_grad, query_grad, key_grad, value_grad, output_grad = middle.finish(
        chain,
        (conv_up.shape, False), ((channels, block), True),
        *[((block, third), False)] * 3, ((third, block), True),
    )
    gains, gains_too = hop(gains, 1)
    (one_up,) = one_up.finish(chain, ((block, hidden_width), False))
    gains = add(gains, gains_too)
    one_down.step(chain)
    (two_down,) = two_down.finish(chain, ((hidden_width, block), True))
    channel_sums = gains[:, width:]
    scale_grad = channel_sums[KW + 1] * (1.0 / lax.axis_size("dp"))
    shift_grad = channel_sums[KW] * (1.0 / lax.axis_size("dp"))
    gains = lax.dynamic_slice_in_dim(gains, place, part, axis=1)

    frames_grad = in_order(frames_own, frames_other)
    smallest = [
        *(gains[index] for index in range(6)),
        channel_sums[KW + 2, :heads],
        channel_sums[:KW],
        scale_grad,
        shift_grad,
    ]
    frames_grad, *smallest = chain.after(frames_grad, *smallest)
    (one_down,) = one_down.finish(chain, ((hidden_width, block), True))

    return (
        chain.last,
        frames_grad,
        smallest[0],
        smallest[1],
        one_up,
        one_down,
        smallest[2],
        query_grad,
        key_grad,
        value_grad,
        output_grad,
        smallest[6],
        smallest[3],
        conv_up_grad,
        smallest[7],
        smallest[8],
        smallest[9],
        conv_down_grad,
        smallest[4],
        two_up,
        two_down,
        smallest[5],
    )


def k_attn_wrapped(info, slopes, starts, *refs):
    k_attn(info, starts, slopes, *refs)


def solution(mesh):
    every, split, by_column = P(("dp", "tensor")), P("tensor"), P(None, "tensor")
    rows_by = P("dp", "tensor", None)
    return jax.shard_map(
        per_device,
        mesh=mesh,
        in_specs=(
            rows_by,
            P("dp"),
            P("dp", None),
            every,
            every,
            by_column,
            P("tensor", None),
            every,
            by_column,
            by_column,
            by_column,
            P("tensor", None),
            split,
            every,
            P("dp", None, "tensor"),
            by_column,
            split,
            split,
            P("tensor", "dp"),
            every,
            by_column,
            P("tensor", None),
            every,
            rows_by,
        ),
        out_specs=(
            rows_by,
            rows_by,
            every,
            every,
            P("dp", "tensor"),
            P("tensor", "dp"),
            every,
            P("dp", "tensor"),
            P("dp", "tensor"),
            P("dp", "tensor"),
            P("tensor", "dp"),
            split,
            every,
            P("dp", None, "tensor"),
            by_column,
            split,
            split,
            P("tensor", "dp"),
            every,
            P("dp", "tensor"),
            P("tensor", "dp"),
            every,
        ),
        check_vma=False,
    )
```

```python
import functools

import jax
import jax.numpy as jnp
from jax import lax
from jax.experimental import pallas as pl
from jax.experimental.pallas import tpu as pltpu
from jax.sharding import PartitionSpec as P

DH = 128
KW = 5
SPAN = 10
REACH = 128
EPSILON = 1e-05
MASKED_SCORE = -1000000000.0
BF = jnp.bfloat16
F32 = jnp.float32
STEP = 32
TILE = 256
EDGE = 8
MIB = 1024 * 1024
COST = 30_000_000

VMEM_SPEC = pl.BlockSpec(memory_space=pltpu.VMEM)
SMEM_SPEC = pl.BlockSpec(memory_space=pltpu.SMEM)


def product(left, right):
    return jnp.dot(left, right, preferred_element_type=F32)


def inner_rows(left, right):
    return lax.dot_general(left, right, (((0,), (0,)), ((), ())), preferred_element_type=F32)


def times_back(left, right):
    return lax.dot_general(left, right, (((1,), (1,)), ((), ())), preferred_element_type=F32)


def sigmoid(values):
    return 0.5 * jnp.tanh(0.5 * values) + 0.5


def norm_unit(values):
    centre = jnp.mean(values, axis=-1, keepdims=True)
    centred = values - centre
    inverse = lax.rsqrt(jnp.mean(centred * centred, axis=-1, keepdims=True) + EPSILON)
    return centred * inverse, inverse


def norm_back(grad_out, unit_rows, inverse, norm_gain):
    grad_unit = grad_out * norm_gain
    first_mean = jnp.mean(grad_unit, axis=-1, keepdims=True)
    second_mean = jnp.mean(grad_unit * unit_rows, axis=-1, keepdims=True)
    return (
        inverse * (grad_unit - first_mean - unit_rows * second_mean),
        jnp.sum(grad_out * unit_rows, axis=0, keepdims=True),
    )


def silu_slope(values):
    gate_value = sigmoid(values)
    return gate_value * (1.0 + values * (1.0 - gate_value))


def over_rows(count, body, init=0, step=STEP):
    def one(index, carry):
        return body(pl.ds(pl.multiple_of(index * step, step), step), index * step, carry)

    return lax.fori_loop(0, count // step, one, init, unroll=4)


def row_iota(first, rows, columns):
    return first + lax.broadcasted_iota(jnp.int32, (rows, columns), 0)


def mask_col(starts_ref, first, rows, length):
    starts = starts_ref[...]
    at = row_iota(first, rows, starts.shape[1])
    hit = (starts <= at) & (at < starts + SPAN) & (at < length)
    return jnp.max(jnp.where(hit, 1.0, 0.0), axis=1, keepdims=True)


def valid_col(first, rows, columns, length):
    return jnp.where(row_iota(first, rows, columns) < length, 1.0, 0.0)


def masked_rows(frame_rows, mask, mask_row):
    return jnp.where(
        jnp.broadcast_to(mask, frame_rows.shape) > 0.5, mask_row, frame_rows.astype(F32)
    )


def pair_sum(mine, theirs, rows):
    return mine[rows, :].astype(F32) + theirs[rows, :].astype(F32)


class Late:
    def __init__(self, source, held, semaphore):
        self.copy = pltpu.make_async_copy(source, held, semaphore)
        self.copy.start()
        self.held, self.shape, self.dtype, self.waited = held, held.shape, held.dtype, False

    def arrive(self):
        if not self.waited:
            self.copy.wait()
            self.waited = True

    def __getitem__(self, index):
        assert self.waited
        return self.held[index]


class Leaving:
    def __init__(self, target, held, semaphore):
        self.copy = pltpu.make_async_copy(held, target, semaphore)
        self.held, self.shape, self.dtype, self.started = held, held.shape, held.dtype, False

    def leave(self):
        if not self.started:
            self.copy.start()
            self.started = True

    def finish(self):
        self.leave()
        self.copy.wait()

    def __getitem__(self, index):
        return self.held[index]

    def __setitem__(self, index, value):
        assert not self.started
        self.held[index] = value


def arrive(*refs):
    for ref in refs:
        if isinstance(ref, Late):
            ref.arrive()


def leave(*refs):
    for ref in refs:
        if isinstance(ref, Leaving):
            ref.leave()


def columns(index, size=TILE):
    return slice(index * size, (index + 1) * size)


def ffn_up(branch, ups, hidden, active_own, active_cross):
    normed = branch[...]
    for shard, weight in enumerate(ups):
        arrive(weight)
        tiles = weight.shape[1] // TILE
        for index in range(tiles):
            at = columns(index)
            values = product(normed, weight[:, at])
            hidden[:, columns(index + shard * tiles)] = values
            (active_own, active_cross)[shard][:, at] = (values * sigmoid(values)).astype(BF)


def ffn_down(active_own, active_cross, downs, part):
    width = downs[0].shape[1]
    own, cross = active_own[...], active_cross[...]
    arrive(*downs)
    for index in range(width // TILE):
        at = columns(index)
        part[:, at] = (product(own, downs[0][:, at]) + product(cross, downs[1][:, at])).astype(BF)


def ffn_grad_hidden(branch, downs, hidden, grad_own, grad_cross):
    grad_branch = branch[...]
    for shard, weight in enumerate(downs):
        arrive(weight)
        tiles = weight.shape[0] // TILE
        for index in range(tiles):
            at = columns(index)
            slope = silu_slope(hidden[:, columns(index + shard * tiles)])
            grad = (times_back(grad_branch, weight[at, :]) * slope).astype(BF)
            (grad_own, grad_cross)[shard][:, at] = grad


def ffn_grad_input(grad_own, grad_cross, ups, store):
    own, cross = grad_own[...], grad_cross[...]
    arrive(*ups)
    for index in range(ups[0].shape[0] // TILE):
        at = columns(index)
        store(at, times_back(own, ups[0][at, :]) + times_back(cross, ups[1][at, :]))


def k_pick(info, block, across_block, sent):
    core = info[0]
    sent[0] = block[pl.ds(1 - core, 1)][0]
    sent[1] = across_block[pl.ds(1 - core, 1)][0]


def place_rows(info, block, across_block, arrived, whole):
    core, high = info[0], info[1]
    rows = block.shape[1]
    places = (
        (2 * high + core, block[pl.ds(core, 1)][0]),
        (2 * (1 - high) + core, across_block[pl.ds(core, 1)][0]),
        (2 * high + 1 - core, arrived[0]),
        (2 * (1 - high) + 1 - core, arrived[1]),
    )
    for place, value in places:
        whole[pl.ds(pl.multiple_of(place * rows, rows), rows), :] = value


def k_ffn_one(
    info, starts, block, across_block, arrived, small, up_o, up_t, down_o, down_t,
    frames, branch, active_cross, active_own, hidden, part, whole,
):
    length = info[2]
    rows, width = whole.shape
    place_rows(info, block, across_block, arrived, whole)
    frames[...] = whole[...]

    def normalise(at, first, carry):
        mask = mask_col(starts, first, STEP, length)
        unit_rows, _ = norm_unit(masked_rows(whole[at, :], mask, small[0:1, :]))
        branch[at, :] = (unit_rows * small[1:2, :]).astype(BF)
        return carry

    over_rows(rows, normalise)
    ffn_up(branch, (up_o, up_t), hidden, active_own, active_cross)
    ffn_down(active_own, active_cross, (down_o, down_t), part)


def k_attn(
    info, starts, slopes, mine, theirs, frames, small, qkv_o, qkv_t, out_o, out_t,
    stream, branch, context_cross, context_own, qkv, weights, part,
):
    length = info[2]
    rows, width = frames.shape
    arrive(frames)

    def normalise(at, first, carry):
        mask = mask_col(starts, first, STEP, length)
        inputs = masked_rows(frames[at, :], mask, small[0:1, :])
        values = inputs + 0.5 * pair_sum(mine, theirs, at)
        stream[at, :] = values
        unit_rows, _ = norm_unit(values)
        branch[at, :] = (unit_rows * small[2:3, :]).astype(BF)
        return carry

    over_rows(rows, normalise)
    normed = branch[...]
    third = qkv_o.shape[1] // 3
    for shard, weight in enumerate((qkv_o, qkv_t)):
        arrive(weight)
        for index in range(3):
            at = columns(index, third)
            qkv[:, columns(3 * shard + index, third)] = product(normed, weight[:, at]).astype(BF)
    heads = third // DH
    span = rows // 2
    for shard in range(2):
        base = 3 * third * shard
        for head in range(heads):
            place = shard * heads + head
            key = qkv[:, base + third + head * DH : base + third + (head + 1) * DH]
            value = qkv[:, base + 2 * third + head * DH : base + 2 * third + (head + 1) * DH]
            for part_index in range(2):
                at = columns(part_index, span)
                query = qkv[at, base + head * DH : base + (head + 1) * DH]
                scores = times_back(query, key) * DH ** (-0.5)
                key_place = lax.broadcasted_iota(jnp.int32, (span, rows), 1)
                away = key_place - row_iota(part_index * span, span, rows)
                relative = jnp.clip(away, -REACH, REACH).astype(F32) * (1.0 / REACH)
                scores = scores + slopes[place] * relative
                scores = jnp.where(key_place < length, scores, MASKED_SCORE)
                raised = jnp.exp(scores - jnp.max(scores, axis=-1, keepdims=True))
                soft = raised * (1.0 / jnp.sum(raised, axis=-1, keepdims=True))
                weights[place, at, :] = soft
                context = product(soft.astype(BF), value).astype(BF)
                if shard == 0:
                    context_own[at, columns(head, DH)] = context
                else:
                    context_cross[at, columns(head, DH)] = context
    arrive(out_o, out_t)
    own = context_own[...]
    other = context_cross[...]
    for index in range(width // TILE):
        at = columns(index)
        part[:, at] = (product(own, out_o[:, at]) + product(other, out_t[:, at])).astype(BF)


def k_conv_front(
    info, mine, theirs, stream_in, small, params, conv_o, conv_t,
    stream, normed, value, gate, padded, convolved, stats,
):
    length = info[2]
    rows, width = stream_in.shape
    channels = params.shape[1] // 2
    arrive(stream_in)

    def normalise(at, first, carry):
        values = stream_in[at, :] + pair_sum(mine, theirs, at)
        stream[at, :] = values
        unit_rows, _ = norm_unit(values)
        normed[at, :] = (unit_rows * small[3:4, :]).astype(BF)
        return carry

    over_rows(rows, normalise)
    normed_rows = normed[...]
    edge = jnp.zeros((EDGE, 2 * channels), F32)
    padded[:EDGE, :] = edge
    padded[EDGE + rows :, :] = edge
    for shard, weight in enumerate((conv_o, conv_t)):
        arrive(weight)
        at = columns(shard, channels)
        value_rows = product(normed_rows, weight[:, :channels])
        value[:, at] = value_rows
        gate_rows = sigmoid(product(normed_rows, weight[:, channels : 2 * channels]))
        gate[:, at] = gate_rows
        padded[EDGE : EDGE + rows, at] = (
            value_rows * gate_rows * valid_col(0, rows, channels, length)
        )
    count = length.astype(F32)
    for tile in range(2 * channels // DH):
        at = columns(tile, DH)
        total = params[0:1, at] * padded[EDGE - 2 : EDGE - 2 + rows, at]
        for offset in range(1, KW):
            begin = EDGE - 2 + offset
            total = total + params[offset : offset + 1, at] * padded[begin : begin + rows, at]
        convolved[:, at] = total
        keep = valid_col(0, rows, DH, length)
        mean = jnp.sum(total * keep, axis=0, keepdims=True) / count
        centred = (total - mean) * keep
        stats[0:1, at] = jnp.full((1, DH), count, F32)
        stats[1:2, at] = mean
        stats[2:3, at] = jnp.sum(centred * centred, axis=0, keepdims=True)
        stats[3:8, at] = jnp.zeros((5, DH), F32)


def merged(mine, theirs):
    total = mine[0:1, :] + theirs[0:1, :]
    apart = mine[1:2, :] - theirs[1:2, :]
    mean = (mine[0:1, :] * mine[1:2, :] + theirs[0:1, :] * theirs[1:2, :]) / total
    share = mine[0:1, :] * theirs[0:1, :] / total
    spread = mine[2:3, :] + theirs[2:3, :] + apart * apart * share
    return total, mean, spread


def k_merge(mine, theirs, result):
    total, mean, spread = merged(mine, theirs)
    result[0:1, :] = total
    result[1:2, :] = mean
    result[2:3, :] = spread
    result[3:8, :] = jnp.zeros((5, result.shape[1]), F32)


def k_add(mine, theirs, result):
    result[...] = mine[...] + theirs[...]


def shaped_rows(convolved, stats, params, at):
    unit_bn = (convolved[at, :] - stats[1:2, :]) * stats[2:3, :]
    return unit_bn, unit_bn * params[5:6, :] + params[6:7, :]


def k_conv_rear(
    mine, theirs, convolved, params, normed, conv_o, conv_t,
    stats, active_own, active_cross, part,
):
    rows, width = normed.shape
    channels = params.shape[1] // 2
    total, mean, spread = merged(mine, theirs)
    arrive(convolved)
    stats[0:1, :] = total
    stats[1:2, :] = mean
    stats[2:3, :] = lax.rsqrt(spread / total + EPSILON)
    stats[3:8, :] = jnp.zeros((5, stats.shape[1]), F32)

    def activate(at, first, carry):
        _, shaped = shaped_rows(convolved, stats, params, at)
        active = (shaped * sigmoid(shaped)).astype(BF)
        active_own[at, :] = active[:, :channels]
        active_cross[at, :] = active[:, channels:]
        return carry

    over_rows(rows, activate)
    arrive(conv_o, conv_t)
    own = active_own[...]
    other = active_cross[...]
    for index in range(width // TILE):
        at = columns(index)
        part[:, at] = (
            times_back(own, conv_o[at, 2 * channels :])
            + times_back(other, conv_t[at, 2 * channels :])
        ).astype(BF)


def k_ffn_two(
    mine, theirs, stream_in, small, up_o, up_t, down_o, down_t,
    stream, branch, active_cross, active_own, hidden, part,
):
    rows, width = stream_in.shape
    arrive(stream_in)

    def normalise(at, first, carry):
        values = stream_in[at, :] + pair_sum(mine, theirs, at)
        stream[at, :] = values
        unit_rows, _ = norm_unit(values)
        branch[at, :] = (unit_rows * small[4:5, :]).astype(BF)
        return carry

    over_rows(rows, normalise)
    ffn_up(branch, (up_o, up_t), hidden, active_own, active_cross)
    ffn_down(active_own, active_cross, (down_o, down_t), part)


def split_blocks(info, rows, source, own, sent):
    core, high = info[0], info[1]
    own[...] = source[pl.ds((2 * high + core) * rows, rows), :]
    sent[...] = source[pl.ds((2 * high + 1 - core) * rows, rows), :]


def k_ffn_two_back(
    info, mine, theirs, stream, small, block, across_block, arrived, hidden,
    up_o, up_t, down_o, down_t,
    out_own, out_sent, grad_four, gain_sum, branch, grad_cross, grad_own, part, out_rows, grads,
):
    rows, width = stream.shape
    arrive(block, across_block, arrived)
    place_rows(info, block, across_block, arrived, grads)
    arrive(stream)

    def pass_back(at, first, carry):
        values = stream[at, :] + 0.5 * pair_sum(mine, theirs, at)
        unit_rows, inverse = norm_unit(values)
        out_rows[at, :] = (unit_rows * small[5:6, :]).astype(BF)
        grad, fresh = norm_back(grads[at, :].astype(F32), unit_rows, inverse, small[5:6, :])
        grad_four[at, :] = grad
        branch[at, :] = (0.5 * grad).astype(BF)
        return carry + fresh

    gain_sum[...] = over_rows(rows, pass_back, jnp.zeros((1, width), F32))
    split_blocks(info, rows // 4, out_rows, out_own, out_sent)
    ffn_grad_hidden(branch, (down_o, down_t), hidden, grad_own, grad_cross)

    def store(at, values):
        part[:, at] = values.astype(BF)

    ffn_grad_input(grad_own, grad_cross, (up_o, up_t), store)


def k_conv_back_front(
    mine, theirs, stream, small, grad_in, convolved, stats, params, conv_o, conv_t,
    grad_out, gain_sum, branch, grad_shaped, sums,
):
    rows, width = stream.shape
    channels = params.shape[1] // 2
    arrive(stream)

    def pass_back(at, first, carry):
        unit_rows, inverse = norm_unit(stream[at, :])
        grad, fresh = norm_back(pair_sum(mine, theirs, at), unit_rows, inverse, small[4:5, :])
        grad = grad_in[at, :] + grad
        grad_out[at, :] = grad
        branch[at, :] = grad.astype(BF)
        return carry + fresh

    gain_sum[...] = over_rows(rows, pass_back, jnp.zeros((1, width), F32))
    branch_rows = branch[...]
    arrive(convolved)
    for shard, weight in enumerate((conv_o, conv_t)):
        arrive(weight)
        grad_shaped[:, columns(shard, channels)] = product(branch_rows, weight[:, 2 * channels :])

    def slope(at, first, carry):
        unit_bn, shaped = shaped_rows(convolved, stats, params, at)
        grad = grad_shaped[at, :] * silu_slope(shaped)
        grad_shaped[at, :] = grad
        return (
            carry[0] + jnp.sum(grad, axis=0, keepdims=True),
            carry[1] + jnp.sum(grad * unit_bn, axis=0, keepdims=True),
        )

    zero = jnp.zeros((1, 2 * channels), F32)
    shift_sum, scale_sum = over_rows(rows, slope, (zero, zero))
    sums[0:1, :] = shift_sum
    sums[1:2, :] = scale_sum
    sums[2:8, :] = jnp.zeros((6, 2 * channels), F32)


def k_conv_back_rear(
    info, sums_mine, sums_theirs, grad_shaped, convolved, stats, params, padded, value, gate, branch,
    conv_o, conv_t,
    small_sums, mixed_own, mixed_cross, part, grad_padded,
):
    length = info[2]
    rows, width = branch.shape
    channels = params.shape[1] // 2
    sums = sums_mine[0:2, :] + sums_theirs[0:2, :]
    small_sums[5:6, :] = sums[0:1, :]
    small_sums[6:7, :] = sums[1:2, :]
    small_sums[7:8, :] = jnp.zeros((1, 2 * channels), F32)
    edge = jnp.zeros((EDGE, 2 * channels), F32)
    grad_padded[:EDGE, :] = edge
    grad_padded[EDGE + rows :, :] = edge
    arrive(convolved)
    count, bn_inverse, scale_row = stats[0:1, :], stats[2:3, :], params[5:6, :]
    grad_centre = -bn_inverse * scale_row * sums[0:1, :]
    grad_spread = -bn_inverse * bn_inverse * scale_row * sums[1:2, :]

    def spread(at, first, carry):
        centred = convolved[at, :] - stats[1:2, :]
        keep = valid_col(first, STEP, 2 * channels, length)
        grad = grad_shaped[at, :] * scale_row * bn_inverse + keep * (
            grad_centre + grad_spread * centred
        ) * (1.0 / count)
        grad_padded[pl.ds(pl.multiple_of(EDGE + first, EDGE), STEP), :] = grad
        return carry

    over_rows(rows, spread)
    arrive(padded, gate, value)
    for tile in range(2 * channels // DH):
        at = columns(tile, DH)
        grad = grad_padded[EDGE : EDGE + rows, at]
        back = None
        for offset in range(KW):
            begin = EDGE + 2 - offset
            term = params[offset : offset + 1, at] * grad_padded[begin : begin + rows, at]
            back = term if back is None else back + term
            begin = EDGE - 2 + offset
            small_sums[offset : offset + 1, at] = jnp.sum(
                grad * padded[begin : begin + rows, at], axis=0, keepdims=True
            )
        back = back * valid_col(0, rows, DH, length)
        gate_rows = gate[:, at]
        first_grad = (back * gate_rows).astype(BF)
        second_grad = (back * value[:, at] * gate_rows * (1.0 - gate_rows)).astype(BF)
        inner = (tile * DH) % channels
        if tile * DH < channels:
            mixed_own[:, inner : inner + DH] = first_grad
            mixed_own[:, channels + inner : channels + inner + DH] = second_grad
        else:
            mixed_cross[:, inner : inner + DH] = first_grad
            mixed_cross[:, channels + inner : channels + inner + DH] = second_grad
    arrive(conv_o, conv_t)
    own = mixed_own[...]
    other = mixed_cross[...]
    for index in range(width // TILE):
        at = columns(index)
        part[:, at] = (
            times_back(own, conv_o[at, : 2 * channels])
            + times_back(other, conv_t[at, : 2 * channels])
        ).astype(BF)


def k_attn_back(
    mine, theirs, stream, small, grad_in, sums_in, qkv, weights, qkv_o, qkv_t, out_o, out_t,
    grad_out, gain_sum, branch, three_cross, three_own, small_sums, part, grad_context,
):
    rows, width = stream.shape
    arrive(stream)
    third = qkv_o.shape[1] // 3
    heads = third // DH

    def pass_back(at, first, carry):
        unit_rows, inverse = norm_unit(stream[at, :])
        grad, fresh = norm_back(pair_sum(mine, theirs, at), unit_rows, inverse, small[3:4, :])
        grad = grad_in[at, :] + grad
        grad_out[at, :] = grad
        branch[at, :] = grad.astype(BF)
        return carry + fresh

    gain_sum[...] = over_rows(rows, pass_back, jnp.zeros((1, width), F32))
    branch_rows = branch[...]
    for shard, weight in enumerate((out_o, out_t)):
        arrive(weight)
        grad_context[:, columns(shard, third)] = times_back(branch_rows, weight[...]).astype(BF)
    away = lax.broadcasted_iota(jnp.int32, (rows, rows), 1) - row_iota(0, rows, rows)
    relative = jnp.clip(away, -REACH, REACH).astype(F32) * (1.0 / REACH)
    scale = DH ** (-0.5)
    arrive(qkv, weights)
    lanes = small_sums.shape[1]
    lane = lax.broadcasted_iota(jnp.int32, (1, lanes), 1)
    slope_row = jnp.zeros((1, lanes), F32)
    for shard in range(2):
        base = 3 * third * shard
        for head in range(heads):
            place = shard * heads + head
            query = qkv[:, base + head * DH : base + (head + 1) * DH]
            key = qkv[:, base + third + head * DH : base + third + (head + 1) * DH]
            value = qkv[:, base + 2 * third + head * DH : base + 2 * third + (head + 1) * DH]
            grad_head = grad_context[:, place * DH : (place + 1) * DH]
            soft = weights[place]
            grad_soft = times_back(grad_head, value)
            grad_value = inner_rows(soft.astype(BF), grad_head)
            dots = jnp.sum(soft * grad_soft, axis=-1, keepdims=True)
            grad_scores = (soft * (grad_soft - dots)).astype(BF)
            tilted = jnp.sum(grad_scores.astype(F32) * relative, axis=0, keepdims=True)
            slope = jnp.broadcast_to(jnp.sum(tilted, axis=1, keepdims=True), (1, lanes))
            slope_row = jnp.where(lane == shard * (lanes // 2) + head, slope, slope_row)
            grads = (
                product(grad_scores, key) * scale,
                inner_rows(grad_scores, query) * scale,
                grad_value,
            )
            for index, grad in enumerate(grads):
                begin = index * third + head * DH
                if shard == 0:
                    three_own[:, begin : begin + DH] = grad.astype(BF)
                else:
                    three_cross[:, begin : begin + DH] = grad.astype(BF)
    small_sums[:7, :] = sums_in[:7, :]
    small_sums[7:8, :] = slope_row
    arrive(qkv_o, qkv_t)
    own = three_own[...]
    other = three_cross[...]
    for index in range(width // TILE):
        at = columns(index)
        part[:, at] = (times_back(own, qkv_o[at, :]) + times_back(other, qkv_t[at, :])).astype(BF)


def k_ffn_one_back(
    info, mine, theirs, stream, small, grad_in, hidden, up_o, up_t, down_o, down_t,
    grad_out, gain_sum, branch, grad_cross, grad_own, part_own, part_sent, whole,
):
    high = info[1]
    rows, width = stream.shape
    span = rows // 2
    arrive(stream)

    def pass_back(at, first, carry):
        unit_rows, inverse = norm_unit(stream[at, :])
        grad, fresh = norm_back(pair_sum(mine, theirs, at), unit_rows, inverse, small[2:3, :])
        grad = grad_in[at, :] + grad
        grad_out[at, :] = grad
        branch[at, :] = (0.5 * grad).astype(BF)
        return carry + fresh

    gain_sum[...] = over_rows(rows, pass_back, jnp.zeros((1, width), F32))
    ffn_grad_hidden(branch, (down_o, down_t), hidden, grad_own, grad_cross)

    def store(at, values):
        whole[:, at] = values

    ffn_grad_input(grad_own, grad_cross, (up_o, up_t), store)
    part_own[...] = whole[pl.ds(high * span, span), :]
    part_sent[...] = whole[pl.ds((1 - high) * span, span), :].astype(BF)


def k_last(
    info, starts, part_own, arrived, frames, small, grad_in,
    grad_own, grad_sent, sums, grads,
):
    core, high, length = info[0], info[1], info[2]
    span, width = part_own.shape
    arrive(frames)

    def pass_back(at, first, carry):
        begin = pl.multiple_of(high * span + first, STEP)
        mask = mask_col(starts, begin, STEP, length)
        unit_rows, inverse = norm_unit(
            masked_rows(frames[pl.ds(begin, STEP), :], mask, small[0:1, :])
        )
        grad_normed = part_own[at, :] + arrived[at, :].astype(F32)
        grad, fresh = norm_back(grad_normed, unit_rows, inverse, small[1:2, :])
        grad = grad_in[pl.ds(begin, STEP), :] + grad
        hit = jnp.broadcast_to(mask, grad.shape) > 0.5
        grads[at, :] = jnp.where(hit, 0.0, grad)
        masked_part = jnp.sum(jnp.where(hit, grad, 0.0), axis=0, keepdims=True)
        return carry[0] + masked_part, carry[1] + fresh

    zero = jnp.zeros((1, width), F32)
    mask_sum, gain_sum = over_rows(span, pass_back, (zero, zero))
    sums[0:1, :] = mask_sum
    sums[1:2, :] = gain_sum
    rows = span // 2
    grad_own[...] = grads[pl.ds(core * rows, rows), :]
    grad_sent[...] = grads[pl.ds((1 - core) * rows, rows), :]


def k_weights(pairs, bit, tiles, info, *refs):
    count = 1 + max(max(pair[place] for place in (0, 1, 2, 4)) for pair in pairs)
    inputs, kept, sent = refs[:count], refs[count], refs[count + 1]
    mine = (info[3] >> bit) & 1
    low = bit - tiles
    rows = kept.shape[1]

    def one(index, carry):
        for side in range(2):
            tile = ((index >> low) * 2 + (mine ^ side)) * (1 << low) + (index & ((1 << low) - 1))
            at = pl.ds(pl.multiple_of(tile * rows, rows), rows)
            begin = 0
            for left, left_too, right, shift, right_too, shift_too, size in pairs:
                for piece in range(0, size, TILE):
                    grad = inner_rows(
                        inputs[left][:, at],
                        inputs[right][:, shift + piece : shift + piece + TILE],
                    ) + inner_rows(
                        inputs[left_too][:, at],
                        inputs[right_too][:, shift_too + piece : shift_too + piece + TILE],
                    )
                    spot = slice(begin + piece, begin + piece + TILE)
                    if side == 0:
                        kept[index, :, spot] = grad
                    else:
                        sent[index, :, spot] = grad.astype(BF)
                begin += size
        return carry

    lax.fori_loop(0, kept.shape[0], one, 0, unroll=2)


def k_fold(bit, count, info, held, *refs):
    arrivals, kept, sent = refs[:count], refs[count], refs[count + 1]
    mine = (info[3] >> bit) & 1
    for index in range(held.shape[0]):
        for side in range(2):
            at = pl.ds(mine ^ side, 1)
            begin = 0
            for entry in arrivals:
                spot = slice(begin, begin + entry.shape[3])
                total = held[index, at, :, spot][0] + entry[index, at][0].astype(F32)
                if side == 0:
                    kept[index, :, spot] = total
                else:
                    sent[index, :, spot] = total.astype(BF)
                begin = spot.stop


def k_finish(turned, count, info, kept, *refs):
    arrivals, results = refs[:count], refs[count:]
    cut = arrivals[0].shape[1]
    begin = 0
    for result, turn in zip(results, turned):
        size = result.shape[0] if turn else result.size // result.shape[0]
        for piece in range(begin, begin + size, DH):
            spot = slice(piece, piece + DH)
            at = piece - begin
            inside = slice(piece % cut, piece % cut + DH)
            total = kept[:, spot] + arrivals[piece // cut][:, inside].astype(F32)
            if turn:
                result[at : at + DH, :] = total.T
            elif len(result.shape) == 3:
                result[:, at // result.shape[2], pl.ds(at % result.shape[2], DH)] = total
            else:
                result[:, at : at + DH] = total
        begin += size


def k_in_order(info, own, other, result):
    core = info[0]
    result[pl.ds(core, 1)] = own[...][None]
    result[pl.ds(1 - core, 1)] = other[...][None]


def k_gather(bit, info, held, arrived, result):
    mine = (info[3] >> bit) & 1
    result[:, pl.ds(mine, 1)] = held[...][:, None]
    result[:, pl.ds(1 - mine, 1)] = arrived[...][:, None]


def k_smalls(last, attn, conv, two, final, channel_sums, result):
    width = attn.shape[1]
    result[0:2, :width] = last[...]
    for place, entry in enumerate((attn, conv, two, final), 2):
        result[place : place + 1, :width] = 0.5 * entry[...]
    result[6:8, :width] = jnp.zeros((2, width), F32)
    result[:, width:] = channel_sums[...]


def k_smalls_cross(smalls, result):
    width = smalls.shape[1] - 2 * (smalls.shape[1] - result.shape[1])
    channels = result.shape[1] - width
    result[:, :width] = smalls[:, :width]
    result[:, width:] = smalls[:, width + channels :]


def k_gains(mine, theirs, channel_sums, result):
    width = mine.shape[1]
    result[:, :width] = mine[...] + theirs[...]
    result[:, width:] = channel_sums[...]


def k_smalls_add(smalls, arrived, result):
    size = result.shape[1]
    result[...] = smalls[:, :size] + arrived[...]


def run(kernel, results, arguments, scalars=1, scratch=(), late=(), leaving=(), cost=1):
    given, made = len(arguments), len(results)
    hbm_shapes = [(arguments[place].shape, arguments[place].dtype) for place in late]
    hbm_shapes += [results[place] for place in leaving]
    buffers = [pltpu.VMEM(shape, kind) for shape, kind in hbm_shapes]
    own = [pltpu.VMEM(shape, kind) for shape, kind in scratch]
    hbm = pl.BlockSpec(memory_space=pltpu.HBM)

    def body(*refs):
        ins, outs = list(refs[:given]), list(refs[given : given + made])
        rest = refs[given + made :]
        extra, held, semaphores = rest[: len(own)], rest[len(own) : -1], rest[-1]
        for index, place in enumerate(late):
            ins[place] = Late(ins[place], held[index], semaphores.at[index])
        for index, place in enumerate(leaving, len(late)):
            outs[place] = Leaving(outs[place], held[index], semaphores.at[index])
        kernel(*ins, *outs, *extra)
        arrive(*ins)
        for place in leaving:
            outs[place].finish()

    def plain(*refs):
        kernel(*refs)

    held_bytes = sum(
        functools.reduce(lambda a, b: a * b, shape) * jnp.dtype(kind).itemsize
        for shape, kind in [*scratch, *hbm_shapes]
    )
    specs = [SMEM_SPEC] * scalars + [VMEM_SPEC] * (given - scalars)
    out_specs = [VMEM_SPEC] * made
    for place in late:
        specs[place] = hbm
    for place in leaving:
        out_specs[place] = hbm
    many = len(hbm_shapes)
    return pl.pallas_call(
        body if many else plain,
        out_shape=[
            pltpu.HBM(shape, kind) if place in leaving else pltpu.VMEM(shape, kind)
            for place, (shape, kind) in enumerate(results)
        ],
        in_specs=specs,
        out_specs=out_specs,
        scratch_shapes=own + buffers + ([pltpu.SemaphoreType.DMA((many,))] if many else []),
        compiler_params=pltpu.CompilerParams(vmem_limit_bytes=held_bytes + 8 * MIB),
        cost_estimate=pl.CostEstimate(flops=cost, bytes_accessed=cost, transcendentals=0),
    )(*(
        entry if place < scalars else pltpu.with_memory_space_constraint(
            entry, pltpu.HBM if place in late else pltpu.VMEM
        )
        for place, entry in enumerate(arguments)
    ))


def swap(value, axis, bit):
    size = lax.axis_size(axis)
    return lax.ppermute(value, axis, [(place, place ^ bit) for place in range(size)])


def across(value):
    return swap(value, "tensor", 2)


def beside(value):
    return swap(value, "tensor", 1)


def bit_of(axis, bit):
    return (lax.axis_index(axis) & bit) != 0


def tie(*values):
    return lax.optimization_barrier(values)


class RowSum:
    def __init__(self, info, inputs, pairs, width, first_bits, cuts=(), cost=1):
        size = lax.axis_size("dp")
        levels = size.bit_length() - 1
        tiles = max(levels - 3, 0)
        order = [tiles + bit for bit in first_bits]
        self.order = order + [bit for bit in range(levels - 1, -1, -1) if bit not in order]
        self.left = list(range(levels - 1, -1, -1))
        self.total = sum(pair[-1] for pair in pairs)
        self.block = width // size
        self.info = info
        count = size >> tiles
        shape = (count // 2, width // count)
        self.kept, *self.sent = run(
            functools.partial(k_weights, pairs, self.order[0], tiles),
            [((*shape, self.total), F32)]
            + [((*shape, size), BF) for size in (cuts or (self.total,))],
            [info] + inputs,
            cost=cost,
        )
        self.begin()

    def begin(self):
        self.bit = self.order.pop(0)
        self.left.remove(self.bit)
        self.arrived = []

    def send(self, chain=None):
        piece = self.sent.pop(0)
        if chain is not None:
            (piece,) = chain.after(piece)
        self.arrived.append(swap(piece, "dp", 1 << self.bit))

    def here(self, chain):
        (self.arrived[-1],) = chain.after(self.arrived[-1])

    def fold(self, chain, cost=1):
        bit = self.order[0]
        place = self.left.index(bit)
        inner = self.block << (len(self.left) - 1 - place)
        outer = 1 << place
        kept, *arrived = chain.after(self.kept, *self.arrived)
        self.kept, *self.sent = run(
            functools.partial(k_fold, bit, len(arrived)),
            [((outer, inner, self.total), F32), ((outer, inner, self.total), BF)],
            [self.info, kept.reshape(outer, 2, inner, self.total)]
            + [entry.reshape(outer, 2, inner, -1) for entry in arrived],
            cost=cost,
        )
        self.kept, chain.last = tie(self.kept, chain.last)
        self.begin()

    def step(self, chain, cost=1):
        self.fold(chain, cost=cost)
        self.send()

    def finish(self, chain, *results):
        while self.order:
            self.step(chain)
        shape = (self.block, self.total)
        kept, *arrived = chain.after(
            self.kept.reshape(shape), *(entry.reshape(self.block, -1) for entry in self.arrived)
        )
        sums = run(
            functools.partial(k_finish, tuple(turn for _, turn in results), len(arrived)),
            [(size, F32) for size, _ in results],
            [self.info, kept, *arrived],
        )
        *sums, chain.last = tie(*sums, chain.last)
        return sums


class Chain:
    def __init__(self, last):
        self.last = last

    def after(self, *values):
        *values, self.last = tie(*values, self.last)
        return values


class Gather:
    def __init__(self, info, block):
        self.info, self.held = info, block.reshape(1, *block.shape)
        self.bit = lax.axis_size("dp") // 2
        self.shape = (lax.axis_size("dp") * block.shape[0], block.shape[1])

    def send(self):
        self.arrived = swap(self.held, "dp", self.bit)

    def take(self):
        outer, rows, width = self.held.shape
        (held,) = run(
            functools.partial(k_gather, self.bit.bit_length() - 1),
            [((outer, 2, rows, width), self.held.dtype)],
            [self.info, self.held, self.arrived],
        )
        self.held = held.reshape(outer * 2, rows, width)
        self.bit //= 2

    def whole(self):
        while self.bit:
            self.send()
            self.take()
        return self.held.reshape(self.shape)


def sum_pair(value, axis, merge=None):
    bit, size = 1, lax.axis_size(axis)
    while bit * 2 < size:
        (value,) = run(
            merge or k_add, [(value.shape, F32)], [value, swap(value, axis, bit)], scalars=0
        )
        bit *= 2
    return value, swap(value, axis, bit)


def per_device(
    frames,
    lengths,
    span_starts,
    mask_vector,
    ffn1_gain,
    ffn1_up,
    ffn1_down,
    attn_gain,
    query_weight,
    key_weight,
    value_weight,
    output_weight,
    rel_slope,
    conv_gain,
    conv_up,
    conv_depth,
    bn_scale,
    bn_shift,
    conv_down,
    ffn2_gain,
    ffn2_up,
    ffn2_down,
    final_gain,
    cotangent,
):
    batches, row_count, width = frames.shape
    length = row_count * lax.axis_size("tensor")
    span = 2 * row_count
    channels = conv_depth.shape[1]
    hidden_width = ffn1_up.shape[1]
    heads = rel_slope.shape[0]
    third = query_weight.shape[1]
    core = lax.axis_index("tensor") & 1
    high = (lax.axis_index("tensor") >> 1) & 1
    group = lax.axis_index("dp")
    on_first = core == 0
    own_length = jnp.where(on_first, lengths[0], lengths[1])
    info = jnp.stack([core, high, own_length, group]).astype(jnp.int32)
    starts = jnp.where(on_first, span_starts[0:1], span_starts[1:2])

    frames_across = across(frames)
    conv_block = jnp.concatenate(
        [conv_up.reshape(conv_up.shape[0], 2 * channels), conv_down.T], axis=1
    )
    conv_weights = Gather(info, conv_block)
    conv_weights.send()

    part = mask_vector.shape[0]
    place = (group * lax.axis_size("tensor") + lax.axis_index("tensor")) * part
    vectors = jnp.stack(
        [mask_vector.astype(F32), ffn1_gain, attn_gain, conv_gain, ffn2_gain, final_gain,
         jnp.zeros_like(ffn1_gain), jnp.zeros_like(ffn1_gain)]
    )
    small = lax.dynamic_update_slice(jnp.zeros((8, width), F32), vectors, (0, place))
    hops = [("tensor", 1), ("dp", 2), ("dp", 1), ("tensor", 2)]
    bit = 4
    while bit < lax.axis_size("dp"):
        hops.append(("dp", bit))
        bit *= 2
    for step, (axis, bit) in enumerate(hops):
        if step == 4:
            (sent,) = run(k_pick, [(frames.shape, BF)], [info, frames, frames_across])
            sent, small = tie(sent, small)
        if step == 3:
            query_weight, key_weight, conv_depth, rel_slope, small = tie(
                query_weight, key_weight, conv_depth, rel_slope, small
            )
            own_qkv = jnp.concatenate([query_weight, key_weight, value_weight], axis=1)
            slope_row = jnp.pad(rel_slope[None], ((0, 0), (0, channels - heads)))
            own_params = jnp.concatenate([conv_depth, bn_scale[None], bn_shift[None], slope_row])
            other_params = beside(own_params)
            conv_weights.arrived, small = tie(conv_weights.arrived, small)
            conv_weights.take()
            if conv_weights.bit:
                conv_weights.send()
        if bit < lax.axis_size(axis):
            (small,) = run(
                k_add, [(small.shape, F32)], [small, swap(small, axis, bit)], scalars=0
            )
    if conv_weights.bit:
        conv_weights.arrived, small = tie(conv_weights.arrived, small)
        conv_weights.take()
    frame_parts = [frames, frames_across, beside(sent)]
    own_qkv, other_params, conv_weights.held, small = tie(
        own_qkv, other_params, conv_weights.held, small
    )
    params = jnp.concatenate([own_params, other_params], axis=1)
    slopes = jnp.concatenate([rel_slope, other_params[KW + 2, :heads]])
    if conv_weights.bit:
        conv_weights.send()
    up_one, down_one = beside(ffn1_up), beside(ffn1_down)

    wide = (length, width)
    ffn_outs = [
        (wide, BF),
        ((length, hidden_width), BF),
        ((length, hidden_width), BF),
        ((length, 2 * hidden_width), F32),
        (wide, BF),
    ]
    whole, norm_one, cross_one, active_one, hidden_one, partial = run(
        k_ffn_one,
        [(wide, BF)] + ffn_outs,
        [info, starts, *frame_parts, small, ffn1_up, up_one, ffn1_down, down_one],
        scratch=[(wide, BF)], late=(6, 8),
    )
    output_weight, active_one = tie(output_weight, active_one)
    other_qkv, other_out = beside(own_qkv), beside(output_weight)
    stream_one, norm_attn, context_cross, context_own, qkv, weights, partial = run(
        k_attn_wrapped,
        [
            (wide, F32),
            (wide, BF),
            ((length, third), BF),
            ((length, third), BF),
            ((length, 6 * third), BF),
            ((2 * heads, length, length), F32),
            (wide, BF),
        ],
        [info, slopes, starts, partial, across(partial), whole, small, own_qkv, other_qkv,
         output_weight, other_out],
        scalars=2, late=(7, 9),
    )
    conv_weights.arrived, norm_one, cross_one, context_own = tie(
        conv_weights.arrived, norm_one, cross_one, context_own
    )
    conv_weights.take()
    own_conv = conv_weights.whole()
    other_conv = beside(own_conv)
    norm_one_too, cross_one_too = beside(norm_one), beside(cross_one)
    norm_one_too, cross_one_too, params = tie(norm_one_too, cross_one_too, params)
    both_channels = (length, 2 * channels)
    stat_shape = ((8, 2 * channels), F32)
    stream_two, norm_conv, value, gate, padded, convolved, stats = run(
        k_conv_front,
        [
            (wide, F32),
            (wide, BF),
            (both_channels, F32),
            (both_channels, F32),
            ((length + 2 * EDGE, 2 * channels), F32),
            (both_channels, F32),
            stat_shape,
        ],
        [info, partial, across(partial), stream_one, small, params, own_conv, other_conv],
        late=(6,),
    )
    norm_attn, context_cross, cotangent, ffn2_up, ffn2_down, value = tie(
        norm_attn, context_cross, cotangent, ffn2_up, ffn2_down, value
    )
    stats, stats_too = sum_pair(stats, "dp", k_merge)
    grad_across = across(cotangent)
    up_two, down_two = beside(ffn2_up), beside(ffn2_down)
    norm_attn_too, context_cross_too = beside(norm_attn), beside(context_cross)
    params, grad_across = tie(params, grad_across)
    stats, active_conv, cross_conv, partial = run(
        k_conv_rear,
        [stat_shape, ((length, channels), BF), ((length, channels), BF), (wide, BF)],
        [stats, stats_too, convolved, params, norm_conv, own_conv, other_conv],
        scalars=0, late=(5,),
    )
    grad_across, active_conv = tie(grad_across, active_conv)
    (sent,) = run(k_pick, [(cotangent.shape, BF)], [info, cotangent, grad_across])
    grad_parts = [cotangent, grad_across, beside(sent)]
    grad_parts[2], small = tie(grad_parts[2], small)
    stream_three, norm_two, cross_two, active_two, hidden_two, partial = run(
        k_ffn_two,
        [(wide, F32)] + ffn_outs,
        [partial, across(partial), stream_two, small, ffn2_up, up_two, ffn2_down, down_two],
        scalars=0, late=(4, 6),
    )
    norm_two, cross_two, norm_conv, cross_conv, active_two = tie(
        norm_two, cross_two, norm_conv, cross_conv, active_two
    )
    norm_two_too, cross_two_too = beside(norm_two), beside(cross_two)
    norm_conv_too, cross_conv_too = beside(norm_conv), beside(cross_conv)
    (
        norm_two_too, cross_two_too, norm_conv_too, cross_conv_too, norm_attn_too,
        context_cross_too, small,
    ) = tie(
        norm_two_too, cross_two_too, norm_conv_too, cross_conv_too, norm_attn_too,
        context_cross_too, small,
    )

    row_shape = ((1, width), F32)
    block_shape = (row_count, width)
    out_own, out_sent, grad_four, sum_final, back_two, hid_cross_two, hid_two, partial = run(
        k_ffn_two_back,
        [
            (block_shape, BF),
            (block_shape, BF),
            (wide, F32),
            row_shape,
            (wide, BF),
            ((length, hidden_width), BF),
            ((length, hidden_width), BF),
            (wide, BF),
        ],
        [info, partial, across(partial), stream_three, small, *grad_parts, hidden_two,
         ffn2_up, up_two, ffn2_down, down_two],
        scratch=[(wide, BF), (wide, BF)], late=(9, 11),
    )
    back_two_too, hid_cross_two_too = beside(back_two), beside(hid_cross_two)
    ffn_pair = ((0, 1, 2, 0, 3, 0, hidden_width),)
    two_up = RowSum(
        info, [norm_two, norm_two_too, hid_two, hid_cross_two_too], ffn_pair, width, (0, 1, 2)
    )
    two_down = RowSum(
        info, [back_two, back_two_too, active_two, cross_two_too], ffn_pair, width, (1, 2, 0)
    )
    grad_four, two_up.sent[0], two_down.sent[0] = tie(
        grad_four, two_up.sent[0], two_down.sent[0]
    )
    grad_three, sum_two, back_conv, grad_shaped, sums = run(
        k_conv_back_front,
        [(wide, F32), row_shape, (wide, BF), (both_channels, F32), stat_shape],
        [partial, across(partial), stream_three, small, grad_four, convolved, stats, params,
         own_conv, other_conv],
        scalars=0, late=(8,),
    )
    out_sent, sum_two, back_conv = tie(out_sent, sum_two, back_conv)
    out_other, back_conv_too = beside(out_sent), beside(back_conv)
    bits = [1 << level for level in range(lax.axis_size("dp").bit_length() - 1)]
    for bit in bits[:-1]:
        (sums,) = run(
            k_add, [(sums.shape, F32)], [sums, swap(sums, "dp", bit)], scalars=0
        )
        chain = Chain(sums)
        if bit == 1:
            two_up.send(chain)
        if bit == 2:
            two_down.send(chain)
        sums = chain.last
    sums_too = swap(sums, "dp", bits[-1])
    sums_too, out_other, back_conv_too = tie(sums_too, out_other, back_conv_too)
    small_sums, mixed_own, mixed_cross, partial = run(
        k_conv_back_rear,
        [
            stat_shape,
            ((length, 2 * channels), BF),
            ((length, 2 * channels), BF),
            (wide, BF),
        ],
        [info, sums, sums_too, grad_shaped, convolved, stats, params, padded, value, gate,
         back_conv, own_conv, other_conv],
        scratch=[((length + 2 * EDGE, 2 * channels), F32)], late=(11,),
    )
    mixed_cross_too = beside(mixed_cross)
    mixed_cross_too, grad_three = tie(mixed_cross_too, grad_three)
    grad_two, sum_conv, back_attn, three_cross, three_own, small_sums, partial = run(
        k_attn_back,
        [
            (wide, F32),
            row_shape,
            (wide, BF),
            ((length, 3 * third), BF),
            ((length, 3 * third), BF),
            stat_shape,
            (wide, BF),
        ],
        [partial, across(partial), stream_two, small, grad_three, small_sums, qkv, weights,
         own_qkv, other_qkv, output_weight, other_out],
        scalars=0,
        scratch=[((length, 2 * third), BF)], late=(8, 10),
    )
    back_attn_too, three_cross_too = beside(back_attn), beside(three_cross)
    chain = Chain(small_sums)
    for entry in (two_up, two_down):
        entry.step(chain)
    back_attn, three_own = chain.after(back_attn, three_own)
    small_sums = chain.last
    middle = RowSum(
        info,
        [norm_conv, norm_conv_too, mixed_own, mixed_cross_too,
         back_conv, back_conv_too, active_conv, cross_conv_too,
         norm_attn, norm_attn_too, three_own, three_cross_too,
         back_attn, back_attn_too, context_own, context_cross_too],
        (
            (0, 1, 2, 0, 3, 0, 2 * channels),
            (4, 5, 6, 0, 7, 0, channels),
            (8, 9, 10, 0, 11, 0, 3 * third),
            (12, 13, 14, 0, 15, 0, third),
        ),
        width, (0, 1, 2),
    )
    middle.send()
    middle.kept, grad_two = tie(middle.kept, grad_two)
    grad_one, sum_attn, back_one, hid_cross_one, hid_one, last_own, last_sent = run(
        k_ffn_one_back,
        [
            (wide, F32),
            row_shape,
            (wide, BF),
            ((length, hidden_width), BF),
            ((length, hidden_width), BF),
            ((span, width), F32),
            ((span, width), BF),
        ],
        [info, partial, across(partial), stream_one, small, grad_two, hidden_one,
         ffn1_up, up_one, ffn1_down, down_one],
        scratch=[(wide, F32)], late=(7, 9),
    )
    back_one_too, hid_cross_one_too = beside(back_one), beside(hid_cross_one)
    chain = Chain(sum_attn)
    for entry in (two_up, two_down):
        entry.step(chain, cost=COST)
    hid_one, active_one = chain.after(hid_one, active_one)
    one_up = RowSum(
        info, [norm_one, norm_one_too, hid_one, hid_cross_one_too], ffn_pair, width, (0, 1, 2),
        cost=COST,
    )
    one_down = RowSum(
        info, [back_one, back_one_too, active_one, cross_one_too], ffn_pair, width, (0, 1, 2),
        cost=COST,
    )
    one_up.send(chain)
    one_up.kept, chain.last = tie(one_up.kept, chain.last)
    one_down.send(chain)
    one_down.kept, chain.last = tie(one_down.kept, chain.last)
    block = width // lax.axis_size("dp")
    (starts,) = chain.after(starts)
    sum_attn = chain.last
    frames_own, frames_sent, last_sums = run(
        k_last,
        [(block_shape, F32), (block_shape, F32), ((2, width), F32)],
        [info, starts, last_own, across(last_sent), whole, small, grad_one],
        scratch=[((span, width), F32)],
    )
    frames_other = beside(frames_sent)
    (smalls,) = run(
        k_smalls, [((8, width + 2 * channels), F32)],
        [last_sums, sum_attn, sum_conv, sum_two, sum_final, small_sums], scalars=0,
    )
    (smalls_sent,) = run(k_smalls_cross, [((8, width + channels), F32)], [smalls], scalars=0)
    (smalls,) = run(
        k_smalls_add, [((8, width + channels), F32)], [smalls, beside(smalls_sent)], scalars=0
    )
    gains, gains_too = smalls[:, :width], across(smalls[:, :width])
    (gains,) = run(
        k_gains, [(smalls.shape, F32)], [gains, gains_too, smalls[:, width:]], scalars=0
    )

    def in_order(own, other):
        return run(k_in_order, [((2, *own.shape), own.dtype)], [info, own, other])[0]

    chain = Chain(in_order(out_own, out_other))

    def hop(value, bit):
        (value,) = chain.after(value)
        return value, swap(value, "dp", bit)

    def add(value, other):
        (total,) = run(k_add, [(value.shape, F32)], chain.after(value, other), scalars=0)
        return total

    first, *between = [1 << level for level in range(1, lax.axis_size("dp").bit_length() - 1)]
    gains = add(*hop(gains, first))
    gains, chain.last = tie(gains, chain.last)
    (two_up,) = two_up.finish(chain, ((block, hidden_width), False))
    middle.step(chain)
    for bit in between:
        gains = add(*hop(gains, bit))
    gains, chain.last = tie(gains, chain.last)
    middle.step(chain)
    one_up.step(chain)
    one_down.step(chain)
    one_up.step(chain)
    conv_up_grad, conv_down_grad, query_grad, key_grad, value_grad, output_grad = middle.finish(
        chain,
        (conv_up.shape, False), ((channels, block), True),
        *[((block, third), False)] * 3, ((third, block), True),
    )
    gains, gains_too = hop(gains, 1)
    (one_up,) = one_up.finish(chain, ((block, hidden_width), False))
    gains = add(gains, gains_too)
    one_down.step(chain)
    (two_down,) = two_down.finish(chain, ((hidden_width, block), True))
    channel_sums = gains[:, width:]
    scale_grad = channel_sums[KW + 1] * (1.0 / lax.axis_size("dp"))
    shift_grad = channel_sums[KW] * (1.0 / lax.axis_size("dp"))
    gains = lax.dynamic_slice_in_dim(gains, place, part, axis=1)

    frames_grad = in_order(frames_own, frames_other)
    smallest = [
        *(gains[index] for index in range(6)),
        channel_sums[KW + 2, :heads],
        channel_sums[:KW],
        scale_grad,
        shift_grad,
    ]
    frames_grad, *smallest = chain.after(frames_grad, *smallest)
    (one_down,) = one_down.finish(chain, ((hidden_width, block), True))

    return (
        chain.last,
        frames_grad,
        smallest[0],
        smallest[1],
        one_up,
        one_down,
        smallest[2],
        query_grad,
        key_grad,
        value_grad,
        output_grad,
        smallest[6],
        smallest[3],
        conv_up_grad,
        smallest[7],
        smallest[8],
        smallest[9],
        conv_down_grad,
        smallest[4],
        two_up,
        two_down,
        smallest[5],
    )


def k_attn_wrapped(info, slopes, starts, *refs):
    k_attn(info, starts, slopes, *refs)


def solution(mesh):
    every, split, by_column = P(("dp", "tensor")), P("tensor"), P(None, "tensor")
    rows_by = P("dp", "tensor", None)
    return jax.shard_map(
        per_device,
        mesh=mesh,
        in_specs=(
            rows_by,
            P("dp"),
            P("dp", None),
            every,
            every,
            by_column,
            P("tensor", None),
            every,
            by_column,
            by_column,
            by_column,
            P("tensor", None),
            split,
            every,
            P("dp", None, "tensor"),
            by_column,
            split,
            split,
            P("tensor", "dp"),
            every,
            by_column,
            P("tensor", None),
            every,
            rows_by,
        ),
        out_specs=(
            rows_by,
            rows_by,
            every,
            every,
            P("dp", "tensor"),
            P("tensor", "dp"),
            every,
            P("dp", "tensor"),
            P("dp", "tensor"),
            P("dp", "tensor"),
            P("tensor", "dp"),
            split,
            every,
            P("dp", None, "tensor"),
            by_column,
            split,
            split,
            P("tensor", "dp"),
            every,
            P("dp", "tensor"),
            P("tensor", "dp"),
            every,
        ),
        check_vma=False,
    )
```

```python
import functools

import jax
import jax.numpy as jnp
from jax import lax
from jax.experimental import pallas as pl
from jax.experimental.pallas import tpu as pltpu
from jax.sharding import PartitionSpec as P

DH = 128
KW = 5
SPAN = 10
REACH = 128
EPSILON = 1e-05
MASKED_SCORE = -1000000000.0
BF = jnp.bfloat16
F32 = jnp.float32
STEP = 32
TILE = 256
EDGE = 8
MIB = 1024 * 1024
COST = 30_000_000

VMEM_SPEC = pl.BlockSpec(memory_space=pltpu.VMEM)
SMEM_SPEC = pl.BlockSpec(memory_space=pltpu.SMEM)


def product(left, right):
    return jnp.dot(left, right, preferred_element_type=F32)


def inner_rows(left, right):
    return lax.dot_general(left, right, (((0,), (0,)), ((), ())), preferred_element_type=F32)


def times_back(left, right):
    return lax.dot_general(left, right, (((1,), (1,)), ((), ())), preferred_element_type=F32)


def sigmoid(values):
    return 0.5 * jnp.tanh(0.5 * values) + 0.5


def norm_unit(values):
    centre = jnp.mean(values, axis=-1, keepdims=True)
    centred = values - centre
    inverse = lax.rsqrt(jnp.mean(centred * centred, axis=-1, keepdims=True) + EPSILON)
    return centred * inverse, inverse


def norm_back(grad_out, unit_rows, inverse, norm_gain):
    grad_unit = grad_out * norm_gain
    first_mean = jnp.mean(grad_unit, axis=-1, keepdims=True)
    second_mean = jnp.mean(grad_unit * unit_rows, axis=-1, keepdims=True)
    return (
        inverse * (grad_unit - first_mean - unit_rows * second_mean),
        jnp.sum(grad_out * unit_rows, axis=0, keepdims=True),
    )


def silu_slope(values):
    gate_value = sigmoid(values)
    return gate_value * (1.0 + values * (1.0 - gate_value))


def over_rows(count, body, init=0, step=STEP):
    def one(index, carry):
        return body(pl.ds(pl.multiple_of(index * step, step), step), index * step, carry)

    return lax.fori_loop(0, count // step, one, init, unroll=4)


def row_iota(first, rows, columns):
    return first + lax.broadcasted_iota(jnp.int32, (rows, columns), 0)


def mask_col(starts_ref, first, rows, length):
    starts = starts_ref[...]
    at = row_iota(first, rows, starts.shape[1])
    hit = (starts <= at) & (at < starts + SPAN) & (at < length)
    return jnp.max(jnp.where(hit, 1.0, 0.0), axis=1, keepdims=True)


def valid_col(first, rows, columns, length):
    return jnp.where(row_iota(first, rows, columns) < length, 1.0, 0.0)


def masked_rows(frame_rows, mask, mask_row):
    return jnp.where(
        jnp.broadcast_to(mask, frame_rows.shape) > 0.5, mask_row, frame_rows.astype(F32)
    )


def pair_sum(mine, theirs, rows):
    return mine[rows, :].astype(F32) + theirs[rows, :].astype(F32)


class Late:
    def __init__(self, source, held, semaphore):
        self.copy = pltpu.make_async_copy(source, held, semaphore)
        self.copy.start()
        self.held, self.shape, self.dtype, self.waited = held, held.shape, held.dtype, False

    def arrive(self):
        if not self.waited:
            self.copy.wait()
            self.waited = True

    def __getitem__(self, index):
        assert self.waited
        return self.held[index]


class Leaving:
    def __init__(self, target, held, semaphore):
        self.copy = pltpu.make_async_copy(held, target, semaphore)
        self.held, self.shape, self.dtype, self.started = held, held.shape, held.dtype, False

    def leave(self):
        if not self.started:
            self.copy.start()
            self.started = True

    def finish(self):
        self.leave()
        self.copy.wait()

    def __getitem__(self, index):
        return self.held[index]

    def __setitem__(self, index, value):
        assert not self.started
        self.held[index] = value


def arrive(*refs):
    for ref in refs:
        if isinstance(ref, Late):
            ref.arrive()


def leave(*refs):
    for ref in refs:
        if isinstance(ref, Leaving):
            ref.leave()


def columns(index, size=TILE):
    return slice(index * size, (index + 1) * size)


def ffn_up(branch, ups, hidden, active_own, active_cross):
    normed = branch[...]
    for shard, weight in enumerate(ups):
        arrive(weight)
        tiles = weight.shape[1] // TILE
        for index in range(tiles):
            at = columns(index)
            values = product(normed, weight[:, at])
            hidden[:, columns(index + shard * tiles)] = values
            (active_own, active_cross)[shard][:, at] = (values * sigmoid(values)).astype(BF)


def ffn_down(active_own, active_cross, downs, part):
    width = downs[0].shape[1]
    own, cross = active_own[...], active_cross[...]
    arrive(*downs)
    for index in range(width // TILE):
        at = columns(index)
        part[:, at] = (product(own, downs[0][:, at]) + product(cross, downs[1][:, at])).astype(BF)


def ffn_grad_hidden(branch, downs, hidden, grad_own, grad_cross):
    grad_branch = branch[...]
    for shard, weight in enumerate(downs):
        arrive(weight)
        tiles = weight.shape[0] // TILE
        for index in range(tiles):
            at = columns(index)
            slope = silu_slope(hidden[:, columns(index + shard * tiles)])
            grad = (times_back(grad_branch, weight[at, :]) * slope).astype(BF)
            (grad_own, grad_cross)[shard][:, at] = grad


def ffn_grad_input(grad_own, grad_cross, ups, store):
    own, cross = grad_own[...], grad_cross[...]
    arrive(*ups)
    for index in range(ups[0].shape[0] // TILE):
        at = columns(index)
        store(at, times_back(own, ups[0][at, :]) + times_back(cross, ups[1][at, :]))


def k_pick(info, block, across_block, sent):
    core = info[0]
    sent[0] = block[pl.ds(1 - core, 1)][0]
    sent[1] = across_block[pl.ds(1 - core, 1)][0]


def place_rows(info, block, across_block, arrived, whole):
    core, high = info[0], info[1]
    rows = block.shape[1]
    places = (
        (2 * high + core, block[pl.ds(core, 1)][0]),
        (2 * (1 - high) + core, across_block[pl.ds(core, 1)][0]),
        (2 * high + 1 - core, arrived[0]),
        (2 * (1 - high) + 1 - core, arrived[1]),
    )
    for place, value in places:
        whole[pl.ds(pl.multiple_of(place * rows, rows), rows), :] = value


def k_ffn_one(
    info, starts, block, across_block, arrived, small, up_o, up_t, down_o, down_t,
    frames, branch, active_cross, active_own, hidden, part, whole,
):
    length = info[2]
    rows, width = whole.shape
    place_rows(info, block, across_block, arrived, whole)
    frames[...] = whole[...]

    def normalise(at, first, carry):
        mask = mask_col(starts, first, STEP, length)
        unit_rows, _ = norm_unit(masked_rows(whole[at, :], mask, small[0:1, :]))
        branch[at, :] = (unit_rows * small[1:2, :]).astype(BF)
        return carry

    over_rows(rows, normalise)
    ffn_up(branch, (up_o, up_t), hidden, active_own, active_cross)
    ffn_down(active_own, active_cross, (down_o, down_t), part)


def k_attn(
    info, starts, slopes, mine, theirs, frames, small, qkv_o, qkv_t, out_o, out_t,
    stream, branch, context_cross, context_own, qkv, weights, part,
):
    length = info[2]
    rows, width = frames.shape
    arrive(frames)

    def normalise(at, first, carry):
        mask = mask_col(starts, first, STEP, length)
        inputs = masked_rows(frames[at, :], mask, small[0:1, :])
        values = inputs + 0.5 * pair_sum(mine, theirs, at)
        stream[at, :] = values
        unit_rows, _ = norm_unit(values)
        branch[at, :] = (unit_rows * small[2:3, :]).astype(BF)
        return carry

    over_rows(rows, normalise)
    normed = branch[...]
    third = qkv_o.shape[1] // 3
    for shard, weight in enumerate((qkv_o, qkv_t)):
        arrive(weight)
        for index in range(3):
            at = columns(index, third)
            qkv[:, columns(3 * shard + index, third)] = product(normed, weight[:, at]).astype(BF)
    heads = third // DH
    span = rows // 2
    for shard in range(2):
        base = 3 * third * shard
        for head in range(heads):
            place = shard * heads + head
            key = qkv[:, base + third + head * DH : base + third + (head + 1) * DH]
            value = qkv[:, base + 2 * third + head * DH : base + 2 * third + (head + 1) * DH]
            for part_index in range(2):
                at = columns(part_index, span)
                query = qkv[at, base + head * DH : base + (head + 1) * DH]
                scores = times_back(query, key) * DH ** (-0.5)
                key_place = lax.broadcasted_iota(jnp.int32, (span, rows), 1)
                away = key_place - row_iota(part_index * span, span, rows)
                relative = jnp.clip(away, -REACH, REACH).astype(F32) * (1.0 / REACH)
                scores = scores + slopes[place] * relative
                scores = jnp.where(key_place < length, scores, MASKED_SCORE)
                raised = jnp.exp(scores - jnp.max(scores, axis=-1, keepdims=True))
                soft = raised * (1.0 / jnp.sum(raised, axis=-1, keepdims=True))
                weights[place, at, :] = soft
                context = product(soft.astype(BF), value).astype(BF)
                if shard == 0:
                    context_own[at, columns(head, DH)] = context
                else:
                    context_cross[at, columns(head, DH)] = context
    arrive(out_o, out_t)
    own = context_own[...]
    other = context_cross[...]
    for index in range(width // TILE):
        at = columns(index)
        part[:, at] = (product(own, out_o[:, at]) + product(other, out_t[:, at])).astype(BF)


def k_conv_front(
    info, mine, theirs, stream_in, small, params, conv_o, conv_t,
    stream, normed, value, gate, padded, convolved, stats,
):
    length = info[2]
    rows, width = stream_in.shape
    channels = params.shape[1] // 2
    arrive(stream_in)

    def normalise(at, first, carry):
        values = stream_in[at, :] + pair_sum(mine, theirs, at)
        stream[at, :] = values
        unit_rows, _ = norm_unit(values)
        normed[at, :] = (unit_rows * small[3:4, :]).astype(BF)
        return carry

    over_rows(rows, normalise)
    normed_rows = normed[...]
    edge = jnp.zeros((EDGE, 2 * channels), F32)
    padded[:EDGE, :] = edge
    padded[EDGE + rows :, :] = edge
    for shard, weight in enumerate((conv_o, conv_t)):
        arrive(weight)
        at = columns(shard, channels)
        value_rows = product(normed_rows, weight[:, :channels])
        value[:, at] = value_rows
        gate_rows = sigmoid(product(normed_rows, weight[:, channels : 2 * channels]))
        gate[:, at] = gate_rows
        padded[EDGE : EDGE + rows, at] = (
            value_rows * gate_rows * valid_col(0, rows, channels, length)
        )
    count = length.astype(F32)
    for tile in range(2 * channels // DH):
        at = columns(tile, DH)
        total = params[0:1, at] * padded[EDGE - 2 : EDGE - 2 + rows, at]
        for offset in range(1, KW):
            begin = EDGE - 2 + offset
            total = total + params[offset : offset + 1, at] * padded[begin : begin + rows, at]
        convolved[:, at] = total
        keep = valid_col(0, rows, DH, length)
        mean = jnp.sum(total * keep, axis=0, keepdims=True) / count
        centred = (total - mean) * keep
        stats[0:1, at] = jnp.full((1, DH), count, F32)
        stats[1:2, at] = mean
        stats[2:3, at] = jnp.sum(centred * centred, axis=0, keepdims=True)
        stats[3:8, at] = jnp.zeros((5, DH), F32)


def merged(mine, theirs):
    total = mine[0:1, :] + theirs[0:1, :]
    apart = mine[1:2, :] - theirs[1:2, :]
    mean = (mine[0:1, :] * mine[1:2, :] + theirs[0:1, :] * theirs[1:2, :]) / total
    share = mine[0:1, :] * theirs[0:1, :] / total
    spread = mine[2:3, :] + theirs[2:3, :] + apart * apart * share
    return total, mean, spread


def k_merge(mine, theirs, result):
    total, mean, spread = merged(mine, theirs)
    result[0:1, :] = total
    result[1:2, :] = mean
    result[2:3, :] = spread
    result[3:8, :] = jnp.zeros((5, result.shape[1]), F32)


def k_add(mine, theirs, result):
    result[...] = mine[...] + theirs[...]


def shaped_rows(convolved, stats, params, at):
    unit_bn = (convolved[at, :] - stats[1:2, :]) * stats[2:3, :]
    return unit_bn, unit_bn * params[5:6, :] + params[6:7, :]


def k_conv_rear(
    mine, theirs, convolved, params, normed, conv_o, conv_t,
    stats, active_own, active_cross, part,
):
    rows, width = normed.shape
    channels = params.shape[1] // 2
    total, mean, spread = merged(mine, theirs)
    arrive(convolved)
    stats[0:1, :] = total
    stats[1:2, :] = mean
    stats[2:3, :] = lax.rsqrt(spread / total + EPSILON)
    stats[3:8, :] = jnp.zeros((5, stats.shape[1]), F32)

    def activate(at, first, carry):
        _, shaped = shaped_rows(convolved, stats, params, at)
        active = (shaped * sigmoid(shaped)).astype(BF)
        active_own[at, :] = active[:, :channels]
        active_cross[at, :] = active[:, channels:]
        return carry

    over_rows(rows, activate)
    arrive(conv_o, conv_t)
    own = active_own[...]
    other = active_cross[...]
    for index in range(width // TILE):
        at = columns(index)
        part[:, at] = (
            times_back(own, conv_o[at, 2 * channels :])
            + times_back(other, conv_t[at, 2 * channels :])
        ).astype(BF)


def k_ffn_two(
    mine, theirs, stream_in, small, up_o, up_t, down_o, down_t,
    stream, branch, active_cross, active_own, hidden, part,
):
    rows, width = stream_in.shape
    arrive(stream_in)

    def normalise(at, first, carry):
        values = stream_in[at, :] + pair_sum(mine, theirs, at)
        stream[at, :] = values
        unit_rows, _ = norm_unit(values)
        branch[at, :] = (unit_rows * small[4:5, :]).astype(BF)
        return carry

    over_rows(rows, normalise)
    ffn_up(branch, (up_o, up_t), hidden, active_own, active_cross)
    ffn_down(active_own, active_cross, (down_o, down_t), part)


def split_blocks(info, rows, source, own, sent):
    core, high = info[0], info[1]
    own[...] = source[pl.ds((2 * high + core) * rows, rows), :]
    sent[...] = source[pl.ds((2 * high + 1 - core) * rows, rows), :]


def k_ffn_two_back(
    info, mine, theirs, stream, small, block, across_block, arrived, hidden,
    up_o, up_t, down_o, down_t,
    out_own, out_sent, grad_four, gain_sum, branch, grad_cross, grad_own, part, out_rows, grads,
):
    rows, width = stream.shape
    arrive(block, across_block, arrived)
    place_rows(info, block, across_block, arrived, grads)
    arrive(stream)

    def pass_back(at, first, carry):
        values = stream[at, :] + 0.5 * pair_sum(mine, theirs, at)
        unit_rows, inverse = norm_unit(values)
        out_rows[at, :] = (unit_rows * small[5:6, :]).astype(BF)
        grad, fresh = norm_back(grads[at, :].astype(F32), unit_rows, inverse, small[5:6, :])
        grad_four[at, :] = grad
        branch[at, :] = (0.5 * grad).astype(BF)
        return carry + fresh

    gain_sum[...] = over_rows(rows, pass_back, jnp.zeros((1, width), F32))
    split_blocks(info, rows // 4, out_rows, out_own, out_sent)
    ffn_grad_hidden(branch, (down_o, down_t), hidden, grad_own, grad_cross)

    def store(at, values):
        part[:, at] = values.astype(BF)

    ffn_grad_input(grad_own, grad_cross, (up_o, up_t), store)


def k_conv_back_front(
    mine, theirs, stream, small, grad_in, convolved, stats, params, conv_o, conv_t,
    grad_out, gain_sum, branch, grad_shaped, sums,
):
    rows, width = stream.shape
    channels = params.shape[1] // 2
    arrive(stream)

    def pass_back(at, first, carry):
        unit_rows, inverse = norm_unit(stream[at, :])
        grad, fresh = norm_back(pair_sum(mine, theirs, at), unit_rows, inverse, small[4:5, :])
        grad = grad_in[at, :] + grad
        grad_out[at, :] = grad
        branch[at, :] = grad.astype(BF)
        return carry + fresh

    gain_sum[...] = over_rows(rows, pass_back, jnp.zeros((1, width), F32))
    branch_rows = branch[...]
    arrive(convolved)
    for shard, weight in enumerate((conv_o, conv_t)):
        arrive(weight)
        grad_shaped[:, columns(shard, channels)] = product(branch_rows, weight[:, 2 * channels :])

    def slope(at, first, carry):
        unit_bn, shaped = shaped_rows(convolved, stats, params, at)
        grad = grad_shaped[at, :] * silu_slope(shaped)
        grad_shaped[at, :] = grad
        return (
            carry[0] + jnp.sum(grad, axis=0, keepdims=True),
            carry[1] + jnp.sum(grad * unit_bn, axis=0, keepdims=True),
        )

    zero = jnp.zeros((1, 2 * channels), F32)
    shift_sum, scale_sum = over_rows(rows, slope, (zero, zero))
    sums[0:1, :] = shift_sum
    sums[1:2, :] = scale_sum
    sums[2:8, :] = jnp.zeros((6, 2 * channels), F32)


def k_conv_back_rear(
    info, sums_mine, sums_theirs, grad_shaped, convolved, stats, params, padded, value, gate, branch,
    conv_o, conv_t,
    small_sums, mixed_own, mixed_cross, part, grad_padded,
):
    length = info[2]
    rows, width = branch.shape
    channels = params.shape[1] // 2
    sums = sums_mine[0:2, :] + sums_theirs[0:2, :]
    small_sums[5:6, :] = sums[0:1, :]
    small_sums[6:7, :] = sums[1:2, :]
    small_sums[7:8, :] = jnp.zeros((1, 2 * channels), F32)
    edge = jnp.zeros((EDGE, 2 * channels), F32)
    grad_padded[:EDGE, :] = edge
    grad_padded[EDGE + rows :, :] = edge
    arrive(convolved)
    count, bn_inverse, scale_row = stats[0:1, :], stats[2:3, :], params[5:6, :]
    grad_centre = -bn_inverse * scale_row * sums[0:1, :]
    grad_spread = -bn_inverse * bn_inverse * scale_row * sums[1:2, :]

    def spread(at, first, carry):
        centred = convolved[at, :] - stats[1:2, :]
        keep = valid_col(first, STEP, 2 * channels, length)
        grad = grad_shaped[at, :] * scale_row * bn_inverse + keep * (
            grad_centre + grad_spread * centred
        ) * (1.0 / count)
        grad_padded[pl.ds(pl.multiple_of(EDGE + first, EDGE), STEP), :] = grad
        return carry

    over_rows(rows, spread)
    arrive(padded, gate, value)
    for tile in range(2 * channels // DH):
        at = columns(tile, DH)
        grad = grad_padded[EDGE : EDGE + rows, at]
        back = None
        for offset in range(KW):
            begin = EDGE + 2 - offset
            term = params[offset : offset + 1, at] * grad_padded[begin : begin + rows, at]
            back = term if back is None else back + term
            begin = EDGE - 2 + offset
            small_sums[offset : offset + 1, at] = jnp.sum(
                grad * padded[begin : begin + rows, at], axis=0, keepdims=True
            )
        back = back * valid_col(0, rows, DH, length)
        gate_rows = gate[:, at]
        first_grad = (back * gate_rows).astype(BF)
        second_grad = (back * value[:, at] * gate_rows * (1.0 - gate_rows)).astype(BF)
        inner = (tile * DH) % channels
        if tile * DH < channels:
            mixed_own[:, inner : inner + DH] = first_grad
            mixed_own[:, channels + inner : channels + inner + DH] = second_grad
        else:
            mixed_cross[:, inner : inner + DH] = first_grad
            mixed_cross[:, channels + inner : channels + inner + DH] = second_grad
    arrive(conv_o, conv_t)
    own = mixed_own[...]
    other = mixed_cross[...]
    for index in range(width // TILE):
        at = columns(index)
        part[:, at] = (
            times_back(own, conv_o[at, : 2 * channels])
            + times_back(other, conv_t[at, : 2 * channels])
        ).astype(BF)


def k_attn_back(
    mine, theirs, stream, small, grad_in, sums_in, qkv, weights, qkv_o, qkv_t, out_o, out_t,
    grad_out, gain_sum, branch, three_cross, three_own, small_sums, part, grad_context,
):
    rows, width = stream.shape
    arrive(stream)
    third = qkv_o.shape[1] // 3
    heads = third // DH

    def pass_back(at, first, carry):
        unit_rows, inverse = norm_unit(stream[at, :])
        grad, fresh = norm_back(pair_sum(mine, theirs, at), unit_rows, inverse, small[3:4, :])
        grad = grad_in[at, :] + grad
        grad_out[at, :] = grad
        branch[at, :] = grad.astype(BF)
        return carry + fresh

    gain_sum[...] = over_rows(rows, pass_back, jnp.zeros((1, width), F32))
    branch_rows = branch[...]
    for shard, weight in enumerate((out_o, out_t)):
        arrive(weight)
        grad_context[:, columns(shard, third)] = times_back(branch_rows, weight[...]).astype(BF)
    away = lax.broadcasted_iota(jnp.int32, (rows, rows), 1) - row_iota(0, rows, rows)
    relative = jnp.clip(away, -REACH, REACH).astype(F32) * (1.0 / REACH)
    scale = DH ** (-0.5)
    arrive(qkv, weights)
    lanes = small_sums.shape[1]
    lane = lax.broadcasted_iota(jnp.int32, (1, lanes), 1)
    slope_row = jnp.zeros((1, lanes), F32)
    for shard in range(2):
        base = 3 * third * shard
        for head in range(heads):
            place = shard * heads + head
            query = qkv[:, base + head * DH : base + (head + 1) * DH]
            key = qkv[:, base + third + head * DH : base + third + (head + 1) * DH]
            value = qkv[:, base + 2 * third + head * DH : base + 2 * third + (head + 1) * DH]
            grad_head = grad_context[:, place * DH : (place + 1) * DH]
            soft = weights[place]
            grad_soft = times_back(grad_head, value)
            grad_value = inner_rows(soft.astype(BF), grad_head)
            dots = jnp.sum(soft * grad_soft, axis=-1, keepdims=True)
            grad_scores = (soft * (grad_soft - dots)).astype(BF)
            tilted = jnp.sum(grad_scores.astype(F32) * relative, axis=0, keepdims=True)
            slope = jnp.broadcast_to(jnp.sum(tilted, axis=1, keepdims=True), (1, lanes))
            slope_row = jnp.where(lane == shard * (lanes // 2) + head, slope, slope_row)
            grads = (
                product(grad_scores, key) * scale,
                inner_rows(grad_scores, query) * scale,
                grad_value,
            )
            for index, grad in enumerate(grads):
                begin = index * third + head * DH
                if shard == 0:
                    three_own[:, begin : begin + DH] = grad.astype(BF)
                else:
                    three_cross[:, begin : begin + DH] = grad.astype(BF)
    small_sums[:7, :] = sums_in[:7, :]
    small_sums[7:8, :] = slope_row
    arrive(qkv_o, qkv_t)
    own = three_own[...]
    other = three_cross[...]
    for index in range(width // TILE):
        at = columns(index)
        part[:, at] = (times_back(own, qkv_o[at, :]) + times_back(other, qkv_t[at, :])).astype(BF)


def k_ffn_one_back(
    info, mine, theirs, stream, small, grad_in, hidden, up_o, up_t, down_o, down_t,
    grad_out, gain_sum, branch, grad_cross, grad_own, part_own, part_sent, whole,
):
    high = info[1]
    rows, width = stream.shape
    span = rows // 2
    arrive(stream)

    def pass_back(at, first, carry):
        unit_rows, inverse = norm_unit(stream[at, :])
        grad, fresh = norm_back(pair_sum(mine, theirs, at), unit_rows, inverse, small[2:3, :])
        grad = grad_in[at, :] + grad
        grad_out[at, :] = grad
        branch[at, :] = (0.5 * grad).astype(BF)
        return carry + fresh

    gain_sum[...] = over_rows(rows, pass_back, jnp.zeros((1, width), F32))
    ffn_grad_hidden(branch, (down_o, down_t), hidden, grad_own, grad_cross)

    def store(at, values):
        whole[:, at] = values

    ffn_grad_input(grad_own, grad_cross, (up_o, up_t), store)
    part_own[...] = whole[pl.ds(high * span, span), :]
    part_sent[...] = whole[pl.ds((1 - high) * span, span), :].astype(BF)


def k_last(
    info, starts, part_own, arrived, frames, small, grad_in,
    grad_own, grad_sent, sums, grads,
):
    core, high, length = info[0], info[1], info[2]
    span, width = part_own.shape
    arrive(frames)

    def pass_back(at, first, carry):
        begin = pl.multiple_of(high * span + first, STEP)
        mask = mask_col(starts, begin, STEP, length)
        unit_rows, inverse = norm_unit(
            masked_rows(frames[pl.ds(begin, STEP), :], mask, small[0:1, :])
        )
        grad_normed = part_own[at, :] + arrived[at, :].astype(F32)
        grad, fresh = norm_back(grad_normed, unit_rows, inverse, small[1:2, :])
        grad = grad_in[pl.ds(begin, STEP), :] + grad
        hit = jnp.broadcast_to(mask, grad.shape) > 0.5
        grads[at, :] = jnp.where(hit, 0.0, grad)
        masked_part = jnp.sum(jnp.where(hit, grad, 0.0), axis=0, keepdims=True)
        return carry[0] + masked_part, carry[1] + fresh

    zero = jnp.zeros((1, width), F32)
    mask_sum, gain_sum = over_rows(span, pass_back, (zero, zero))
    sums[0:1, :] = mask_sum
    sums[1:2, :] = gain_sum
    rows = span // 2
    grad_own[...] = grads[pl.ds(core * rows, rows), :]
    grad_sent[...] = grads[pl.ds((1 - core) * rows, rows), :]


def k_weights(pairs, bit, tiles, info, *refs):
    count = 1 + max(max(pair[place] for place in (0, 1, 2, 4)) for pair in pairs)
    inputs, kept, sent = refs[:count], refs[count], refs[count + 1]
    mine = (info[3] >> bit) & 1
    low = bit - tiles
    rows = kept.shape[1]

    def one(index, carry):
        for side in range(2):
            tile = ((index >> low) * 2 + (mine ^ side)) * (1 << low) + (index & ((1 << low) - 1))
            at = pl.ds(pl.multiple_of(tile * rows, rows), rows)
            begin = 0
            for left, left_too, right, shift, right_too, shift_too, size in pairs:
                for piece in range(0, size, TILE):
                    grad = inner_rows(
                        inputs[left][:, at],
                        inputs[right][:, shift + piece : shift + piece + TILE],
                    ) + inner_rows(
                        inputs[left_too][:, at],
                        inputs[right_too][:, shift_too + piece : shift_too + piece + TILE],
                    )
                    spot = slice(begin + piece, begin + piece + TILE)
                    if side == 0:
                        kept[index, :, spot] = grad
                    else:
                        sent[index, :, spot] = grad.astype(BF)
                begin += size
        return carry

    lax.fori_loop(0, kept.shape[0], one, 0, unroll=2)


def k_fold(bit, count, info, held, *refs):
    arrivals, kept, sent = refs[:count], refs[count], refs[count + 1]
    mine = (info[3] >> bit) & 1
    for index in range(held.shape[0]):
        for side in range(2):
            at = pl.ds(mine ^ side, 1)
            begin = 0
            for entry in arrivals:
                spot = slice(begin, begin + entry.shape[3])
                total = held[index, at, :, spot][0] + entry[index, at][0].astype(F32)
                if side == 0:
                    kept[index, :, spot] = total
                else:
                    sent[index, :, spot] = total.astype(BF)
                begin = spot.stop


def k_finish(turned, count, info, kept, *refs):
    arrivals, results = refs[:count], refs[count:]
    cut = arrivals[0].shape[1]
    begin = 0
    for result, turn in zip(results, turned):
        size = result.shape[0] if turn else result.size // result.shape[0]
        for piece in range(begin, begin + size, DH):
            spot = slice(piece, piece + DH)
            at = piece - begin
            inside = slice(piece % cut, piece % cut + DH)
            total = kept[:, spot] + arrivals[piece // cut][:, inside].astype(F32)
            if turn:
                result[at : at + DH, :] = total.T
            elif len(result.shape) == 3:
                result[:, at // result.shape[2], pl.ds(at % result.shape[2], DH)] = total
            else:
                result[:, at : at + DH] = total
        begin += size


def k_in_order(info, own, other, result):
    core = info[0]
    result[pl.ds(core, 1)] = own[...][None]
    result[pl.ds(1 - core, 1)] = other[...][None]


def k_gather(bit, info, held, arrived, result):
    mine = (info[3] >> bit) & 1
    result[:, pl.ds(mine, 1)] = held[...][:, None]
    result[:, pl.ds(1 - mine, 1)] = arrived[...][:, None]


def k_smalls(last, attn, conv, two, final, channel_sums, result):
    width = attn.shape[1]
    result[0:2, :width] = last[...]
    for place, entry in enumerate((attn, conv, two, final), 2):
        result[place : place + 1, :width] = 0.5 * entry[...]
    result[6:8, :width] = jnp.zeros((2, width), F32)
    result[:, width:] = channel_sums[...]


def k_smalls_cross(smalls, result):
    width = smalls.shape[1] - 2 * (smalls.shape[1] - result.shape[1])
    channels = result.shape[1] - width
    result[:, :width] = smalls[:, :width]
    result[:, width:] = smalls[:, width + channels :]


def k_gains(mine, theirs, channel_sums, result):
    width = mine.shape[1]
    result[:, :width] = mine[...] + theirs[...]
    result[:, width:] = channel_sums[...]


def k_smalls_add(smalls, arrived, result):
    size = result.shape[1]
    result[...] = smalls[:, :size] + arrived[...]


def run(kernel, results, arguments, scalars=1, scratch=(), late=(), leaving=(), cost=1):
    given, made = len(arguments), len(results)
    hbm_shapes = [(arguments[place].shape, arguments[place].dtype) for place in late]
    hbm_shapes += [results[place] for place in leaving]
    buffers = [pltpu.VMEM(shape, kind) for shape, kind in hbm_shapes]
    own = [pltpu.VMEM(shape, kind) for shape, kind in scratch]
    hbm = pl.BlockSpec(memory_space=pltpu.HBM)

    def body(*refs):
        ins, outs = list(refs[:given]), list(refs[given : given + made])
        rest = refs[given + made :]
        extra, held, semaphores = rest[: len(own)], rest[len(own) : -1], rest[-1]
        for index, place in enumerate(late):
            ins[place] = Late(ins[place], held[index], semaphores.at[index])
        for index, place in enumerate(leaving, len(late)):
            outs[place] = Leaving(outs[place], held[index], semaphores.at[index])
        kernel(*ins, *outs, *extra)
        arrive(*ins)
        for place in leaving:
            outs[place].finish()

    def plain(*refs):
        kernel(*refs)

    held_bytes = sum(
        functools.reduce(lambda a, b: a * b, shape) * jnp.dtype(kind).itemsize
        for shape, kind in [*scratch, *hbm_shapes]
    )
    specs = [SMEM_SPEC] * scalars + [VMEM_SPEC] * (given - scalars)
    out_specs = [VMEM_SPEC] * made
    for place in late:
        specs[place] = hbm
    for place in leaving:
        out_specs[place] = hbm
    many = len(hbm_shapes)
    return pl.pallas_call(
        body if many else plain,
        out_shape=[
            pltpu.HBM(shape, kind) if place in leaving else pltpu.VMEM(shape, kind)
            for place, (shape, kind) in enumerate(results)
        ],
        in_specs=specs,
        out_specs=out_specs,
        scratch_shapes=own + buffers + ([pltpu.SemaphoreType.DMA((many,))] if many else []),
        compiler_params=pltpu.CompilerParams(vmem_limit_bytes=held_bytes + 8 * MIB),
        cost_estimate=pl.CostEstimate(flops=cost, bytes_accessed=cost, transcendentals=0),
    )(*(
        entry if place < scalars else pltpu.with_memory_space_constraint(
            entry, pltpu.HBM if place in late else pltpu.VMEM
        )
        for place, entry in enumerate(arguments)
    ))


def swap(value, axis, bit):
    size = lax.axis_size(axis)
    return lax.ppermute(value, axis, [(place, place ^ bit) for place in range(size)])


def across(value):
    return swap(value, "tensor", 2)


def beside(value):
    return swap(value, "tensor", 1)


def bit_of(axis, bit):
    return (lax.axis_index(axis) & bit) != 0


def tie(*values):
    return lax.optimization_barrier(values)


class RowSum:
    def __init__(self, info, inputs, pairs, width, first_bits, cuts=(), cost=1):
        size = lax.axis_size("dp")
        levels = size.bit_length() - 1
        tiles = max(levels - 3, 0)
        order = [tiles + bit for bit in first_bits]
        self.order = order + [bit for bit in range(levels - 1, -1, -1) if bit not in order]
        self.left = list(range(levels - 1, -1, -1))
        self.total = sum(pair[-1] for pair in pairs)
        self.block = width // size
        self.info = info
        count = size >> tiles
        shape = (count // 2, width // count)
        self.kept, *self.sent = run(
            functools.partial(k_weights, pairs, self.order[0], tiles),
            [((*shape, self.total), F32)]
            + [((*shape, size), BF) for size in (cuts or (self.total,))],
            [info] + inputs,
            cost=cost,
        )
        self.begin()

    def begin(self):
        self.bit = self.order.pop(0)
        self.left.remove(self.bit)
        self.arrived = []

    def send(self, chain=None):
        piece = self.sent.pop(0)
        if chain is not None:
            (piece,) = chain.after(piece)
        self.arrived.append(swap(piece, "dp", 1 << self.bit))

    def here(self, chain):
        (self.arrived[-1],) = chain.after(self.arrived[-1])

    def fold(self, chain, cost=1):
        bit = self.order[0]
        place = self.left.index(bit)
        inner = self.block << (len(self.left) - 1 - place)
        outer = 1 << place
        kept, *arrived = chain.after(self.kept, *self.arrived)
        self.kept, *self.sent = run(
            functools.partial(k_fold, bit, len(arrived)),
            [((outer, inner, self.total), F32), ((outer, inner, self.total), BF)],
            [self.info, kept.reshape(outer, 2, inner, self.total)]
            + [entry.reshape(outer, 2, inner, -1) for entry in arrived],
            cost=cost,
        )
        self.kept, chain.last = tie(self.kept, chain.last)
        self.begin()

    def step(self, chain, cost=1):
        self.fold(chain, cost=cost)
        self.send()

    def finish(self, chain, *results):
        while self.order:
            self.step(chain)
        shape = (self.block, self.total)
        kept, *arrived = chain.after(
            self.kept.reshape(shape), *(entry.reshape(self.block, -1) for entry in self.arrived)
        )
        sums = run(
            functools.partial(k_finish, tuple(turn for _, turn in results), len(arrived)),
            [(size, F32) for size, _ in results],
            [self.info, kept, *arrived],
        )
        *sums, chain.last = tie(*sums, chain.last)
        return sums


class Chain:
    def __init__(self, last):
        self.last = last

    def after(self, *values):
        *values, self.last = tie(*values, self.last)
        return values


class Gather:
    def __init__(self, info, block):
        self.info, self.held = info, block.reshape(1, *block.shape)
        self.bit = lax.axis_size("dp") // 2
        self.shape = (lax.axis_size("dp") * block.shape[0], block.shape[1])

    def send(self):
        self.arrived = swap(self.held, "dp", self.bit)

    def take(self):
        outer, rows, width = self.held.shape
        (held,) = run(
            functools.partial(k_gather, self.bit.bit_length() - 1),
            [((outer, 2, rows, width), self.held.dtype)],
            [self.info, self.held, self.arrived],
        )
        self.held = held.reshape(outer * 2, rows, width)
        self.bit //= 2

    def whole(self):
        while self.bit:
            self.send()
            self.take()
        return self.held.reshape(self.shape)


def sum_pair(value, axis, merge=None):
    bit, size = 1, lax.axis_size(axis)
    while bit * 2 < size:
        (value,) = run(
            merge or k_add, [(value.shape, F32)], [value, swap(value, axis, bit)], scalars=0
        )
        bit *= 2
    return value, swap(value, axis, bit)


def per_device(
    frames,
    lengths,
    span_starts,
    mask_vector,
    ffn1_gain,
    ffn1_up,
    ffn1_down,
    attn_gain,
    query_weight,
    key_weight,
    value_weight,
    output_weight,
    rel_slope,
    conv_gain,
    conv_up,
    conv_depth,
    bn_scale,
    bn_shift,
    conv_down,
    ffn2_gain,
    ffn2_up,
    ffn2_down,
    final_gain,
    cotangent,
):
    batches, row_count, width = frames.shape
    length = row_count * lax.axis_size("tensor")
    span = 2 * row_count
    channels = conv_depth.shape[1]
    hidden_width = ffn1_up.shape[1]
    heads = rel_slope.shape[0]
    third = query_weight.shape[1]
    core = lax.axis_index("tensor") & 1
    high = (lax.axis_index("tensor") >> 1) & 1
    group = lax.axis_index("dp")
    on_first = core == 0
    own_length = jnp.where(on_first, lengths[0], lengths[1])
    info = jnp.stack([core, high, own_length, group]).astype(jnp.int32)
    starts = jnp.where(on_first, span_starts[0:1], span_starts[1:2])

    frames_across = across(frames)
    conv_block = jnp.concatenate(
        [conv_up.reshape(conv_up.shape[0], 2 * channels), conv_down.T], axis=1
    )
    conv_weights = Gather(info, conv_block)
    conv_weights.send()

    part = mask_vector.shape[0]
    place = (group * lax.axis_size("tensor") + lax.axis_index("tensor")) * part
    vectors = jnp.stack(
        [mask_vector.astype(F32), ffn1_gain, attn_gain, conv_gain, ffn2_gain, final_gain,
         jnp.zeros_like(ffn1_gain), jnp.zeros_like(ffn1_gain)]
    )
    small = lax.dynamic_update_slice(jnp.zeros((8, width), F32), vectors, (0, place))
    hops = [("tensor", 1), ("dp", 2), ("dp", 1), ("tensor", 2)]
    bit = 4
    while bit < lax.axis_size("dp"):
        hops.append(("dp", bit))
        bit *= 2
    for step, (axis, bit) in enumerate(hops):
        if step == 4:
            (sent,) = run(k_pick, [(frames.shape, BF)], [info, frames, frames_across])
            sent, small = tie(sent, small)
        if step == 3:
            query_weight, key_weight, conv_depth, rel_slope, small = tie(
                query_weight, key_weight, conv_depth, rel_slope, small
            )
            own_qkv = jnp.concatenate([query_weight, key_weight, value_weight], axis=1)
            slope_row = jnp.pad(rel_slope[None], ((0, 0), (0, channels - heads)))
            own_params = jnp.concatenate([conv_depth, bn_scale[None], bn_shift[None], slope_row])
            other_params = beside(own_params)
            conv_weights.arrived, small = tie(conv_weights.arrived, small)
            conv_weights.take()
            if conv_weights.bit:
                conv_weights.send()
        if bit < lax.axis_size(axis):
            (small,) = run(
                k_add, [(small.shape, F32)], [small, swap(small, axis, bit)], scalars=0
            )
    if conv_weights.bit:
        conv_weights.arrived, small = tie(conv_weights.arrived, small)
        conv_weights.take()
    frame_parts = [frames, frames_across, beside(sent)]
    own_qkv, other_params, conv_weights.held, small = tie(
        own_qkv, other_params, conv_weights.held, small
    )
    params = jnp.concatenate([own_params, other_params], axis=1)
    slopes = jnp.concatenate([rel_slope, other_params[KW + 2, :heads]])
    if conv_weights.bit:
        conv_weights.send()
    up_one, down_one = beside(ffn1_up), beside(ffn1_down)

    wide = (length, width)
    ffn_outs = [
        (wide, BF),
        ((length, hidden_width), BF),
        ((length, hidden_width), BF),
        ((length, 2 * hidden_width), F32),
        (wide, BF),
    ]
    whole, norm_one, cross_one, active_one, hidden_one, partial = run(
        k_ffn_one,
        [(wide, BF)] + ffn_outs,
        [info, starts, *frame_parts, small, ffn1_up, up_one, ffn1_down, down_one],
        scratch=[(wide, BF)], late=(6, 8),
    )
    output_weight, active_one = tie(output_weight, active_one)
    other_qkv, other_out = beside(own_qkv), beside(output_weight)
    stream_one, norm_attn, context_cross, context_own, qkv, weights, partial = run(
        k_attn_wrapped,
        [
            (wide, F32),
            (wide, BF),
            ((length, third), BF),
            ((length, third), BF),
            ((length, 6 * third), BF),
            ((2 * heads, length, length), F32),
            (wide, BF),
        ],
        [info, slopes, starts, partial, across(partial), whole, small, own_qkv, other_qkv,
         output_weight, other_out],
        scalars=2, late=(7, 9),
    )
    conv_weights.arrived, norm_one, cross_one, context_own = tie(
        conv_weights.arrived, norm_one, cross_one, context_own
    )
    conv_weights.take()
    own_conv = conv_weights.whole()
    other_conv = beside(own_conv)
    norm_one_too, cross_one_too = beside(norm_one), beside(cross_one)
    norm_one_too, cross_one_too, params = tie(norm_one_too, cross_one_too, params)
    both_channels = (length, 2 * channels)
    stat_shape = ((8, 2 * channels), F32)
    stream_two, norm_conv, value, gate, padded, convolved, stats = run(
        k_conv_front,
        [
            (wide, F32),
            (wide, BF),
            (both_channels, F32),
            (both_channels, F32),
            ((length + 2 * EDGE, 2 * channels), F32),
            (both_channels, F32),
            stat_shape,
        ],
        [info, partial, across(partial), stream_one, small, params, own_conv, other_conv],
        late=(6,),
    )
    norm_attn, context_cross, cotangent, ffn2_up, ffn2_down, value = tie(
        norm_attn, context_cross, cotangent, ffn2_up, ffn2_down, value
    )
    stats, stats_too = sum_pair(stats, "dp", k_merge)
    grad_across = across(cotangent)
    up_two, down_two = beside(ffn2_up), beside(ffn2_down)
    norm_attn_too, context_cross_too = beside(norm_attn), beside(context_cross)
    params, grad_across = tie(params, grad_across)
    stats, active_conv, cross_conv, partial = run(
        k_conv_rear,
        [stat_shape, ((length, channels), BF), ((length, channels), BF), (wide, BF)],
        [stats, stats_too, convolved, params, norm_conv, own_conv, other_conv],
        scalars=0, late=(5,),
    )
    grad_across, active_conv = tie(grad_across, active_conv)
    (sent,) = run(k_pick, [(cotangent.shape, BF)], [info, cotangent, grad_across])
    grad_parts = [cotangent, grad_across, beside(sent)]
    grad_parts[2], small = tie(grad_parts[2], small)
    stream_three, norm_two, cross_two, active_two, hidden_two, partial = run(
        k_ffn_two,
        [(wide, F32)] + ffn_outs,
        [partial, across(partial), stream_two, small, ffn2_up, up_two, ffn2_down, down_two],
        scalars=0, late=(4, 6),
    )
    norm_two, cross_two, norm_conv, cross_conv, active_two = tie(
        norm_two, cross_two, norm_conv, cross_conv, active_two
    )
    norm_two_too, cross_two_too = beside(norm_two), beside(cross_two)
    norm_conv_too, cross_conv_too = beside(norm_conv), beside(cross_conv)
    (
        norm_two_too, cross_two_too, norm_conv_too, cross_conv_too, norm_attn_too,
        context_cross_too, small,
    ) = tie(
        norm_two_too, cross_two_too, norm_conv_too, cross_conv_too, norm_attn_too,
        context_cross_too, small,
    )

    row_shape = ((1, width), F32)
    block_shape = (row_count, width)
    out_own, out_sent, grad_four, sum_final, back_two, hid_cross_two, hid_two, partial = run(
        k_ffn_two_back,
        [
            (block_shape, BF),
            (block_shape, BF),
            (wide, F32),
            row_shape,
            (wide, BF),
            ((length, hidden_width), BF),
            ((length, hidden_width), BF),
            (wide, BF),
        ],
        [info, partial, across(partial), stream_three, small, *grad_parts, hidden_two,
         ffn2_up, up_two, ffn2_down, down_two],
        scratch=[(wide, BF), (wide, BF)], late=(9, 11),
    )
    back_two_too, hid_cross_two_too = beside(back_two), beside(hid_cross_two)
    ffn_pair = ((0, 1, 2, 0, 3, 0, hidden_width),)
    two_up = RowSum(
        info, [norm_two, norm_two_too, hid_two, hid_cross_two_too], ffn_pair, width, (0, 1, 2)
    )
    two_down = RowSum(
        info, [back_two, back_two_too, active_two, cross_two_too], ffn_pair, width, (1, 2, 0)
    )
    grad_four, two_up.sent[0], two_down.sent[0] = tie(
        grad_four, two_up.sent[0], two_down.sent[0]
    )
    grad_three, sum_two, back_conv, grad_shaped, sums = run(
        k_conv_back_front,
        [(wide, F32), row_shape, (wide, BF), (both_channels, F32), stat_shape],
        [partial, across(partial), stream_three, small, grad_four, convolved, stats, params,
         own_conv, other_conv],
        scalars=0, late=(8,),
    )
    out_sent, sum_two, back_conv = tie(out_sent, sum_two, back_conv)
    out_other, back_conv_too = beside(out_sent), beside(back_conv)
    bits = [1 << level for level in range(lax.axis_size("dp").bit_length() - 1)]
    for bit in bits[:-1]:
        (sums,) = run(
            k_add, [(sums.shape, F32)], [sums, swap(sums, "dp", bit)], scalars=0
        )
        chain = Chain(sums)
        if bit == 1:
            two_up.send(chain)
        if bit == 2:
            two_down.send(chain)
        sums = chain.last
    sums_too = swap(sums, "dp", bits[-1])
    sums_too, out_other, back_conv_too = tie(sums_too, out_other, back_conv_too)
    small_sums, mixed_own, mixed_cross, partial = run(
        k_conv_back_rear,
        [
            stat_shape,
            ((length, 2 * channels), BF),
            ((length, 2 * channels), BF),
            (wide, BF),
        ],
        [info, sums, sums_too, grad_shaped, convolved, stats, params, padded, value, gate,
         back_conv, own_conv, other_conv],
        scratch=[((length + 2 * EDGE, 2 * channels), F32)], late=(11,),
    )
    mixed_cross_too = beside(mixed_cross)
    mixed_cross_too, grad_three = tie(mixed_cross_too, grad_three)
    grad_two, sum_conv, back_attn, three_cross, three_own, small_sums, partial = run(
        k_attn_back,
        [
            (wide, F32),
            row_shape,
            (wide, BF),
            ((length, 3 * third), BF),
            ((length, 3 * third), BF),
            stat_shape,
            (wide, BF),
        ],
        [partial, across(partial), stream_two, small, grad_three, small_sums, qkv, weights,
         own_qkv, other_qkv, output_weight, other_out],
        scalars=0,
        scratch=[((length, 2 * third), BF)], late=(8, 10),
    )
    back_attn_too, three_cross_too = beside(back_attn), beside(three_cross)
    chain = Chain(small_sums)
    for entry in (two_up, two_down):
        entry.step(chain)
    back_attn, three_own = chain.after(back_attn, three_own)
    small_sums = chain.last
    middle = RowSum(
        info,
        [norm_conv, norm_conv_too, mixed_own, mixed_cross_too,
         back_conv, back_conv_too, active_conv, cross_conv_too,
         norm_attn, norm_attn_too, three_own, three_cross_too,
         back_attn, back_attn_too, context_own, context_cross_too],
        (
            (0, 1, 2, 0, 3, 0, 2 * channels),
            (4, 5, 6, 0, 7, 0, channels),
            (8, 9, 10, 0, 11, 0, 3 * third),
            (12, 13, 14, 0, 15, 0, third),
        ),
        width, (0, 1, 2),
    )
    middle.send()
    middle.kept, grad_two = tie(middle.kept, grad_two)
    grad_one, sum_attn, back_one, hid_cross_one, hid_one, last_own, last_sent = run(
        k_ffn_one_back,
        [
            (wide, F32),
            row_shape,
            (wide, BF),
            ((length, hidden_width), BF),
            ((length, hidden_width), BF),
            ((span, width), F32),
            ((span, width), BF),
        ],
        [info, partial, across(partial), stream_one, small, grad_two, hidden_one,
         ffn1_up, up_one, ffn1_down, down_one],
        scratch=[(wide, F32)], late=(7, 9),
    )
    back_one_too, hid_cross_one_too = beside(back_one), beside(hid_cross_one)
    chain = Chain(sum_attn)
    for entry in (two_up, two_down):
        entry.step(chain, cost=COST)
    hid_one, active_one = chain.after(hid_one, active_one)
    one_up = RowSum(
        info, [norm_one, norm_one_too, hid_one, hid_cross_one_too], ffn_pair, width, (0, 1, 2),
        cost=COST,
    )
    one_down = RowSum(
        info, [back_one, back_one_too, active_one, cross_one_too], ffn_pair, width, (0, 1, 2),
        cost=COST,
    )
    one_up.send(chain)
    one_up.kept, chain.last = tie(one_up.kept, chain.last)
    one_down.send(chain)
    one_down.kept, chain.last = tie(one_down.kept, chain.last)
    block = width // lax.axis_size("dp")
    (starts,) = chain.after(starts)
    sum_attn = chain.last
    frames_own, frames_sent, last_sums = run(
        k_last,
        [(block_shape, F32), (block_shape, F32), ((2, width), F32)],
        [info, starts, last_own, across(last_sent), whole, small, grad_one],
        scratch=[((span, width), F32)],
    )
    frames_other = beside(frames_sent)
    chain = Chain(last_sums)
    middle.step(chain)
    last_sums = chain.last
    (smalls,) = run(
        k_smalls, [((8, width + 2 * channels), F32)],
        [last_sums, sum_attn, sum_conv, sum_two, sum_final, small_sums], scalars=0,
    )
    (smalls_sent,) = run(k_smalls_cross, [((8, width + channels), F32)], [smalls], scalars=0)
    (smalls,) = run(
        k_smalls_add, [((8, width + channels), F32)], [smalls, beside(smalls_sent)], scalars=0
    )
    gains, gains_too = smalls[:, :width], across(smalls[:, :width])
    (gains,) = run(
        k_gains, [(smalls.shape, F32)], [gains, gains_too, smalls[:, width:]], scalars=0
    )

    def in_order(own, other):
        return run(k_in_order, [((2, *own.shape), own.dtype)], [info, own, other])[0]

    chain = Chain(in_order(out_own, out_other))

    def hop(value, bit):
        (value,) = chain.after(value)
        return value, swap(value, "dp", bit)

    def add(value, other):
        (total,) = run(k_add, [(value.shape, F32)], chain.after(value, other), scalars=0)
        return total

    first, *between = [1 << level for level in range(1, lax.axis_size("dp").bit_length() - 1)]
    (two_up,) = two_up.finish(chain, ((block, hidden_width), False))
    middle.step(chain)
    one_up.step(chain)
    for bit in [first, *between]:
        gains = add(*hop(gains, bit))
    gains, chain.last = tie(gains, chain.last)
    one_down.step(chain)
    one_up.step(chain)
    conv_up_grad, conv_down_grad, query_grad, key_grad, value_grad, output_grad = middle.finish(
        chain,
        (conv_up.shape, False), ((channels, block), True),
        *[((block, third), False)] * 3, ((third, block), True),
    )
    gains, gains_too = hop(gains, 1)
    (one_up,) = one_up.finish(chain, ((block, hidden_width), False))
    gains = add(gains, gains_too)
    one_down.step(chain)
    (two_down,) = two_down.finish(chain, ((hidden_width, block), True))
    channel_sums = gains[:, width:]
    scale_grad = channel_sums[KW + 1] * (1.0 / lax.axis_size("dp"))
    shift_grad = channel_sums[KW] * (1.0 / lax.axis_size("dp"))
    gains = lax.dynamic_slice_in_dim(gains, place, part, axis=1)

    frames_grad = in_order(frames_own, frames_other)
    smallest = [
        *(gains[index] for index in range(6)),
        channel_sums[KW + 2, :heads],
        channel_sums[:KW],
        scale_grad,
        shift_grad,
    ]
    frames_grad, *smallest = chain.after(frames_grad, *smallest)
    (one_down,) = one_down.finish(chain, ((hidden_width, block), True))

    return (
        chain.last,
        frames_grad,
        smallest[0],
        smallest[1],
        one_up,
        one_down,
        smallest[2],
        query_grad,
        key_grad,
        value_grad,
        output_grad,
        smallest[6],
        smallest[3],
        conv_up_grad,
        smallest[7],
        smallest[8],
        smallest[9],
        conv_down_grad,
        smallest[4],
        two_up,
        two_down,
        smallest[5],
    )


def k_attn_wrapped(info, slopes, starts, *refs):
    k_attn(info, starts, slopes, *refs)


def solution(mesh):
    every, split, by_column = P(("dp", "tensor")), P("tensor"), P(None, "tensor")
    rows_by = P("dp", "tensor", None)
    return jax.shard_map(
        per_device,
        mesh=mesh,
        in_specs=(
            rows_by,
            P("dp"),
            P("dp", None),
            every,
            every,
            by_column,
            P("tensor", None),
            every,
            by_column,
            by_column,
            by_column,
            P("tensor", None),
            split,
            every,
            P("dp", None, "tensor"),
            by_column,
            split,
            split,
            P("tensor", "dp"),
            every,
            by_column,
            P("tensor", None),
            every,
            rows_by,
        ),
        out_specs=(
            rows_by,
            rows_by,
            every,
            every,
            P("dp", "tensor"),
            P("tensor", "dp"),
            every,
            P("dp", "tensor"),
            P("dp", "tensor"),
            P("dp", "tensor"),
            P("tensor", "dp"),
            split,
            every,
            P("dp", None, "tensor"),
            by_column,
            split,
            split,
            P("tensor", "dp"),
            every,
            P("dp", "tensor"),
            P("tensor", "dp"),
            every,
        ),
        check_vma=False,
    )
```
